32 devices in a mesh: bulk: 4 (over x, core), grid: 8 (over z, y).
Axes of the slice: x: 2, y: 2, z: 4, core: 2. Of those that a mesh axis runs over, the one named last changes fastest.
Arguments:
- offsets: float32 [8, 3, 4, 24, 128], P('grid', None, 'bulk'), may hold values from -0.75 to 0.75
- flow: float32 [8, 5, 4, 24, 128], P('grid', None, 'bulk'), may hold values from -6 to 6
- control_points: float32 [3, 16384], P(None, ('bulk', 'grid')), may hold values from -7 to 13
- rbf_weights: float32 [3, 16384], P(None, ('bulk', 'grid')), may hold values from -2 to 2
- peer_offset: int32 [8, 720, 1], P('grid', 'bulk'), may hold values from 0 to 6; in each aligned block of 180 rows (0 to 179, 180 to 359, ..., all dimensions but the last counted through in order) at most 28 rows name the same one
- donor_block: int32 [8, 720], P('grid', 'bulk'), may hold values from 0 to 23
- receptor_block: int32 [8, 720], P('grid', 'bulk'), may hold values from 0 to 23
Outputs:
- moved: float32 [8, 3, 4, 24, 128], P('grid', None, 'bulk')
- metric: float32 [8, 4, 24, 128], P('grid', 'bulk')
- fringe: float32 [8, 5, 4, 24, 128], P('grid', None, 'bulk')
The draws below stay inside these ranges and needn't reach their ends.
Inputs may be any that keep to these rules, and one draw needn't show every extreme that they name: `peer_offset`: in the 180 rows of one device no value appears more than 28 times.
All inputs are finite; a program needn't handle non-finite values.
Results may differ from the reference program's by a relative error of at most 0.0003.
Values sent between devices are 32-bit elements; how exact they have to be, the bound alone decides.
A program may use at most 64 MiB of HBM per device.

```python
import math
import jax
import jax.numpy as jnp
import numpy as np
from jax import lax

P_SIZE = 16384
VARS = 5
AI = 1
NJ = 24
NK = 128
SLOTS = 180
CAP = 28
G = 8
NI = 4
N_BULK = 4
N_GRID = 8


def draw_control_points(key, part):
    reach = 1.0 + 0.25 * (NJ - 1)
    unit = jax.random.uniform(key, (3, P_SIZE), jnp.float32)
    lower = jnp.array([-reach, -reach, 0.0], jnp.float32)
    upper = jnp.array([0.5 * (G - 1) + reach, reach, 0.1 * (NK - 1)], jnp.float32)
    return lower[:, None] + (upper - lower)[:, None] * unit


def touch_ends(drawn, key, smallest, top_value):
    spot = [jax.random.randint(jax.random.fold_in(key, axis), (), 0, length) for axis, length in enumerate(drawn.shape)]
    longest = drawn.shape.index(max(drawn.shape))
    beside = spot[:longest] + [(spot[longest] + 1) % drawn.shape[longest]] + spot[longest + 1:]
    return drawn.at[tuple(spot)].set(smallest).at[tuple(beside)].set(top_value)


def level_of(rng, extent, shards, least, top_value):
    def one(axis_at, parts):
        steps = jax.random.uniform(jax.random.fold_in(jax.random.fold_in(rng, 6), axis_at), (parts,), jnp.float32, least / len(shards), top_value / len(shards))
        return jnp.repeat(jnp.exp(steps), extent[axis_at] // parts).reshape((-1,) + (1,) * (len(extent) - axis_at - 1))

    loudness = one(*shards[0])
    for cut in shards[1:]:
        loudness = loudness * one(*cut)
    return loudness


def assign_block(stream_key, own, number, rows, amount, top, most, slope):
    ranking = jax.random.permutation(stream_key, amount)
    crowded, common = load_shares(amount, rows * top, most, slope, True), load_shares(amount, rows * top, most, slope, False)
    places = jnp.arange(amount)

    def named(tallies, offset_by):
        used = int((tallies > 0).sum())
        fixed = max(1, used // 4)
        moved = fixed + (places - fixed + offset_by * (used - fixed)) % max(1, amount - fixed)
        return jnp.zeros((amount,), jnp.int32).at[ranking[jnp.where(places < fixed, places, moved)]].set(jnp.asarray(tallies, jnp.int32))

    tallies = jnp.where(number % 4 == 0, named(crowded, number // 4), named(common, number - number // 4 - 1))
    mixed = jax.random.permutation(jax.random.fold_in(own, 3), amount)
    source_of, taker = mixed[0:amount // 2 * 2:2], mixed[1:amount // 2 * 2:2]
    slack = jnp.minimum(tallies[source_of] - 1, most - tallies[taker]) // 2
    slack = jnp.where((source_of == ranking[0]) | (taker == ranking[0]) | (tallies[taker] == 0), 0, jnp.maximum(slack, 0))
    moved = jax.random.randint(jax.random.fold_in(own, 4), (amount // 2,), 0, 1 << 20) % (slack + 1)
    tallies = tallies.at[source_of].add(-moved).at[taker].add(moved)
    members = jnp.searchsorted(jnp.cumsum(tallies), jnp.arange(rows * top), side="right").astype(jnp.int32)
    grid = members.reshape(top, rows).T
    grid = grid[jax.random.permutation(jax.random.fold_in(own, 1), rows)]
    offset_by = jax.random.randint(jax.random.fold_in(own, 2), (rows, 1), 0, top)
    return jnp.take_along_axis(grid, (jnp.arange(top)[None, :] + offset_by) % top, axis=1)


def load_shares(count, total, bound, slope, full):
    loads = [(1 << 20) // math.isqrt(standing ** slope) + 1 for standing in range(1, count + 1)]
    largest = bound if full else min(bound, max(-(-total // count), total * loads[0] // sum(loads)))
    least = 1 if total - largest >= count - 1 else 0
    holding, spare = [largest] + [least] * (count - 1), total - largest - least * (count - 1)
    while spare > 0:
        candidates = [i for i in range(1, count) if holding[i] < largest] or [i for i in range(1, count) if holding[i] < bound]
        whole, remaining = sum([loads[i] for i in candidates]), spare
        for i in candidates:
            addition = min(bound - holding[i], max(1, remaining * loads[i] // whole), spare)
            holding[i] = holding[i] + addition
            spare = spare - addition
    return np.array(holding)


def scatter_about(rng, dims, spread, limit, shards=(), kind=jnp.bfloat16):
    values = jax.random.normal(rng, dims, jnp.float32) * spread
    if len(shards) > 0:
        values = level_of(rng, dims, shards, -0.22, 0.18) * values
    return jnp.clip(values, min=-limit, max=limit).astype(kind)


def setup_inputs(seed: int = 0) -> dict:
    arg_keys = jax.random.split(jax.random.key(seed), 8)
    offsets = scatter_about(arg_keys[0], (G, 3, NI, NJ, NK), 0.05, 0.75, ((0, 8), (2, 4)), jnp.float32)
    flow = scatter_about(arg_keys[1], (G, VARS, NI, NJ, NK), 1.0, 6.0, ((0, 8), (2, 4)), jnp.float32)
    control_points = draw_control_points(jax.random.fold_in(arg_keys[7], 71), 0)
    rbf_weights = scatter_about(arg_keys[3], (3, P_SIZE), 0.15, 2.0, ((1, 32),), jnp.float32)
    peer_offset_keys = jax.random.split(jax.random.fold_in(arg_keys[4], 1), G * (N_BULK * SLOTS) // SLOTS)
    peer_offset_turns = jax.random.permutation(jax.random.fold_in(arg_keys[4], 3), G * (N_BULK * SLOTS) // SLOTS)
    peer_offset = jax.vmap(lambda own, number: assign_block(jax.random.fold_in(arg_keys[4], 2), own, number, SLOTS, N_GRID - 1, 1, CAP, 2))(peer_offset_keys, peer_offset_turns).reshape((G, N_BULK * SLOTS, 1))
    donor_block = touch_ends(jax.random.randint(arg_keys[5], (G, N_BULK * SLOTS), 0, AI * NJ), jax.random.fold_in(arg_keys[5], 1), 0, (AI * NJ) - 1).astype(jnp.int32)
    receptor_block = touch_ends(jax.random.randint(arg_keys[6], (G, N_BULK * SLOTS), 0, AI * NJ), jax.random.fold_in(arg_keys[6], 1), 0, (AI * NJ) - 1).astype(jnp.int32)
    return {"offsets": offsets, "flow": flow, "control_points": control_points, "rbf_weights": rbf_weights, "peer_offset": peer_offset, "donor_block": donor_block, "receptor_block": receptor_block}


HIGHEST = lax.Precision.HIGHEST
SUPPORT = 1.25

def lattice(grid_ids, plane_ids, planes_total, radial, lines):
    theta = 2.0 * math.pi * plane_ids.astype(jnp.float32) / planes_total
    radius = 1.0 + 0.25 * jnp.arange(radial, dtype=jnp.float32)
    height = 0.1 * jnp.arange(lines, dtype=jnp.float32)
    centre = 0.5 * grid_ids.astype(jnp.float32)
    xcoord = centre[:, None, None, None] + radius[None, None, :, None] * jnp.cos(theta)[None, :, None, None] + 0.0 * height[None, None, None, :]
    ycoord = (radius[None, :, None] * jnp.sin(theta)[:, None, None] + 0.0 * height[None, None, :])[None] + 0.0 * centre[:, None, None, None]
    zcoord = jnp.zeros_like(xcoord) + height[None, None, None, :]
    return jnp.stack([xcoord, ycoord, zcoord], axis=1)

def kernel_sum(nodes, points, weights):
    squared = (nodes[0][:, None] - points[0][None, :]) ** 2
    squared = squared + (nodes[1][:, None] - points[1][None, :]) ** 2
    squared = squared + (nodes[2][:, None] - points[2][None, :]) ** 2
    scaled = jnp.sqrt(squared) / SUPPORT
    inside = jnp.maximum(1.0 - scaled, 0.0)
    basis = inside ** 4 * (4.0 * scaled + 1.0)
    return jnp.einsum('ck,nk->cn', weights, basis, precision=HIGHEST)

def along_axis(field, axis):
    total = field.shape[axis]
    ahead = lax.slice_in_dim(field, 2, total, axis=axis)
    behind = lax.slice_in_dim(field, 0, total - 2, axis=axis)
    first = lax.slice_in_dim(field, 1, 2, axis=axis) - lax.slice_in_dim(field, 0, 1, axis=axis)
    last = lax.slice_in_dim(field, total - 1, total, axis=axis) - lax.slice_in_dim(field, total - 2, total - 1, axis=axis)
    return jnp.concatenate([first, (ahead - behind) * 0.5, last], axis=axis)

def jacobian(slope_plane, slope_radial, slope_height):
    cross_x = slope_radial[:, 1] * slope_height[:, 2] - slope_radial[:, 2] * slope_height[:, 1]
    cross_y = slope_radial[:, 2] * slope_height[:, 0] - slope_radial[:, 0] * slope_height[:, 2]
    cross_z = slope_radial[:, 0] * slope_height[:, 1] - slope_radial[:, 1] * slope_height[:, 0]
    return slope_plane[:, 0] * cross_x + slope_plane[:, 1] * cross_y + slope_plane[:, 2] * cross_z

def blend(receptor_xyz, donor_xyz, donor_values):
    squared = (receptor_xyz[:, 0, :, None] - donor_xyz[:, 0, None, :]) ** 2
    squared = squared + (receptor_xyz[:, 1, :, None] - donor_xyz[:, 1, None, :]) ** 2
    squared = squared + (receptor_xyz[:, 2, :, None] - donor_xyz[:, 2, None, :]) ** 2
    weight = 1.0 / (0.25 + squared)
    totals = lax.optimization_barrier(jnp.sum(weight, axis=2))
    weighted = jnp.einsum('nad,nvd->nva', weight, donor_values, precision=HIGHEST)
    return weighted / totals[:, None, :]

def reference(offsets, flow, control_points, rbf_weights, peer_offset, donor_block, receptor_block):
    grids = offsets.shape[0]
    planes = offsets.shape[2]
    base = lattice(jnp.arange(grids, dtype=jnp.int32), jnp.arange(planes, dtype=jnp.int32), planes, NJ, NK) + offsets
    flat = jnp.transpose(base, (1, 0, 2, 3, 4)).reshape(3, -1)
    tile_nodes = NJ * NK
    tiles = jnp.transpose(flat.reshape(3, -1, tile_nodes), (1, 0, 2))
    moves = lax.map(lambda tile: kernel_sum(tile, control_points, rbf_weights), tiles)
    shifts = jnp.transpose(moves, (1, 0, 2)).reshape(3, grids, planes, NJ, NK)
    moved = base + jnp.transpose(shifts, (1, 0, 2, 3, 4))
    wrapped = jnp.concatenate([moved[:, :, -1:], moved, moved[:, :, :1]], axis=2)
    slope_plane = (wrapped[:, :, 2:] - wrapped[:, :, :-2]) * 0.5
    slope_radial = along_axis(moved, 3)
    slope_height = along_axis(moved, 4)
    metric = jacobian(slope_plane, slope_radial, slope_height)
    values = metric[:, None] * flow
    payload = jnp.concatenate([moved, values], axis=1).reshape(grids, 3 + VARS, planes * NJ, NK)
    coords = moved.reshape(grids, 3, planes * NJ, NK)
    entries = peer_offset.shape[1]
    source_grid = jnp.broadcast_to(jnp.arange(grids, dtype=jnp.int32)[:, None], (grids, entries))
    receiver = (source_grid + 1 + peer_offset[:, :, 0]) % grids
    quarter = (jnp.arange(entries, dtype=jnp.int32) // SLOTS)[None, :] * (AI * NJ)
    donor_ids = (quarter + donor_block).reshape(-1, SLOTS)
    receptor_ids = (quarter + receptor_block).reshape(-1, SLOTS)
    source_ids = source_grid.reshape(-1, SLOTS)
    receiver_ids = receiver.reshape(-1, SLOTS)

    def group(items):
        source_now, receiver_now, donor_now, receptor_now = items
        donor = payload[source_now, :, donor_now]
        receptor_xyz = coords[receiver_now, :, receptor_now]
        return blend(receptor_xyz, donor[:, :3], donor[:, 3:])
    pieces = lax.map(group, (source_ids, receiver_ids, donor_ids, receptor_ids))
    pieces = pieces.reshape(-1, VARS, NK)
    fringe = jnp.zeros((grids, VARS, planes * NJ, NK), jnp.float32)
    fringe = fringe.at[receiver_ids.reshape(-1), :, receptor_ids.reshape(-1)].add(pieces)
    return (moved, metric, fringe.reshape(grids, VARS, planes, NJ, NK))
```

```python
import functools
import math

import jax
import jax.numpy as jnp
from jax import lax
from jax.experimental import pallas as pl
from jax.experimental.pallas import tpu as pltpu
from jax.sharding import PartitionSpec as P

MESH = pl.DeviceIdType.MESH
SUPPORT = 1.25
CULL = SUPPORT * SUPPORT * 1.0001
FAR = 1.0e9
UNROLL = 8
JOIN = 2
ENTRY_UNROLL = 32
F32 = jnp.float32
I32 = jnp.int32
BF16 = jnp.bfloat16
VMEM_SPEC = pl.BlockSpec(memory_space=pltpu.VMEM)
SMEM_SPEC = pl.BlockSpec(memory_space=pltpu.SMEM)


def lattice(grid_ids, plane_ids, planes_total, radial, lines):
    theta = 2.0 * math.pi * plane_ids.astype(jnp.float32) / planes_total
    radius = 1.0 + 0.25 * jnp.arange(radial, dtype=jnp.float32)
    height = 0.1 * jnp.arange(lines, dtype=jnp.float32)
    centre = 0.5 * grid_ids.astype(jnp.float32)
    xcoord = (
        centre[:, None, None, None]
        + radius[None, None, :, None] * jnp.cos(theta)[None, :, None, None]
        + 0.0 * height[None, None, None, :]
    )
    ycoord = (radius[None, :, None] * jnp.sin(theta)[:, None, None] + 0.0 * height[None, None, :])[
        None
    ] + 0.0 * centre[:, None, None, None]
    zcoord = jnp.zeros_like(xcoord) + height[None, None, None, :]
    return jnp.stack([xcoord, ycoord, zcoord], axis=1)


def take_lanes(x, idx):
    dims = lax.GatherDimensionNumbers(
        offset_dims=(),
        collapsed_slice_dims=(1,),
        start_index_map=(1,),
        operand_batching_dims=(0,),
        start_indices_batching_dims=(0,),
    )
    return lax.gather(
        x, idx[..., None], dims, slice_sizes=(1, 1), mode=lax.GatherScatterMode.PROMISE_IN_BOUNDS
    )


def iota(shape, axis):
    return lax.broadcasted_iota(I32, shape, axis)


def search(counts, target):
    pos = jnp.zeros(counts.shape, I32)
    step = counts.shape[1] // 2
    while step:
        seen = take_lanes(counts, pos + (step - 1))
        pos = jnp.where(seen <= target, pos + step, pos)
        step //= 2
    return pos


def halves(n):
    return (n // 2, 2) if n % 2 == 0 else (n, 1)


def line_and_pair(me, n):
    high, low = halves(n)
    place = lax.rem(me, low)
    line = [lax.rem(me // low + m, high) * low + place for m in range(1, high)]
    pair = [me + 1 - 2 * place] if low == 2 else []
    return line, pair


def gather_kernel(
    nb, ng, pts_ref, lst_ref, flow_ref, allp_ref, alll_ref, allf_ref, sp, rp, sl, rl, sf, rf
):
    b = lax.axis_index("bulk")
    g = lax.axis_index("grid")
    gline, gpair = line_and_pair(g, ng)
    bline, bpair = line_and_pair(b, nb)
    barrier = pltpu.get_barrier_semaphore()
    peers = [(b, t) for t in gline + gpair] + [(t, g) for t in bline + bpair]
    for peer in peers:
        pl.semaphore_signal(barrier, inc=1, device_id=peer, device_id_type=MESH)
    pl.semaphore_wait(barrier, len(peers))
    sent = {"p": [], "l": [], "f": []}

    def send(kind, slot, peer, own):
        source, full, ss, rs = {
            "p": (pts_ref, allp_ref, sp, rp),
            "l": (lst_ref, alll_ref, sl, rl),
            "f": (flow_ref, allf_ref, sf, rf),
        }[kind]
        copy = pltpu.make_async_remote_copy(
            src_ref=source if own else full.at[slot],
            dst_ref=full.at[slot],
            send_sem=ss.at[len(sent[kind])],
            recv_sem=rs.at[slot],
            device_id=peer,
            device_id_type=MESH,
        )
        copy.start()
        sent[kind].append(copy)

    def arrived(kind, slot):
        full, ss, rs = {
            "p": (allp_ref, sp, rp),
            "l": (alll_ref, sl, rl),
            "f": (allf_ref, sf, rf),
        }[kind]
        pltpu.make_async_remote_copy(
            src_ref=full.at[slot],
            dst_ref=full.at[slot],
            send_sem=ss.at[0],
            recv_sem=rs.at[slot],
            device_id=peers[0],
            device_id_type=MESH,
        ).wait_recv()

    def across(s, own):
        for t in bline + bpair:
            send("p", b * ng + s, (t, g), own)

    for t in gline + gpair:
        send("p", b * ng + g, (b, t), True)
    across(g, True)
    for kind in ("l", "f"):
        for t in gline + gpair:
            send(kind, g, (b, t), True)
    allp_ref[b * ng + g] = pts_ref[...]
    alll_ref[g] = lst_ref[...]
    for s in gline:
        arrived("p", b * ng + s)
        for t in gpair:
            send("p", b * ng + s, (b, t), False)
        across(s, False)
    for s in gline:
        for kind in ("l", "f"):
            arrived(kind, s)
            for t in gpair:
                send(kind, s, (b, t), False)
    low = halves(ng)[1]
    other = gpair + [t + gpair[0] - g for t in gline] if low == 2 else []
    for s in other:
        arrived("p", b * ng + s)
        across(s, False)
    for x in bline:
        for s in [g] + gline + other:
            arrived("p", x * ng + s)
            for t in bpair:
                send("p", x * ng + s, (t, g), False)
    for t in bpair:
        for x in [t] + [u + t - b for u in bline]:
            for s in [g] + gline + other:
                arrived("p", x * ng + s)
    for s in other:
        arrived("l", s)
        arrived("f", s)
    for kind in sent:
        for copy in sent[kind]:
            copy.wait_send()


def rbf_kernel(
    nd,
    rows,
    ng,
    lrows,
    here_ref,
    base_ref,
    pts_ref,
    lst_ref,
    moved_ref,
    don_ref,
    rec_ref,
    num_ref,
    pnt,
    fil,
    node,
    box,
    out,
    basec,
    cntv,
    cnts,
    shift,
    names,
    sem,
):
    radial = base_ref.shape[1]
    npat = radial // JOIN
    lane8 = iota((8, 128), 1)
    sub8 = iota((8, 128), 0)
    blocks_of_lanes = lane8 // 16
    within = lane8 - 16 * blocks_of_lanes
    upper = (iota((128, 128), 0) <= iota((128, 128), 1)).astype(F32).astype(BF16)

    def running(mask):
        return jnp.dot(
            mask.astype(F32).astype(BF16), upper, preferred_element_type=F32
        ).astype(I32)

    nrow = ng * lrows
    for k in range(ng):
        for c in range(3):
            names[c, k * lrows : (k + 1) * lrows, :] = lst_ref[k, c * lrows : (c + 1) * lrows, :]
    owner = iota((nrow, 128), 0) // lrows
    target = owner + 1 + names[0]
    target = jnp.where(target >= ng, target - ng, target)
    counts = running(target == here_ref[0])
    pos = search(counts, iota((nrow, 128), 1))
    don_ref[...] = owner * radial + take_lanes(names[1], pos)
    rec_ref[...] = take_lanes(names[2], pos)
    num_ref[...] = take_lanes(counts, jnp.full((nrow, 128), 127, I32))

    for d in range(nd):
        for c in range(6):
            pnt[c, d * rows : (d + 1) * rows, :] = pts_ref[d, c * rows : (c + 1) * rows, :]

    lows, highs = [], []
    for c in range(3):
        for jg in range(radial // 8):
            v = base_ref[c, 8 * jg : 8 * jg + 8, :]
            got = jnp.zeros((8, 128), F32)
            for j in range(8):
                row = jnp.broadcast_to(v[j : j + 1, :], (8, 128))
                got = jnp.where(blocks_of_lanes == j, take_lanes(row, 16 * sub8 + within), got)
            node[c, 8 * jg : 8 * jg + 8, :] = got
        full = node[c]
        lo = jnp.min(full, axis=1, keepdims=True)
        hi = jnp.max(full, axis=1, keepdims=True)
        for q in range(npat):
            mine = slice(q * JOIN, (q + 1) * JOIN)
            least = jnp.min(lo[mine], axis=0, keepdims=True)
            most = jnp.max(hi[mine], axis=0, keepdims=True)
            box[2 * c, q] = jnp.broadcast_to(least, (8, 128))
            box[2 * c + 1, q] = jnp.broadcast_to(most, (8, 128))
        lows.append(jnp.min(lo, axis=0, keepdims=True))
        highs.append(jnp.max(hi, axis=0, keepdims=True))

    dist = jnp.zeros((128, 128), F32)
    for c in range(3):
        p = pnt[c]
        e = jnp.maximum(jnp.maximum(lows[c] - p, p - highs[c]), 0.0)
        dist = dist + e * e
    counts = running(dist < CULL)
    lane = iota((128, 128), 1)
    pos = search(counts, lane)
    total = take_lanes(counts, jnp.full((128, 128), 127, I32))
    for c in range(6):
        v = take_lanes(pnt[c], pos)
        v = jnp.where(lane < total, v, FAR if c < 3 else 0.0)
        fil[c] = v.T
    groups = (jnp.max(total) + 7) // 8

    shift[...] = jnp.zeros(shift.shape, F32)
    cntv[...] = jnp.zeros(cntv.shape, I32)
    wide = npat * 8
    lane_w = iota((wide, 128), 1)

    def page_body(state):
        page, _ = state
        basec[...] = jnp.zeros(basec.shape, I32)
        out[...] = jnp.zeros(out.shape, F32)

        @pl.loop(0, groups)
        def _(gi):
            start = pl.multiple_of(gi * 8, 8)
            dist = jnp.zeros((npat, 8, 128), F32)
            for c in range(3):
                p = fil[c, pl.ds(start, 8), :][None]
                e = jnp.maximum(jnp.maximum(box[2 * c] - p, p - box[2 * c + 1]), 0.0)
                dist = dist + e * e
            before = basec[...]
            counts = before + running((dist < CULL).astype(F32).reshape(wide, 128))
            target = lane_w + 128 * page
            pos = search(counts, target)
            after = take_lanes(counts, jnp.full((wide, 128), 127, I32))
            keep = jnp.logical_and(target >= before, target < after)
            for c in range(6):
                src = jnp.broadcast_to(
                    fil[c, pl.ds(start, 8), :][None], (npat, 8, 128)
                ).reshape(wide, 128)
                out[c] = jnp.where(keep, take_lanes(src, pos), out[c])
            basec[...] = after

        most = jnp.max(basec[...].reshape(npat, 8, 128), axis=1)
        cntv[0:npat, :] = most
        copy = pltpu.make_async_copy(cntv, cnts, sem)
        copy.start()
        copy.wait()

        @pl.loop(0, npat)
        def _(p):
            n = jnp.minimum(cnts[p, 0] - 128 * page, 128)
            turns = (jnp.maximum(n, 0) + (UNROLL - 1)) // UNROLL
            at = [
                [
                    jnp.broadcast_to(node[c, pl.ds(p * JOIN + m, 1), :] * 0.8, (8, 128))
                    for c in range(3)
                ]
                for m in range(JOIN)
            ]
            first = pl.multiple_of(p * 8, 8)
            cols = [out[c, pl.ds(first, 8), :] for c in range(6)]
            cols = [v * 0.8 for v in cols[:3]] + cols[3:]

            def step(i, acc):
                acc = list(acc)
                for u in range(UNROLL):
                    idx = jnp.full((8, 128), i * UNROLL + u, I32)
                    px, py, pz, wx, wy, wz = [take_lanes(v, idx) for v in cols]
                    for m in range(JOIN):
                        dx = at[m][0] - px
                        dy = at[m][1] - py
                        dz = at[m][2] - pz
                        sq = jnp.maximum(dx * dx + dy * dy + dz * dz, 1e-30)
                        near = jnp.maximum(1.0 - sq * lax.rsqrt(sq), 0.0)
                        two = near * near
                        phi = two * two * (5.0 - 4.0 * near)
                        acc[3 * m] = acc[3 * m] + wx * phi
                        acc[3 * m + 1] = acc[3 * m + 1] + wy * phi
                        acc[3 * m + 2] = acc[3 * m + 2] + wz * phi
                return tuple(acc)

            zero = jnp.zeros((8, 128), F32)
            acc = lax.fori_loop(0, turns, step, (zero,) * (3 * JOIN))
            for m in range(JOIN):
                for c in range(3):
                    total_c = jnp.sum(acc[3 * m + c], axis=0, keepdims=True)
                    shift[c, pl.ds(p * JOIN + m, 1), :] += total_c

        return page + 1, jnp.max(most)

    lax.while_loop(
        lambda state: state[0] * 128 < state[1], page_body, (jnp.int32(0), jnp.int32(1))
    )

    for c in range(3):
        for jg in range(radial // 8):
            s = shift[c, 8 * jg : 8 * jg + 8, :]
            got = jnp.zeros((8, 128), F32)
            for kg in range(8):
                row = jnp.broadcast_to(s[kg : kg + 1, :], (8, 128))
                got = jnp.where(blocks_of_lanes == kg, take_lanes(row, 16 * sub8 + within), got)
            moved_ref[c, 8 * jg : 8 * jg + 8, :] = base_ref[c, 8 * jg : 8 * jg + 8, :] + got


def metric_kernel(nb, ng, mov_ref, met_ref, allm_ref, allt_ref, halo, sh, rh, sm, rm, st, rt):
    b = lax.axis_index("bulk")
    g = lax.axis_index("grid")
    after = lax.rem(b + 1, nb)
    before = lax.rem(b + nb - 1, nb)
    barrier = pltpu.get_barrier_semaphore()
    gline, gpair = line_and_pair(g, ng)
    peers = [(before, g), (after, g)] + [(b, t) for t in gline + gpair]
    for peer in peers:
        pl.semaphore_signal(barrier, inc=1, device_id=peer, device_id_type=MESH)
    pl.semaphore_wait(barrier, len(peers))
    halos = [
        pltpu.make_async_remote_copy(
            src_ref=mov_ref,
            dst_ref=halo.at[i],
            send_sem=sh.at[i],
            recv_sem=rh.at[i],
            device_id=(t, g),
            device_id_type=MESH,
        )
        for i, t in enumerate((after, before))
    ]
    for copy in halos:
        copy.start()

    sent = {"m": [], "t": []}

    def describe(kind, slot, peer, own, n):
        source, full, ss, rs = {
            "m": (mov_ref, allm_ref, sm, rm),
            "t": (met_ref, allt_ref, st, rt),
        }[kind]
        return pltpu.make_async_remote_copy(
            src_ref=source if own else full.at[slot],
            dst_ref=full.at[slot],
            send_sem=ss.at[n],
            recv_sem=rs.at[slot],
            device_id=peer,
            device_id_type=MESH,
        )

    def send(kind, slot, peer, own):
        copy = describe(kind, slot, peer, own, len(sent[kind]))
        copy.start()
        sent[kind].append(copy)

    for t in gline + gpair:
        send("m", g, (b, t), True)
    radial, lines = mov_ref.shape[1:]
    row = iota((radial, lines), 0)
    col = iota((radial, lines), 1)
    dj, dk = [], []
    for c in range(3):
        m = mov_ref[c]
        up, down = pltpu.roll(m, radial - 1, 0), pltpu.roll(m, 1, 0)
        dj.append(
            jnp.where(row == 0, up - m, jnp.where(row == radial - 1, m - down, (up - down) * 0.5))
        )
        up, down = pltpu.roll(m, lines - 1, 1), pltpu.roll(m, 1, 1)
        dk.append(
            jnp.where(col == 0, up - m, jnp.where(col == lines - 1, m - down, (up - down) * 0.5))
        )
    cross = [
        dj[1] * dk[2] - dj[2] * dk[1],
        dj[2] * dk[0] - dj[0] * dk[2],
        dj[0] * dk[1] - dj[1] * dk[0],
    ]
    for copy in halos:
        copy.wait_recv()
    di = [(halo[1, c] - halo[0, c]) * 0.5 for c in range(3)]
    met_ref[...] = di[0] * cross[0] + di[1] * cross[1] + di[2] * cross[2]
    for t in gline + gpair:
        send("t", g, (b, t), True)
    for kind in ("m", "t"):
        for s in gline:
            describe(kind, s, peers[0], False, 0).wait_recv()
            for t in gpair:
                send(kind, s, (b, t), False)
    other = gpair + [t + gpair[0] - g for t in gline] if gpair else []
    for kind in ("m", "t"):
        for s in other:
            describe(kind, s, peers[0], False, 0).wait_recv()
    for copy in halos + sent["m"] + sent["t"]:
        copy.wait_send()


def split(x):
    high = x.astype(BF16).astype(F32)
    rest = x - high
    middle = rest.astype(BF16).astype(F32)
    return high, middle, rest - middle


def features(coords, extra, own):
    rows = []
    for x in coords:
        h, m, t = split(x)
        rows += [h, h, m, h, t, m] if own else [h, m, h, t, h, m]
    total = coords[0] * coords[0] + coords[1] * coords[1] + coords[2] * coords[2] + extra
    one = jnp.ones_like(total)
    square = list(split(total))
    return rows + (square + [one] * 3 if own else [one] * 3 + square)


def blend_kernel(
    don_ref, rec_ref, num_ref, mov_ref, allm_ref, allt_ref, flow_ref, out_ref, rows, own, far, val, acc, fcode, frecv
):
    radial = mov_ref.shape[1]
    nvar = out_ref.shape[0]
    nrow = num_ref.shape[0]
    ng = allm_ref.shape[0]
    zero = jnp.zeros((8, 128), F32)
    centre = []
    for c in range(3):
        m = jnp.sum(jnp.sum(mov_ref[c], axis=0, keepdims=True), axis=1, keepdims=True)
        centre.append(m * (1.0 / (radial * 128)))
    mine = features([mov_ref[c] - centre[c] for c in range(3)], 0.0, True)
    scale = [-2.0] * 18 + [1.0] * 6
    for f in range(24):
        rows[f // 8, pl.ds(f % 8, radial, stride=8), :] = mine[f] * scale[f]
    for r in range(radial):
        parts = [rows[p, r * 8 : (r + 1) * 8, :] for p in range(3)]
        own[r] = jnp.concatenate(parts + [zero], axis=0).astype(BF16)

    @pl.loop(0, ng)
    def _(k):
        theirs = features([allm_ref[k, c] - centre[c] for c in range(3)], 0.25, False)
        for f in range(24):
            far[f // 8, pl.ds(k * (radial * 8) + f % 8, radial, stride=8), :] = theirs[f]
        met = allt_ref[k]
        for v in range(8):
            row = met * flow_ref[k, v] if v < nvar else jnp.full((radial, 128), 1.0 if v == nvar else 0.0, F32)
            val[pl.ds(k * (radial * 8) + v, radial, stride=8), :] = row

    acc[...] = jnp.zeros(acc.shape, F32)

    def flatten(r, at):
        n = num_ref[r, 0]

        @pl.loop(0, (n + 7) // 8)
        def _(i):
            for u in range(8):
                fcode[at + i * 8 + u] = don_ref[r, i * 8 + u]
                frecv[at + i * 8 + u] = rec_ref[r, i * 8 + u]

        return at + n

    total = lax.fori_loop(0, nrow, flatten, jnp.int32(0))
    for u in range(ENTRY_UNROLL):
        fcode[total + u] = 0
        frecv[total + u] = 0

    @pl.loop(0, (total + ENTRY_UNROLL - 1) // ENTRY_UNROLL)
    def _(i):
        found = []
        for u in range(ENTRY_UNROLL):
            e = i * ENTRY_UNROLL + u
            code = fcode[e]
            recv = frecv[e]
            parts = [far[p, pl.ds(pl.multiple_of(code * 8, 8), 8), :] for p in range(3)]
            there = jnp.concatenate(parts + [zero], axis=0).astype(BF16)
            den = lax.dot_general(there, own[recv], (((0,), (0,)), ((), ())), preferred_element_type=F32)
            w = pl.reciprocal(den, approx=False)
            hi = w.astype(BF16)
            lo = (w - hi.astype(F32)).astype(BF16)
            vals = val[pl.ds(pl.multiple_of(code * 8, 8), 8), :]
            vhi = vals.astype(BF16).astype(F32)
            both = jnp.concatenate([vhi, vals - vhi], axis=0).astype(BF16)
            got = lax.dot_general(
                jnp.concatenate([both, both], axis=1),
                jnp.concatenate([hi, lo], axis=0),
                (((1,), (0,)), ((), ())),
                preferred_element_type=F32,
            )
            got = got[0:8] + got[8:16]
            got = got / got[nvar : nvar + 1, :]
            found.append((recv, jnp.where(e < total, got, 0.0)))
        for recv, got in found:
            first = pl.multiple_of(recv * 8, 8)
            acc[pl.ds(first, 8), :] += got

    for v in range(nvar):
        out_ref[v] = acc[pl.ds(v, radial, stride=8), :]


def local(offsets, flow, control_points, rbf_weights, peer_offset, donor_block, receptor_block):
    _, _, planes, radial, lines = offsets.shape
    nvar = flow.shape[1]
    nb = lax.axis_size("bulk")
    ng = lax.axis_size("grid")
    nd = nb * ng
    grid_here = lax.axis_index("grid")
    plane_ids = lax.axis_index("bulk") * planes + jnp.arange(planes, dtype=I32)
    base = lattice(grid_here[None], plane_ids, planes * nb, radial, lines) + offsets
    base = base.reshape(3, radial, lines)
    rows = control_points.shape[1] // 128
    points = jnp.concatenate([control_points, rbf_weights], axis=0).reshape(6 * rows, 128)
    slots = donor_block.shape[1]
    lrows = -(-slots // 128)
    spare = lrows * 128 - slots

    def lanes(x, fill):
        return jnp.pad(x.reshape(-1), (0, spare), constant_values=fill).reshape(lrows, 128)

    lists = jnp.concatenate(
        [lanes(peer_offset, -4 * ng), lanes(donor_block, 0), lanes(receptor_block, 0)], axis=0
    )
    dma = pltpu.SemaphoreType.DMA
    sds = jax.ShapeDtypeStruct
    many = nd + ng
    allp, alll, allf = pl.pallas_call(
        functools.partial(gather_kernel, nb, ng),
        out_shape=(
            sds((nd, 6 * rows, 128), F32),
            sds((ng, 3 * lrows, 128), I32),
            sds((ng, nvar, radial, lines), F32),
        ),
        in_specs=[VMEM_SPEC] * 3,
        out_specs=[VMEM_SPEC] * 3,
        scratch_shapes=[dma((many * 2,)), dma((nd,)), dma((many,)), dma((ng,)), dma((many,)), dma((ng,))],
        compiler_params=pltpu.CompilerParams(collective_id=0, has_side_effects=True),
        name="gather_points",
    )(points, lists, flow.reshape(nvar, radial, lines))
    nrow = ng * lrows
    moved, don, rec, num = pl.pallas_call(
        functools.partial(rbf_kernel, nd, rows, ng, lrows),
        out_shape=(
            sds((3, radial, lines), F32),
            sds((nrow, 128), I32),
            sds((nrow, 128), I32),
            sds((nrow, 128), I32),
        ),
        in_specs=[SMEM_SPEC] + [VMEM_SPEC] * 3,
        out_specs=[VMEM_SPEC] * 4,
        scratch_shapes=[
            pltpu.VMEM((6, nd * rows, 128), F32),
            pltpu.VMEM((6, 128, 128), F32),
            pltpu.VMEM((3, radial, 128), F32),
            pltpu.VMEM((6, radial // JOIN, 8, 128), F32),
            pltpu.VMEM((6, radial // JOIN * 8, 128), F32),
            pltpu.VMEM((radial // JOIN * 8, 128), I32),
            pltpu.VMEM((radial, 128), I32),
            pltpu.SMEM((radial, 128), I32),
            pltpu.VMEM((3, radial, 128), F32),
            pltpu.VMEM((3, nrow, 128), I32),
            dma,
        ],
        cost_estimate=pl.CostEstimate(flops=200000000, bytes_accessed=500000, transcendentals=0),
        name="move_nodes",
    )(grid_here.reshape(1).astype(I32), base, allp, alll)
    metric, allm, allt = pl.pallas_call(
        functools.partial(metric_kernel, nb, ng),
        out_shape=(
            sds((radial, lines), F32),
            sds((ng, 3, radial, lines), F32),
            sds((ng, radial, lines), F32),
        ),
        in_specs=[VMEM_SPEC],
        out_specs=[VMEM_SPEC] * 3,
        scratch_shapes=[
            pltpu.VMEM((2, 3, radial, lines), F32),
            dma((2,)),
            dma((2,)),
            dma((2 * ng,)),
            dma((ng,)),
            dma((2 * ng,)),
            dma((ng,)),
        ],
        compiler_params=pltpu.CompilerParams(collective_id=1, has_side_effects=True),
        name="metric",
    )(moved)
    fringe = pl.pallas_call(
        blend_kernel,
        out_shape=sds((nvar, radial, lines), F32),
        in_specs=[SMEM_SPEC] * 3 + [VMEM_SPEC] * 4,
        out_specs=VMEM_SPEC,
        scratch_shapes=[
            pltpu.VMEM((3, radial * 8, 128), F32),
            pltpu.VMEM((radial, 32, 128), BF16),
            pltpu.VMEM((3, ng * radial * 8, 128), F32),
            pltpu.VMEM((ng * radial * 8, 128), F32),
            pltpu.VMEM((radial * 8, 128), F32),
            pltpu.SMEM((nrow * 128 + 128,), I32),
            pltpu.SMEM((nrow * 128 + 128,), I32),
        ],
        name="blend",
    )(don, rec, num, moved, allm, allt, allf)
    return (
        moved.reshape(1, 3, planes, radial, lines),
        metric.reshape(1, planes, radial, lines),
        fringe.reshape(1, nvar, planes, radial, lines),
    )


def solution(mesh):
    in_specs = (
        P("grid", None, "bulk", None, None),
        P("grid", None, "bulk", None, None),
        P(None, ("bulk", "grid")),
        P(None, ("bulk", "grid")),
        P("grid", "bulk", None),
        P("grid", "bulk"),
        P("grid", "bulk"),
    )
    out_specs = (
        P("grid", None, "bulk", None, None),
        P("grid", "bulk", None, None),
        P("grid", None, "bulk", None, None),
    )
    return jax.shard_map(local, mesh=mesh, in_specs=in_specs, out_specs=out_specs, check_vma=False)
```

```python
import functools
import math

import jax
import jax.numpy as jnp
from jax import lax
from jax.experimental import pallas as pl
from jax.experimental.pallas import tpu as pltpu
from jax.sharding import PartitionSpec as P

MESH = pl.DeviceIdType.MESH
SUPPORT = 1.25
CULL = SUPPORT * SUPPORT * 1.0001
FAR = 1.0e9
JOIN = 2
TILES = 3
ENTRY_UNROLL = 32
F32 = jnp.float32
I32 = jnp.int32
BF16 = jnp.bfloat16
VMEM_SPEC = pl.BlockSpec(memory_space=pltpu.VMEM)
SMEM_SPEC = pl.BlockSpec(memory_space=pltpu.SMEM)


def take_lanes(x, idx):
    dims = lax.GatherDimensionNumbers(
        offset_dims=(),
        collapsed_slice_dims=(1,),
        start_index_map=(1,),
        operand_batching_dims=(0,),
        start_indices_batching_dims=(0,),
    )
    return lax.gather(
        x, idx[..., None], dims, slice_sizes=(1, 1), mode=lax.GatherScatterMode.PROMISE_IN_BOUNDS
    )


def iota(shape, axis):
    return lax.broadcasted_iota(I32, shape, axis)


def search(near, upper, marks, want):
    counts = jnp.dot(near, upper, preferred_element_type=F32).astype(I32)
    known = jnp.dot(near, marks, preferred_element_type=F32).astype(I32)
    high = known[:, 128:256] <= want
    pos = jnp.where(high, 64, 0)
    pos += jnp.where(jnp.where(high, known[:, 256:384], known[:, 0:128]) <= want, 32, 0)
    for step in (16, 8, 4, 2, 1):
        pos = jnp.where(take_lanes(counts, pos + (step - 1)) <= want, pos + step, pos)
    return pos, known[:, 384:512]


def halves(n):
    return (n // 2, 2) if n % 2 == 0 else (n, 1)


def line_and_pair(me, n):
    high, low = halves(n)
    place = lax.rem(me, low)
    line = [lax.rem(me // low + m, high) * low + place for m in range(1, high)]
    pair = [me + 1 - 2 * place] if low == 2 else []
    return line, pair


def split(x):
    high = x.astype(BF16).astype(F32)
    rest = x - high
    middle = rest.astype(BF16).astype(F32)
    return high, middle, rest - middle


def features(coords, extra, own):
    rows = []
    for x in coords:
        h, m, t = split(x)
        rows += [h, h, m, h, t, m] if own else [h, m, h, t, h, m]
    total = coords[0] * coords[0] + coords[1] * coords[1] + coords[2] * coords[2] + extra
    one = jnp.ones_like(total)
    square = list(split(total))
    return rows + (square + [one] * 3 if own else [one] * 3 + square)


def spread(shape, parts):
    depth = iota(shape, 0)
    return (depth < (128 // parts) * (iota(shape, 1) // 128 + 1)).astype(F32).astype(BF16)


def gather_kernel(
    nb,
    ng,
    rows,
    lrows,
    off_ref,
    cp_ref,
    rw_ref,
    po_ref,
    db_ref,
    rb_ref,
    flow_ref,
    base_ref,
    fil_ref,
    tot_ref,
    box_ref,
    midp_ref,
    nfeat_ref,
    don_ref,
    rec_ref,
    num_ref,
    allf_ref,
    pts,
    lst,
    allp,
    alll,
    pnt,
    node,
    mid,
    names,
    sp,
    rp,
    sl,
    rl,
    sf,
    rf,
):
    b = lax.axis_index("bulk")
    g = lax.axis_index("grid")
    gline, gpair = line_and_pair(g, ng)
    barrier = pltpu.get_barrier_semaphore()

    def there(i, j):
        return (lax.rem(b + i, nb), lax.rem(g + j, ng))

    peers = [there(0, j) for j in range(1, ng)] + [there(i, 0) for i in range(1, nb)]
    for peer in peers:
        pl.semaphore_signal(barrier, inc=1, device_id=peer, device_id_type=MESH)

    radial, lines = off_ref.shape[1:]
    slots = po_ref.shape[1]
    for c in range(3):
        for i in range(rows):
            pts[c * rows + i : c * rows + i + 1, :] = cp_ref[c : c + 1, 128 * i : 128 * i + 128]
            pts[(3 + c) * rows + i : (3 + c) * rows + i + 1, :] = rw_ref[c : c + 1, 128 * i : 128 * i + 128]
    for c, (ref, fill) in enumerate(((po_ref, -4 * ng), (db_ref, 0), (rb_ref, 0))):
        for i in range(lrows):
            at = c * lrows + i
            size = min(128, slots - 128 * i)
            if size < 128:
                lst[at : at + 1, :] = jnp.full((1, 128), fill, I32)
            lst[at : at + 1, 0:size] = ref[0:1, 128 * i : 128 * i + size]
    theta = jnp.full((1, 128), 2.0 * math.pi / nb, F32) * b.astype(F32)
    radius = 1.0 + 0.25 * iota((radial, 128), 0).astype(F32)
    height = 0.1 * iota((radial, 128), 1).astype(F32)
    base_ref[0] = (0.5 * g.astype(F32) + radius * jnp.cos(theta)) + off_ref[0]
    base_ref[1] = radius * jnp.sin(theta) + off_ref[1]
    base_ref[2] = height + off_ref[2]
    pl.semaphore_wait(barrier, len(peers))

    sent = {"p": [], "l": [], "f": []}

    def ring(i, j):
        return (-i % nb) * ng + (-j % ng)

    def send_points(source, slot, peer):
        copy = pltpu.make_async_remote_copy(
            src_ref=source,
            dst_ref=allp.at[slot],
            send_sem=sp.at[len(sent["p"])],
            recv_sem=rp.at[slot],
            device_id=peer,
            device_id_type=MESH,
        )
        copy.start()
        sent["p"].append(copy)

    def points_arrived(slot):
        pltpu.make_async_remote_copy(
            src_ref=pts,
            dst_ref=allp.at[slot],
            send_sem=sp.at[0],
            recv_sem=rp.at[slot],
            device_id=peers[0],
            device_id_type=MESH,
        ).wait_recv()

    def send(kind, slot, peer, own):
        source, full, ss, rs = {
            "l": (lst, alll, sl, rl),
            "f": (flow_ref, allf_ref, sf, rf),
        }[kind]
        copy = pltpu.make_async_remote_copy(
            src_ref=source if own else full.at[slot],
            dst_ref=full.at[slot],
            send_sem=ss.at[len(sent[kind])],
            recv_sem=rs.at[slot],
            device_id=peer,
            device_id_type=MESH,
        )
        copy.start()
        sent[kind].append(copy)

    def arrived(kind, slot):
        source, full, rs, ss = {"l": (lst, alll, rl, sl), "f": (flow_ref, allf_ref, rf, sf)}[kind]
        pltpu.make_async_remote_copy(
            src_ref=source,
            dst_ref=full.at[slot],
            send_sem=ss.at[0],
            recv_sem=rs.at[slot],
            device_id=peers[0],
            device_id_type=MESH,
        ).wait_recv()

    for j in range(1, ng):
        send_points(pts, ring(0, j), there(0, j))
    for i in range(1, nb):
        send_points(pts, ring(i, 0), there(i, 0))
    for j in range(1, ng):
        send("l", g, there(0, j), True)
    for t in gline + gpair:
        send("f", g, (b, t), True)
    allp[0] = pts[...]
    alll[g] = lst[...]

    npat = radial // JOIN
    lane8 = iota((8, 128), 1)
    sub8 = iota((8, 128), 0)
    blocks_of_lanes = lane8 // 16
    within = lane8 - 16 * blocks_of_lanes
    upper = (iota((128, 128), 0) <= iota((128, 128), 1)).astype(F32).astype(BF16)
    marks = spread((128, 512), 4)
    lows, highs = [], []
    for c in range(3):
        for jg in range(radial // 8):
            v = base_ref[c, 8 * jg : 8 * jg + 8, :]
            got = jnp.zeros((8, 128), F32)
            for j in range(8):
                row = jnp.broadcast_to(v[j : j + 1, :], (8, 128))
                got = jnp.where(blocks_of_lanes == j, take_lanes(row, 16 * sub8 + within), got)
            node[c, 8 * jg : 8 * jg + 8, :] = got
        full = node[c]
        lo = jnp.min(full, axis=1, keepdims=True)
        hi = jnp.max(full, axis=1, keepdims=True)
        for q in range(npat):
            mine = slice(q * JOIN, (q + 1) * JOIN)
            least = jnp.min(lo[mine], axis=0, keepdims=True)
            most = jnp.max(hi[mine], axis=0, keepdims=True)
            box_ref[2 * c, q] = jnp.broadcast_to(least, (8, 128))
            box_ref[2 * c + 1, q] = jnp.broadcast_to(most, (8, 128))
            half = (least + most) * 0.4
            mid[c, mine, :] = jnp.broadcast_to(half, (JOIN, 128))
            midp_ref[c, q * 4 : (q + 1) * 4, :] = jnp.broadcast_to(half, (4, 128))
        lows.append(jnp.min(lo, axis=0, keepdims=True))
        highs.append(jnp.max(hi, axis=0, keepdims=True))

    for j in range(1, ng):
        points_arrived(j)
        for i in range(1, nb):
            send_points(allp.at[j], (-i % nb) * ng + j, there(i, 0))
    mine = features([node[c] * 0.8 - mid[c] for c in range(3)], 0.0, True)
    for f in range(24):
        nfeat_ref[f // 8, pl.ds(f % 8, radial, stride=8), :] = mine[f] * (-2.0 if f < 18 else 1.0)

    chunk = ng * rows
    lane = iota((chunk, 128), 1)
    peak = jnp.zeros((8, 128), I32)
    for i in range(nb):
        for j in range(ng):
            d = i * ng + j
            if i:
                points_arrived(d)
            for c in range(6):
                pnt[c, d * rows : (d + 1) * rows, :] = allp[d, c * rows : (c + 1) * rows, :]
        mine = slice(i * chunk, (i + 1) * chunk)
        dist = jnp.zeros((chunk, 128), F32)
        for c in range(3):
            p = pnt[c, mine, :]
            e = jnp.maximum(jnp.maximum(lows[c] - p, p - highs[c]), 0.0)
            dist = dist + e * e
        near = (dist < CULL).astype(F32).astype(BF16)
        pos, total = search(near, upper, marks, lane)
        for r in range(chunk // 8):
            peak = jnp.maximum(peak, total[8 * r : 8 * r + 8])
        for c in range(6):
            v = take_lanes(pnt[c, mine, :], pos)
            v = jnp.where(lane < total, v, FAR if c < 3 else 0.0)
            fil_ref[c, :, mine] = v.T
        if i == 0:
            for s in gline:
                arrived("f", s)
                for t in gpair:
                    send("f", s, (b, t), False)
            for j in range(1, ng):
                arrived("l", lax.rem(g + j, ng))
            nrow = ng * lrows
            for k in range(ng):
                for c in range(3):
                    names[c, k * lrows : (k + 1) * lrows, :] = alll[k, c * lrows : (c + 1) * lrows, :]
            owner = iota((nrow, 128), 0) // lrows
            target = owner + 1 + names[0]
            target = jnp.where(target >= ng, target - ng, target)
            chosen = (target == g).astype(F32).astype(BF16)
            pos, total = search(chosen, upper, marks, iota((nrow, 128), 1))
            don_ref[...] = owner * radial + take_lanes(names[1], pos)
            rec_ref[...] = take_lanes(names[2], pos)
            num_ref[...] = total
    tot_ref[...] = peak
    other = gpair + [t + gpair[0] - g for t in gline] if gpair else []
    for s in other:
        arrived("f", s)
    for kind in sent:
        for copy in sent[kind]:
            copy.wait_send()


def rbf_kernel(
    base_ref, fil, tot_ref, box, midp, nfeat, moved_ref, out, basec, pfeat, wts, acc
):
    radial = base_ref.shape[1]
    npat = radial // JOIN
    lane8 = iota((8, 128), 1)
    sub8 = iota((8, 128), 0)
    blocks_of_lanes = lane8 // 16
    within = lane8 - 16 * blocks_of_lanes
    upper = (iota((128, 128), 0) <= iota((128, 128), 1)).astype(F32).astype(BF16)
    groups = (jnp.max(tot_ref[...]) + 7) // 8
    acc[...] = jnp.zeros(acc.shape, F32)
    wide = npat * 8
    none = jnp.zeros((8, 128), F32)
    low_sub = sub8 < 4
    lane_w = iota((wide, 128), 1)
    row_w = iota((wide, 128), 0)
    slot = jnp.where(row_w - 8 * (row_w // 8) < 4, lane_w, 127 - lane_w)
    marks = spread((128, 512), 4)

    def close(gi):
        start = pl.multiple_of(gi * 8, 8)
        src = [fil[c, pl.ds(start, 8), :][None] for c in range(6)]
        dist = jnp.zeros((npat, 8, 128), F32)
        for c in range(3):
            e = jnp.maximum(jnp.maximum(box[2 * c] - src[c], src[c] - box[2 * c + 1]), 0.0)
            dist = dist + e * e
        return src, (dist < CULL).astype(F32).reshape(wide, 128).astype(BF16)

    basec[...] = jnp.zeros(basec.shape, I32)

    @pl.loop(0, groups)
    def _(gi):
        _, near = close(gi)
        basec[...] += jnp.dot(near, marks[:, 384:512], preferred_element_type=F32).astype(I32)

    length = basec[...].reshape(npat, 8, 128)
    pair = length + jnp.concatenate([length[:, 4:8], length[:, 0:4]], axis=1)
    whole = jnp.max(pair) <= 128
    width = jnp.where(whole, 128, 64)
    pages = (jnp.max(length) + width - 1) // width

    @pl.loop(0, pages)
    def _(page):
        basec[...] = jnp.zeros(basec.shape, I32)
        out[...] = jnp.zeros(out.shape, F32)
        target = slot + width * page

        @pl.loop(0, groups)
        def _(gi):
            src, near = close(gi)
            before = basec[...]
            want = target - before
            pos, amount = search(near, upper, marks, want)
            keep = jnp.logical_and(jnp.logical_and(want >= 0, want < amount), slot < width)
            for c in range(6):
                v = jnp.broadcast_to(src[c], (npat, 8, 128)).reshape(wide, 128)
                out[c] = jnp.where(keep, take_lanes(v, pos), out[c])
            basec[...] = before + amount

        cols = []
        for c in range(6):
            parts = []
            for p in range(0, npat, 2):
                one = out[c, p * 8 : p * 8 + 8, :]
                two = out[c, p * 8 + 8 : p * 8 + 16, :]
                one = one + pltpu.roll(one, 4, 0)
                two = two + pltpu.roll(two, 4, 0)
                parts.append(jnp.where(low_sub, one, two))
            cols.append(jnp.concatenate(parts, axis=0))
        theirs = features([cols[c] * 0.8 - midp[c] for c in range(3)], 0.0, False)
        for f in range(24):
            pfeat[f // 8, pl.ds(f % 8, npat * 4, stride=8), :] = theirs[f]
        for c in range(8):
            wts[pl.ds(c, npat * 4, stride=8), :] = 4.0 * cols[3 + c] if c < 3 else jnp.zeros_like(cols[0])

        def tile(p):
            rhs = []
            for m in range(JOIN):
                row = pl.multiple_of((p * JOIN + m) * 8, 8)
                rhs.append(
                    jnp.concatenate([nfeat[t, pl.ds(row, 8), :] for t in range(3)] + [none], axis=0)
                )
            rhs = jnp.concatenate(rhs, axis=1).astype(BF16)
            total = None
            for r in range(4):
                row = pl.multiple_of((p * 4 + r) * 8, 8)
                lhs = jnp.concatenate([pfeat[t, pl.ds(row, 8), :] for t in range(3)] + [none], axis=0)
                sq = lax.dot_general(
                    lhs.astype(BF16), rhs, (((0,), (0,)), ((), ())), preferred_element_type=F32
                )
                sq = jnp.maximum(sq, 1e-30)
                near = jnp.maximum(1.0 - sq * lax.rsqrt(sq), 0.0)
                two = near * near
                phi = two * two * (1.25 - near)
                hi = phi.astype(BF16)
                lo = (phi - hi.astype(F32)).astype(BF16)
                vals = wts[pl.ds(row, 8), :]
                vhi = vals.astype(BF16).astype(F32)
                both = jnp.concatenate([vhi, vals - vhi], axis=0).astype(BF16)
                got = jnp.dot(
                    jnp.concatenate([both, both], axis=1),
                    jnp.concatenate([hi, lo], axis=0),
                    preferred_element_type=F32,
                )
                total = got if total is None else total + got
            return total[0:8] + total[8:16]

        @pl.loop(0, npat // TILES)
        def _(i):
            for q in range(TILES):
                p = i * TILES + q
                total = tile(p)
                for m in range(JOIN):
                    row = pl.multiple_of((p * JOIN + m) * 8, 8)
                    acc[pl.ds(row, 8), :] += total[:, 128 * m : 128 * m + 128]

    for c in range(3):
        for jg in range(radial // 8):
            s = acc[pl.ds(64 * jg + c, 8, stride=8), :]
            got = jnp.zeros((8, 128), F32)
            for kg in range(8):
                row = jnp.broadcast_to(s[kg : kg + 1, :], (8, 128))
                got = jnp.where(blocks_of_lanes == kg, take_lanes(row, 16 * sub8 + within), got)
            moved_ref[c, 8 * jg : 8 * jg + 8, :] = base_ref[c, 8 * jg : 8 * jg + 8, :] + got


def metric_kernel(nb, ng, mov_ref, met_ref, allm_ref, allt_ref, halo, sh, rh, sm, rm, st, rt):
    b = lax.axis_index("bulk")
    g = lax.axis_index("grid")
    after = lax.rem(b + 1, nb)
    before = lax.rem(b + nb - 1, nb)
    barrier = pltpu.get_barrier_semaphore()
    gline, gpair = line_and_pair(g, ng)
    peers = [(before, g), (after, g)] + [(b, t) for t in gline + gpair]
    for peer in peers:
        pl.semaphore_signal(barrier, inc=1, device_id=peer, device_id_type=MESH)
    pl.semaphore_wait(barrier, len(peers))
    halos = [
        pltpu.make_async_remote_copy(
            src_ref=mov_ref,
            dst_ref=halo.at[i],
            send_sem=sh.at[i],
            recv_sem=rh.at[i],
            device_id=(t, g),
            device_id_type=MESH,
        )
        for i, t in enumerate((after, before))
    ]
    for copy in halos:
        copy.start()

    sent = {"m": [], "t": []}

    def describe(kind, slot, peer, own, n):
        source, full, ss, rs = {
            "m": (mov_ref, allm_ref, sm, rm),
            "t": (met_ref, allt_ref, st, rt),
        }[kind]
        return pltpu.make_async_remote_copy(
            src_ref=source if own else full.at[slot],
            dst_ref=full.at[slot],
            send_sem=ss.at[n],
            recv_sem=rs.at[slot],
            device_id=peer,
            device_id_type=MESH,
        )

    def send(kind, slot, peer, own):
        copy = describe(kind, slot, peer, own, len(sent[kind]))
        copy.start()
        sent[kind].append(copy)

    for t in gline + gpair:
        send("m", g, (b, t), True)
    radial, lines = mov_ref.shape[1:]
    row = iota((radial, lines), 0)
    col = iota((radial, lines), 1)
    dj, dk = [], []
    for c in range(3):
        m = mov_ref[c]
        up, down = pltpu.roll(m, radial - 1, 0), pltpu.roll(m, 1, 0)
        dj.append(
            jnp.where(row == 0, up - m, jnp.where(row == radial - 1, m - down, (up - down) * 0.5))
        )
        up, down = pltpu.roll(m, lines - 1, 1), pltpu.roll(m, 1, 1)
        dk.append(
            jnp.where(col == 0, up - m, jnp.where(col == lines - 1, m - down, (up - down) * 0.5))
        )
    cross = [
        dj[1] * dk[2] - dj[2] * dk[1],
        dj[2] * dk[0] - dj[0] * dk[2],
        dj[0] * dk[1] - dj[1] * dk[0],
    ]
    for copy in halos:
        copy.wait_recv()
    di = [(halo[1, c] - halo[0, c]) * 0.5 for c in range(3)]
    met_ref[...] = di[0] * cross[0] + di[1] * cross[1] + di[2] * cross[2]
    for t in gline + gpair:
        send("t", g, (b, t), True)
    for kind in ("m", "t"):
        for s in gline:
            describe(kind, s, peers[0], False, 0).wait_recv()
            for t in gpair:
                send(kind, s, (b, t), False)
    other = gpair + [t + gpair[0] - g for t in gline] if gpair else []
    for kind in ("m", "t"):
        for s in other:
            describe(kind, s, peers[0], False, 0).wait_recv()
    for copy in halos + sent["m"] + sent["t"]:
        copy.wait_send()


def blend_kernel(
    don_ref, rec_ref, num_ref, mov_ref, allm_ref, allt_ref, flow_ref, out_ref, rows, own, far, val, acc, fcode, frecv
):
    radial = mov_ref.shape[1]
    nvar = out_ref.shape[0]
    nrow = num_ref.shape[0]
    ng = allm_ref.shape[0]
    zero = jnp.zeros((8, 128), F32)
    centre = []
    for c in range(3):
        m = jnp.sum(jnp.sum(mov_ref[c], axis=0, keepdims=True), axis=1, keepdims=True)
        centre.append(m * (1.0 / (radial * 128)))
    mine = features([mov_ref[c] - centre[c] for c in range(3)], 0.0, True)
    scale = [-2.0] * 18 + [1.0] * 6
    for f in range(24):
        rows[f // 8, pl.ds(f % 8, radial, stride=8), :] = mine[f] * scale[f]
    for r in range(radial):
        parts = [rows[p, r * 8 : (r + 1) * 8, :] for p in range(3)]
        own[r] = jnp.concatenate(parts + [zero], axis=0).astype(BF16)

    @pl.loop(0, ng)
    def _(k):
        theirs = features([allm_ref[k, c] - centre[c] for c in range(3)], 0.25, False)
        for f in range(24):
            far[f // 8, pl.ds(k * (radial * 8) + f % 8, radial, stride=8), :] = theirs[f]
        met = allt_ref[k]
        for v in range(8):
            row = met * flow_ref[k, v] if v < nvar else jnp.full((radial, 128), 1.0 if v == nvar else 0.0, F32)
            val[pl.ds(k * (radial * 8) + v, radial, stride=8), :] = row

    acc[...] = jnp.zeros(acc.shape, F32)

    def flatten(r, at):
        n = num_ref[r, 0]

        @pl.loop(0, (n + 7) // 8)
        def _(i):
            for u in range(8):
                fcode[at + i * 8 + u] = don_ref[r, i * 8 + u]
                frecv[at + i * 8 + u] = rec_ref[r, i * 8 + u]

        return at + n

    total = lax.fori_loop(0, nrow, flatten, jnp.int32(0))
    for u in range(ENTRY_UNROLL):
        fcode[total + u] = 0
        frecv[total + u] = 0

    @pl.loop(0, (total + ENTRY_UNROLL - 1) // ENTRY_UNROLL)
    def _(i):
        found = []
        for u in range(ENTRY_UNROLL):
            e = i * ENTRY_UNROLL + u
            code = fcode[e]
            recv = frecv[e]
            parts = [far[p, pl.ds(pl.multiple_of(code * 8, 8), 8), :] for p in range(3)]
            there = jnp.concatenate(parts + [zero], axis=0).astype(BF16)
            den = lax.dot_general(there, own[recv], (((0,), (0,)), ((), ())), preferred_element_type=F32)
            w = pl.reciprocal(den, approx=False)
            hi = w.astype(BF16)
            lo = (w - hi.astype(F32)).astype(BF16)
            vals = val[pl.ds(pl.multiple_of(code * 8, 8), 8), :]
            vhi = vals.astype(BF16).astype(F32)
            both = jnp.concatenate([vhi, vals - vhi], axis=0).astype(BF16)
            got = lax.dot_general(
                jnp.concatenate([both, both], axis=1),
                jnp.concatenate([hi, lo], axis=0),
                (((1,), (0,)), ((), ())),
                preferred_element_type=F32,
            )
            got = got[0:8] + got[8:16]
            got = got / got[nvar : nvar + 1, :]
            found.append((recv, jnp.where(e < total, got, 0.0)))
        for recv, got in found:
            first = pl.multiple_of(recv * 8, 8)
            acc[pl.ds(first, 8), :] += got

    for v in range(nvar):
        out_ref[v] = acc[pl.ds(v, radial, stride=8), :]


def local(offsets, flow, control_points, rbf_weights, peer_offset, donor_block, receptor_block):
    _, _, planes, radial, lines = offsets.shape
    nvar = flow.shape[1]
    nb = lax.axis_size("bulk")
    ng = lax.axis_size("grid")
    nd = nb * ng
    nd = nb * ng
    rows = control_points.shape[1] // 128
    slots = donor_block.shape[1]
    lrows = -(-slots // 128)
    nrow = ng * lrows
    npat = radial // JOIN
    dma = pltpu.SemaphoreType.DMA
    sds = jax.ShapeDtypeStruct
    base, fil, tot, box, midp, nfeat, don, rec, num, allf = pl.pallas_call(
        functools.partial(gather_kernel, nb, ng, rows, lrows),
        out_shape=(
            sds((3, radial, lines), F32),
            sds((6, 128, 128), F32),
            sds((8, 128), I32),
            sds((6, npat, 8, 128), F32),
            sds((3, npat * 4, 128), F32),
            sds((3, radial * 8, 128), F32),
            sds((nrow, 128), I32),
            sds((nrow, 128), I32),
            sds((nrow, 128), I32),
            sds((ng, nvar, radial, lines), F32),
        ),
        in_specs=[VMEM_SPEC] * 7,
        out_specs=[VMEM_SPEC] * 10,
        scratch_shapes=[
            pltpu.VMEM((6 * rows, 128), F32),
            pltpu.VMEM((3 * lrows, 128), I32),
            pltpu.VMEM((nd, 6 * rows, 128), F32),
            pltpu.VMEM((ng, 3 * lrows, 128), I32),
            pltpu.VMEM((6, nd * rows, 128), F32),
            pltpu.VMEM((3, radial, 128), F32),
            pltpu.VMEM((3, radial, 128), F32),
            pltpu.VMEM((3, nrow, 128), I32),
            dma((nd,)),
            dma((nd,)),
            dma((ng,)),
            dma((ng,)),
            dma((2 * ng,)),
            dma((ng,)),
        ],
        compiler_params=pltpu.CompilerParams(collective_id=0, has_side_effects=True),
        name="gather_points",
    )(
        offsets.reshape(3, radial, lines),
        control_points,
        rbf_weights,
        peer_offset.reshape(1, slots),
        donor_block,
        receptor_block,
        flow.reshape(nvar, radial, lines),
    )
    moved = pl.pallas_call(
        rbf_kernel,
        out_shape=sds((3, radial, lines), F32),
        in_specs=[VMEM_SPEC] * 6,
        out_specs=VMEM_SPEC,
        scratch_shapes=[
            pltpu.VMEM((6, npat * 8, 128), F32),
            pltpu.VMEM((npat * 8, 128), I32),
            pltpu.VMEM((3, npat * 32, 128), F32),
            pltpu.VMEM((npat * 32, 128), F32),
            pltpu.VMEM((radial * 8, 128), F32),
        ],
        name="move_nodes",
    )(base, fil, tot, box, midp, nfeat)
    metric, allm, allt = pl.pallas_call(
        functools.partial(metric_kernel, nb, ng),
        out_shape=(
            sds((radial, lines), F32),
            sds((ng, 3, radial, lines), F32),
            sds((ng, radial, lines), F32),
        ),
        in_specs=[VMEM_SPEC],
        out_specs=[VMEM_SPEC] * 3,
        scratch_shapes=[
            pltpu.VMEM((2, 3, radial, lines), F32),
            dma((2,)),
            dma((2,)),
            dma((2 * ng,)),
            dma((ng,)),
            dma((2 * ng,)),
            dma((ng,)),
        ],
        compiler_params=pltpu.CompilerParams(collective_id=1, has_side_effects=True),
        name="metric",
    )(moved)
    fringe = pl.pallas_call(
        blend_kernel,
        out_shape=sds((nvar, radial, lines), F32),
        in_specs=[SMEM_SPEC] * 3 + [VMEM_SPEC] * 4,
        out_specs=VMEM_SPEC,
        scratch_shapes=[
            pltpu.VMEM((3, radial * 8, 128), F32),
            pltpu.VMEM((radial, 32, 128), BF16),
            pltpu.VMEM((3, ng * radial * 8, 128), F32),
            pltpu.VMEM((ng * radial * 8, 128), F32),
            pltpu.VMEM((radial * 8, 128), F32),
            pltpu.SMEM((nrow * 128 + 128,), I32),
            pltpu.SMEM((nrow * 128 + 128,), I32),
        ],
        name="blend",
    )(don, rec, num, moved, allm, allt, allf)
    return (
        moved.reshape(1, 3, planes, radial, lines),
        metric.reshape(1, planes, radial, lines),
        fringe.reshape(1, nvar, planes, radial, lines),
    )


def solution(mesh):
    in_specs = (
        P("grid", None, "bulk", None, None),
        P("grid", None, "bulk", None, None),
        P(None, ("bulk", "grid")),
        P(None, ("bulk", "grid")),
        P("grid", "bulk", None),
        P("grid", "bulk"),
        P("grid", "bulk"),
    )
    out_specs = (
        P("grid", None, "bulk", None, None),
        P("grid", "bulk", None, None),
        P("grid", None, "bulk", None, None),
    )
    return jax.shard_map(local, mesh=mesh, in_specs=in_specs, out_specs=out_specs, check_vma=False)
```

```python
import functools
import math

import jax
import jax.numpy as jnp
from jax import lax
from jax.experimental import pallas as pl
from jax.experimental.pallas import tpu as pltpu
from jax.sharding import PartitionSpec as P

MESH = pl.DeviceIdType.MESH
SUPPORT = 1.25
CULL = SUPPORT * SUPPORT * 1.0001
FAR = 1.0e9
JOIN = 2
TILES = 3
MOST = 28
HALF = MOST // 2
HOLD = 32
F32 = jnp.float32
I32 = jnp.int32
BF16 = jnp.bfloat16
VMEM_SPEC = pl.BlockSpec(memory_space=pltpu.VMEM)
SMEM_SPEC = pl.BlockSpec(memory_space=pltpu.SMEM)


def take_lanes(x, idx):
    dims = lax.GatherDimensionNumbers(
        offset_dims=(),
        collapsed_slice_dims=(1,),
        start_index_map=(1,),
        operand_batching_dims=(0,),
        start_indices_batching_dims=(0,),
    )
    return lax.gather(
        x, idx[..., None], dims, slice_sizes=(1, 1), mode=lax.GatherScatterMode.PROMISE_IN_BOUNDS
    )


def iota(shape, axis):
    return lax.broadcasted_iota(I32, shape, axis)


def search(near, upper, marks, want):
    counts = jnp.dot(near, upper, preferred_element_type=F32).astype(I32)
    known = jnp.dot(near, marks, preferred_element_type=F32).astype(I32)
    high = known[:, 128:256] <= want
    pos = jnp.where(high, 64, 0)
    pos += jnp.where(jnp.where(high, known[:, 256:384], known[:, 0:128]) <= want, 32, 0)
    for step in (16, 8, 4, 2, 1):
        pos = jnp.where(take_lanes(counts, pos + (step - 1)) <= want, pos + step, pos)
    return pos, known[:, 384:512]


def halves(n):
    return (n // 2, 2) if n % 2 == 0 else (n, 1)


def split(x):
    high = x.astype(BF16).astype(F32)
    rest = x - high
    middle = rest.astype(BF16).astype(F32)
    return high, middle, rest - middle


def features(coords, extra, own):
    rows = []
    for x in coords:
        h, m, t = split(x)
        rows += [h, h, m, h, t, m] if own else [h, m, h, t, h, m]
    total = coords[0] * coords[0] + coords[1] * coords[1] + coords[2] * coords[2] + extra
    one = jnp.ones_like(total)
    square = list(split(total))
    return rows + (square + [one] * 3 if own else [one] * 3 + square)


def spread(shape, parts):
    depth = iota(shape, 0)
    return (depth < (128 // parts) * (iota(shape, 1) // 128 + 1)).astype(F32).astype(BF16)


def gather_kernel(
    nb,
    ng,
    rows,
    lrows,
    off_ref,
    cp_ref,
    rw_ref,
    po_ref,
    db_ref,
    rb_ref,
    base_ref,
    fil_ref,
    tot_ref,
    box_ref,
    midp_ref,
    nfeat_ref,
    don_ref,
    rec_ref,
    name_ref,
    pts,
    lst,
    allp,
    alll,
    pnt,
    node,
    mid,
    names,
    sp,
    rp,
    sl,
    rl,
):
    b = lax.axis_index("bulk")
    g = lax.axis_index("grid")
    barrier = pltpu.get_barrier_semaphore()

    def there(i, j):
        return (lax.rem(b + i, nb), lax.rem(g + j, ng))

    peers = [there(0, j) for j in range(1, ng)] + [there(i, 0) for i in range(1, nb)]
    for peer in peers:
        pl.semaphore_signal(barrier, inc=1, device_id=peer, device_id_type=MESH)

    radial, lines = off_ref.shape[1:]
    slots = po_ref.shape[1]
    for c in range(3):
        for i in range(rows):
            pts[c * rows + i : c * rows + i + 1, :] = cp_ref[c : c + 1, 128 * i : 128 * i + 128]
            pts[(3 + c) * rows + i : (3 + c) * rows + i + 1, :] = rw_ref[c : c + 1, 128 * i : 128 * i + 128]
    for c, (ref, fill) in enumerate(((po_ref, -4 * ng), (db_ref, 0), (rb_ref, 0))):
        for i in range(lrows):
            at = c * lrows + i
            size = min(128, slots - 128 * i)
            if size < 128:
                lst[at : at + 1, :] = jnp.full((1, 128), fill, I32)
            lst[at : at + 1, 0:size] = ref[0:1, 128 * i : 128 * i + size]
    theta = jnp.full((1, 128), 2.0 * math.pi / nb, F32) * b.astype(F32)
    radius = 1.0 + 0.25 * iota((radial, 128), 0).astype(F32)
    height = 0.1 * iota((radial, 128), 1).astype(F32)
    base_ref[0] = (0.5 * g.astype(F32) + radius * jnp.cos(theta)) + off_ref[0]
    base_ref[1] = radius * jnp.sin(theta) + off_ref[1]
    base_ref[2] = height + off_ref[2]
    pl.semaphore_wait(barrier, len(peers))

    sent = {"p": [], "l": []}

    def ring(i, j):
        return (-i % nb) * ng + (-j % ng)

    def send_points(source, slot, peer):
        copy = pltpu.make_async_remote_copy(
            src_ref=source,
            dst_ref=allp.at[slot],
            send_sem=sp.at[len(sent["p"])],
            recv_sem=rp.at[slot],
            device_id=peer,
            device_id_type=MESH,
        )
        copy.start()
        sent["p"].append(copy)

    def points_arrived(slot):
        pltpu.make_async_remote_copy(
            src_ref=pts,
            dst_ref=allp.at[slot],
            send_sem=sp.at[0],
            recv_sem=rp.at[slot],
            device_id=peers[0],
            device_id_type=MESH,
        ).wait_recv()

    def list_copy(slot, n, peer):
        return pltpu.make_async_remote_copy(
            src_ref=lst,
            dst_ref=alll.at[slot],
            send_sem=sl.at[n],
            recv_sem=rl.at[slot],
            device_id=peer,
            device_id_type=MESH,
        )

    for j in range(1, ng):
        send_points(pts, ring(0, j), there(0, j))
    for i in range(1, nb):
        send_points(pts, ring(i, 0), there(i, 0))
    for j in range(1, ng):
        copy = list_copy(g, j, there(0, j))
        copy.start()
        sent["l"].append(copy)
    allp[0] = pts[...]
    alll[g] = lst[...]

    npat = radial // JOIN
    lane8 = iota((8, 128), 1)
    sub8 = iota((8, 128), 0)
    blocks_of_lanes = lane8 // 16
    within = lane8 - 16 * blocks_of_lanes
    upper = (iota((128, 128), 0) <= iota((128, 128), 1)).astype(F32).astype(BF16)
    marks = spread((128, 512), 4)
    lows, highs = [], []
    for c in range(3):
        for jg in range(radial // 8):
            v = base_ref[c, 8 * jg : 8 * jg + 8, :]
            got = jnp.zeros((8, 128), F32)
            for j in range(8):
                row = jnp.broadcast_to(v[j : j + 1, :], (8, 128))
                got = jnp.where(blocks_of_lanes == j, take_lanes(row, 16 * sub8 + within), got)
            node[c, 8 * jg : 8 * jg + 8, :] = got
        full = node[c]
        lo = jnp.min(full, axis=1, keepdims=True)
        hi = jnp.max(full, axis=1, keepdims=True)
        for q in range(npat):
            mine = slice(q * JOIN, (q + 1) * JOIN)
            least = jnp.min(lo[mine], axis=0, keepdims=True)
            most = jnp.max(hi[mine], axis=0, keepdims=True)
            box_ref[2 * c, q] = jnp.broadcast_to(least, (8, 128))
            box_ref[2 * c + 1, q] = jnp.broadcast_to(most, (8, 128))
            half = (least + most) * 0.4
            mid[c, mine, :] = jnp.broadcast_to(half, (JOIN, 128))
            midp_ref[c, q * 4 : (q + 1) * 4, :] = jnp.broadcast_to(half, (4, 128))
        lows.append(jnp.min(lo, axis=0, keepdims=True))
        highs.append(jnp.max(hi, axis=0, keepdims=True))

    for j in range(1, ng):
        points_arrived(j)
        for i in range(1, nb):
            send_points(allp.at[j], (-i % nb) * ng + j, there(i, 0))
    mine = features([node[c] * 0.8 - mid[c] for c in range(3)], 0.0, True)
    for f in range(24):
        nfeat_ref[f // 8, pl.ds(f % 8, radial, stride=8), :] = mine[f] * (-2.0 if f < 18 else 1.0)

    chunk = ng * rows
    lane = iota((chunk, 128), 1)
    peak = jnp.zeros((8, 128), I32)
    for i in range(nb):
        for j in range(ng):
            d = i * ng + j
            if i:
                points_arrived(d)
            for c in range(6):
                pnt[c, d * rows : (d + 1) * rows, :] = allp[d, c * rows : (c + 1) * rows, :]
        mine = slice(i * chunk, (i + 1) * chunk)
        dist = jnp.zeros((chunk, 128), F32)
        for c in range(3):
            p = pnt[c, mine, :]
            e = jnp.maximum(jnp.maximum(lows[c] - p, p - highs[c]), 0.0)
            dist = dist + e * e
        near = (dist < CULL).astype(F32).astype(BF16)
        pos, total = search(near, upper, marks, lane)
        for r in range(chunk // 8):
            peak = jnp.maximum(peak, total[8 * r : 8 * r + 8])
        for c in range(6):
            v = take_lanes(pnt[c, mine, :], pos)
            v = jnp.where(lane < total, v, FAR if c < 3 else 0.0)
            fil_ref[c, :, mine] = v.T
        if i == 0:
            for j in range(1, ng):
                list_copy(lax.rem(g + j, ng), 0, peers[0]).wait_recv()
            for k in range(ng):
                for r in range(3 * lrows):
                    names[r, k : k + 1, :] = alll[k, r : r + 1, :]
            owner = iota((ng, 128), 0)
            place = iota((ng, 128), 1)
            before = jnp.zeros((ng, 128), I32)
            don = jnp.zeros((ng, 128), I32)
            rec = jnp.zeros((ng, 128), I32)
            for r in range(lrows):
                target = owner + 1 + names[r]
                target = jnp.where(target >= ng, target - ng, target)
                chosen = (target == g).astype(F32).astype(BF16)
                want = place - before
                pos, total = search(chosen, upper, marks, want)
                keep = jnp.logical_and(want >= 0, want < total)
                don = jnp.where(keep, take_lanes(names[lrows + r], pos), don)
                rec = jnp.where(keep, take_lanes(names[2 * lrows + r], pos), rec)
                before = before + total
            don_ref[...] = don
            rec_ref[...] = rec
            name_ref[...] = jnp.where(place < before, rec, -1)
    tot_ref[...] = peak
    for kind in sent:
        for copy in sent[kind]:
            copy.wait_send()


def tile(p, nfeat, pfeat, wts):
    none = jnp.zeros((8, 128), F32)
    rhs = []
    for m in range(JOIN):
        row = pl.multiple_of((p * JOIN + m) * 8, 8)
        rhs.append(
            jnp.concatenate([nfeat[t, pl.ds(row, 8), :] for t in range(3)] + [none], axis=0)
        )
    rhs = jnp.concatenate(rhs, axis=1).astype(BF16)
    total = None
    for r in range(4):
        row = pl.multiple_of((p * 4 + r) * 8, 8)
        lhs = jnp.concatenate([pfeat[t, pl.ds(row, 8), :] for t in range(3)] + [none], axis=0)
        sq = lax.dot_general(
            lhs.astype(BF16), rhs, (((0,), (0,)), ((), ())), preferred_element_type=F32
        )
        sq = jnp.maximum(sq, 1e-30)
        near = jnp.maximum(1.0 - sq * lax.rsqrt(sq), 0.0)
        two = near * near
        phi = two * two * (1.25 - near)
        hi = phi.astype(BF16)
        lo = (phi - hi.astype(F32)).astype(BF16)
        vals = wts[pl.ds(row, 8), :]
        vhi = vals.astype(BF16).astype(F32)
        both = jnp.concatenate([vhi, vals - vhi], axis=0).astype(BF16)
        got = jnp.dot(
            jnp.concatenate([both, both], axis=1),
            jnp.concatenate([hi, lo], axis=0),
            preferred_element_type=F32,
        )
        total = got if total is None else total + got
    return total[0:8] + total[8:16]


def evaluate(npat, nfeat, pfeat, wts, acc):
    @pl.loop(0, npat // TILES)
    def _(i):
        for q in range(TILES):
            p = i * TILES + q
            total = tile(p, nfeat, pfeat, wts)
            for m in range(JOIN):
                row = pl.multiple_of((p * JOIN + m) * 8, 8)
                acc[pl.ds(row, 8), :] += total[:, 128 * m : 128 * m + 128]


def cull_kernel(
    fil, tot_ref, box, midp, nfeat, pfeat_ref, wts_ref, acc_ref, out, basec, pmore, wmore
):
    npat = box.shape[1]
    sub8 = iota((8, 128), 0)
    upper = (iota((128, 128), 0) <= iota((128, 128), 1)).astype(F32).astype(BF16)
    groups = (jnp.max(tot_ref[...]) + 7) // 8
    wide = npat * 8
    low_sub = sub8 < 4
    lane_w = iota((wide, 128), 1)
    row_w = iota((wide, 128), 0)
    slot = jnp.where(row_w - 8 * (row_w // 8) < 4, lane_w, 127 - lane_w)
    marks = spread((128, 512), 4)

    def close(gi):
        start = pl.multiple_of(gi * 8, 8)
        src = [fil[c, pl.ds(start, 8), :][None] for c in range(6)]
        dist = jnp.zeros((npat, 8, 128), F32)
        for c in range(3):
            e = jnp.maximum(jnp.maximum(box[2 * c] - src[c], src[c] - box[2 * c + 1]), 0.0)
            dist = dist + e * e
        return src, (dist < CULL).astype(F32).reshape(wide, 128).astype(BF16)

    basec[...] = jnp.zeros(basec.shape, I32)

    @pl.loop(0, groups)
    def _(gi):
        _, near = close(gi)
        basec[...] += jnp.dot(near, marks[:, 384:512], preferred_element_type=F32).astype(I32)

    length = basec[...].reshape(npat, 8, 128)
    pair = length + jnp.concatenate([length[:, 4:8], length[:, 0:4]], axis=1)
    whole = jnp.max(pair) <= 128
    width = jnp.where(whole, 128, 64)
    pages = (jnp.max(length) + width - 1) // width

    def compact(page, pfeat, wts):
        basec[...] = jnp.zeros(basec.shape, I32)
        out[...] = jnp.zeros(out.shape, F32)
        target = slot + width * page

        @pl.loop(0, groups)
        def _(gi):
            src, near = close(gi)
            before = basec[...]
            want = target - before
            pos, amount = search(near, upper, marks, want)
            keep = jnp.logical_and(jnp.logical_and(want >= 0, want < amount), slot < width)
            for c in range(6):
                v = jnp.broadcast_to(src[c], (npat, 8, 128)).reshape(wide, 128)
                out[c] = jnp.where(keep, take_lanes(v, pos), out[c])
            basec[...] = before + amount

        cols = []
        for c in range(6):
            parts = []
            for p in range(0, npat, 2):
                one = out[c, p * 8 : p * 8 + 8, :]
                two = out[c, p * 8 + 8 : p * 8 + 16, :]
                one = one + pltpu.roll(one, 4, 0)
                two = two + pltpu.roll(two, 4, 0)
                parts.append(jnp.where(low_sub, one, two))
            cols.append(jnp.concatenate(parts, axis=0))
        theirs = features([cols[c] * 0.8 - midp[c] for c in range(3)], 0.0, False)
        for f in range(24):
            pfeat[f // 8, pl.ds(f % 8, npat * 4, stride=8), :] = theirs[f]
        for c in range(8):
            wts[pl.ds(c, npat * 4, stride=8), :] = 4.0 * cols[3 + c] if c < 3 else jnp.zeros_like(cols[0])

    compact(0, pfeat_ref, wts_ref)
    acc_ref[...] = jnp.zeros(acc_ref.shape, F32)

    @pl.loop(1, pages)
    def _(page):
        compact(page, pmore, wmore)
        evaluate(npat, nfeat, pmore, wmore, acc_ref)


def finish_kernel(
    nb,
    ng,
    don_ref,
    rec_ref,
    name_ref,
    base_ref,
    nfeat_ref,
    pfeat_ref,
    wts_ref,
    more_ref,
    flow_ref,
    mov_ref,
    met_ref,
    out_ref,
    acc,
    halo,
    allm,
    allt,
    allf,
    rows,
    own,
    far,
    val,
    wone,
    wtwo,
    res,
    sh,
    rh,
    sm,
    rm,
    st,
    rt,
    sf,
    rf,
):
    b = lax.axis_index("bulk")
    g = lax.axis_index("grid")
    after = lax.rem(b + 1, nb)
    before = lax.rem(b + nb - 1, nb)
    high, low = halves(ng)
    along = g // low
    place = g - along * low

    def source(t):
        flip = t // high
        return lax.rem(along + (t - flip * high), high) * low + lax.rem(place + flip, low)

    near = [source(t) for t in range(1, high)]
    pair = [source(high)] if low == 2 else []
    barrier = pltpu.get_barrier_semaphore()
    peers = [(before, g), (after, g)] + [(b, source(t)) for t in range(1, ng)]
    for peer in peers:
        pl.semaphore_signal(barrier, inc=1, device_id=peer, device_id_type=MESH)

    radial, lines = mov_ref.shape[1:]
    nvar = out_ref.shape[0]
    acc[...] = more_ref[...]
    evaluate(radial // JOIN, nfeat_ref, pfeat_ref, wts_ref, acc)
    lane8 = iota((8, 128), 1)
    sub8 = iota((8, 128), 0)
    blocks_of_lanes = lane8 // 16
    within = lane8 - 16 * blocks_of_lanes
    for c in range(3):
        for jg in range(radial // 8):
            s = acc[pl.ds(64 * jg + c, 8, stride=8), :]
            got = jnp.zeros((8, 128), F32)
            for kg in range(8):
                row = jnp.broadcast_to(s[kg : kg + 1, :], (8, 128))
                got = jnp.where(blocks_of_lanes == kg, take_lanes(row, 16 * sub8 + within), got)
            mov_ref[c, 8 * jg : 8 * jg + 8, :] = base_ref[c, 8 * jg : 8 * jg + 8, :] + got
    pl.semaphore_wait(barrier, len(peers))
    halos = [
        pltpu.make_async_remote_copy(
            src_ref=mov_ref,
            dst_ref=halo.at[i],
            send_sem=sh.at[i],
            recv_sem=rh.at[i],
            device_id=(t, g),
            device_id_type=MESH,
        )
        for i, t in enumerate((after, before))
    ]
    for copy in halos:
        copy.start()
    sent = {"m": [], "t": [], "f": []}

    def describe(kind, slot, peer, mine, n):
        src, full, ss, rs = {
            "m": (mov_ref, allm, sm, rm),
            "t": (met_ref, allt, st, rt),
            "f": (flow_ref, allf, sf, rf),
        }[kind]
        return pltpu.make_async_remote_copy(
            src_ref=src if mine else full.at[slot],
            dst_ref=full.at[slot],
            send_sem=ss.at[n],
            recv_sem=rs.at[slot],
            device_id=(b, peer),
            device_id_type=MESH,
        )

    def send(kind, slot, peer, mine):
        copy = describe(kind, slot, peer, mine, len(sent[kind]))
        copy.start()
        sent[kind].append(copy)

    def arrived(kind, slot):
        describe(kind, slot, source(1), False, 0).wait_recv()

    for kind in ("m", "f"):
        for t in pair + near:
            send(kind, g, t, True)
    row = iota((radial, lines), 0)
    col = iota((radial, lines), 1)
    dj, dk, centre = [], [], []
    for c in range(3):
        m = mov_ref[c]
        up, down = pltpu.roll(m, radial - 1, 0), pltpu.roll(m, 1, 0)
        dj.append(
            jnp.where(row == 0, up - m, jnp.where(row == radial - 1, m - down, (up - down) * 0.5))
        )
        up, down = pltpu.roll(m, lines - 1, 1), pltpu.roll(m, 1, 1)
        dk.append(
            jnp.where(col == 0, up - m, jnp.where(col == lines - 1, m - down, (up - down) * 0.5))
        )
        total = jnp.sum(jnp.sum(m, axis=0, keepdims=True), axis=1, keepdims=True)
        centre.append(total * (1.0 / (radial * lines)))
    cross = [
        dj[1] * dk[2] - dj[2] * dk[1],
        dj[2] * dk[0] - dj[0] * dk[2],
        dj[0] * dk[1] - dj[1] * dk[0],
    ]
    zero = jnp.zeros((8, 128), F32)
    mine = features([mov_ref[c] - centre[c] for c in range(3)], 0.0, True)
    for f in range(24):
        rows[f // 8, pl.ds(f % 8, radial, stride=8), :] = mine[f] * (-2.0 if f < 18 else 1.0)
    for r in range(radial):
        parts = [rows[p, r * 8 : (r + 1) * 8, :] for p in range(3)]
        own[r] = jnp.concatenate(parts + [zero], axis=0).astype(BF16)
    res[...] = jnp.zeros(res.shape, F32)

    for copy in halos:
        copy.wait_recv()
    di = [(halo[1, c] - halo[0, c]) * 0.5 for c in range(3)]
    met_ref[...] = di[0] * cross[0] + di[1] * cross[1] + di[2] * cross[2]
    for t in range(ng - 1, 0, -1):
        send("t", g, source(t), True)
    for s in near:
        arrived("m", s)
        for t in pair:
            send("m", s, t, False)

    none = jnp.zeros((32, 128), BF16)

    def prepare(t, far):
        s = source(t)
        theirs = features([allm[s, c] - centre[c] for c in range(3)], 0.25, False)
        for f in range(24):
            rows[f // 8, pl.ds(f % 8, radial, stride=8), :] = theirs[f]
        for r in range(radial):
            for p in range(3):
                far[p, r] = rows[p, r * 8 : (r + 1) * 8, :]

    def weigh(t, e, far, wgt, slot):
        s = source(t)
        left, right = [], []
        for q in range(2):
            left += [far[p, don_ref[s, e + q]] for p in range(3)] + [zero]
            right.append(own[rec_ref[s, e + q]])
        right = [
            jnp.concatenate([right[0], none], axis=1),
            jnp.concatenate([none, right[1]], axis=1),
        ]
        den = lax.dot_general(
            jnp.concatenate(left, axis=0).astype(BF16),
            jnp.concatenate(right, axis=0),
            (((0,), (0,)), ((), ())),
            preferred_element_type=F32,
        )
        w = pl.reciprocal(den, approx=False)
        hi = w.astype(BF16)
        wgt[slot * HALF + e // 2, 0:128, :] = hi
        wgt[slot * HALF + e // 2, 128:256, :] = (w - hi.astype(F32)).astype(BF16)

    def load(t):
        s = source(t)
        met = allt[s]
        for v in range(8):
            row = met * allf[s, v] if v < nvar else jnp.full((radial, 128), 1.0 if v == nvar else 0.0, F32)
            rows[0, pl.ds(v, radial, stride=8), :] = row
        for r in range(radial):
            val[r] = rows[0, r * 8 : (r + 1) * 8, :]

    def blend(t, e, wgt, slot):
        s = source(t)
        left = []
        for q in range(2):
            vals = val[don_ref[s, e + q]]
            vhi = vals.astype(BF16).astype(F32)
            both = jnp.concatenate([vhi, vals - vhi], axis=0).astype(BF16)
            left.append(jnp.concatenate([both, both], axis=1))
        got = jnp.dot(
            jnp.concatenate(left, axis=0),
            wgt[slot * HALF + e // 2],
            preferred_element_type=F32,
        )
        for q in range(2):
            one = got[16 * q : 16 * q + 8, 128 * q : 128 * q + 128]
            one = one + got[16 * q + 8 : 16 * q + 16, 128 * q : 128 * q + 128]
            one = one / one[nvar : nvar + 1, :]
            at = pl.multiple_of((t * HOLD + e + q) * 8, 8)
            res[pl.ds(at, 8), :] = one

    for s in pair:
        arrived("m", s)
    first = high if pair else high - 1
    rest = ng - 1 - first

    @pl.loop(1, first + 1)
    def _(t):
        prepare(t, far)
        for e in range(0, MOST, 2):
            weigh(t, e, far, wone, t - 1)

    for s in near:
        arrived("f", s)
        for t in pair:
            send("f", s, t, False)
    for s in pair:
        arrived("f", s)

    @pl.loop(1, rest + 1)
    def _(t):
        arrived("m", source(first + t))
        arrived("t", source(t))
        prepare(first + t, far)
        load(t)
        for e in range(0, MOST, 2):
            weigh(first + t, e, far, wtwo, t - 1)
            blend(t, e, wone, t - 1)

    @pl.loop(rest + 1, first + 1)
    def _(t):
        arrived("t", source(t))
        load(t)
        for e in range(0, MOST, 2):
            blend(t, e, wone, t - 1)

    @pl.loop(first + 1, ng)
    def _(t):
        arrived("f", source(t))
        arrived("t", source(t))
        load(t)
        for e in range(0, MOST, 2):
            blend(t, e, wtwo, t - first - 1)

    total = None
    blocks = iota((radial, 128), 0)
    for t in range(1, ng):
        name = jnp.broadcast_to(name_ref[pl.ds(source(t), 1), :], (radial, 128))
        pick = (name == blocks).astype(F32).astype(BF16)[:, 0:HOLD]
        cols = [res[pl.ds(t * HOLD * 8 + v, HOLD, stride=8), :] for v in range(nvar)]
        for part in split(jnp.concatenate(cols, axis=1)):
            got = jnp.dot(pick, part.astype(BF16), preferred_element_type=F32)
            total = got if total is None else total + got
    for v in range(nvar):
        out_ref[v] = total[:, 128 * v : 128 * v + 128]
    for copy in halos + sent["m"] + sent["t"] + sent["f"]:
        copy.wait_send()


def local(offsets, flow, control_points, rbf_weights, peer_offset, donor_block, receptor_block):
    _, _, planes, radial, lines = offsets.shape
    nvar = flow.shape[1]
    nb = lax.axis_size("bulk")
    ng = lax.axis_size("grid")
    nd = nb * ng
    nd = nb * ng
    rows = control_points.shape[1] // 128
    slots = donor_block.shape[1]
    lrows = -(-slots // 128)
    npat = radial // JOIN
    dma = pltpu.SemaphoreType.DMA
    sds = jax.ShapeDtypeStruct
    base, fil, tot, box, midp, nfeat, don, rec, name = pl.pallas_call(
        functools.partial(gather_kernel, nb, ng, rows, lrows),
        out_shape=(
            sds((3, radial, lines), F32),
            sds((6, 128, 128), F32),
            sds((8, 128), I32),
            sds((6, npat, 8, 128), F32),
            sds((3, npat * 4, 128), F32),
            sds((3, radial * 8, 128), F32),
            sds((ng, 128), I32),
            sds((ng, 128), I32),
            sds((ng, 128), I32),
        ),
        in_specs=[VMEM_SPEC] * 6,
        out_specs=[VMEM_SPEC] * 9,
        scratch_shapes=[
            pltpu.VMEM((6 * rows, 128), F32),
            pltpu.VMEM((3 * lrows, 128), I32),
            pltpu.VMEM((nd, 6 * rows, 128), F32),
            pltpu.VMEM((ng, 3 * lrows, 128), I32),
            pltpu.VMEM((6, nd * rows, 128), F32),
            pltpu.VMEM((3, radial, 128), F32),
            pltpu.VMEM((3, radial, 128), F32),
            pltpu.VMEM((3 * lrows, ng, 128), I32),
            dma((nd,)),
            dma((nd,)),
            dma((ng,)),
            dma((ng,)),
        ],
        compiler_params=pltpu.CompilerParams(collective_id=0, has_side_effects=True),
        name="gather_points",
    )(
        offsets.reshape(3, radial, lines),
        control_points,
        rbf_weights,
        peer_offset.reshape(1, slots),
        donor_block,
        receptor_block,
    )
    pfeat, wts, more = pl.pallas_call(
        cull_kernel,
        out_shape=(
            sds((3, npat * 32, 128), F32),
            sds((npat * 32, 128), F32),
            sds((radial * 8, 128), F32),
        ),
        in_specs=[VMEM_SPEC] * 5,
        out_specs=[VMEM_SPEC] * 3,
        scratch_shapes=[
            pltpu.VMEM((6, npat * 8, 128), F32),
            pltpu.VMEM((npat * 8, 128), I32),
            pltpu.VMEM((3, npat * 32, 128), F32),
            pltpu.VMEM((npat * 32, 128), F32),
        ],
        name="cull_points",
    )(fil, tot, box, midp, nfeat)
    first = halves(ng)[0] if halves(ng)[1] == 2 else ng - 1
    moved, metric, fringe = pl.pallas_call(
        functools.partial(finish_kernel, nb, ng),
        out_shape=(
            sds((3, radial, lines), F32),
            sds((radial, lines), F32),
            sds((nvar, radial, lines), F32),
        ),
        in_specs=[SMEM_SPEC] * 2 + [VMEM_SPEC] * 7,
        out_specs=[VMEM_SPEC] * 3,
        scratch_shapes=[
            pltpu.VMEM((radial * 8, 128), F32),
            pltpu.VMEM((2, 3, radial, lines), F32),
            pltpu.VMEM((ng, 3, radial, lines), F32),
            pltpu.VMEM((ng, radial, lines), F32),
            pltpu.VMEM((ng, nvar, radial, lines), F32),
            pltpu.VMEM((3, radial * 8, 128), F32),
            pltpu.VMEM((radial, 32, 128), BF16),
            pltpu.VMEM((3, radial, 8, 128), F32),
            pltpu.VMEM((radial, 8, 128), F32),
            pltpu.VMEM((first * HALF, 256, 256), BF16),
            pltpu.VMEM(((ng - 1 - first) * HALF, 256, 256), BF16),
            pltpu.VMEM((ng * HOLD * 8, 128), F32),
            dma((2,)),
            dma((2,)),
            dma((2 * ng,)),
            dma((ng,)),
            dma((2 * ng,)),
            dma((ng,)),
            dma((2 * ng,)),
            dma((ng,)),
        ],
        compiler_params=pltpu.CompilerParams(
            collective_id=1,
            has_side_effects=True,
            vmem_limit_bytes=60 << 20,
        ),
        name="finish",
    )(don, rec, name, base, nfeat, pfeat, wts, more, flow.reshape(nvar, radial, lines))
    return (
        moved.reshape(1, 3, planes, radial, lines),
        metric.reshape(1, planes, radial, lines),
        fringe.reshape(1, nvar, planes, radial, lines),
    )


def solution(mesh):
    in_specs = (
        P("grid", None, "bulk", None, None),
        P("grid", None, "bulk", None, None),
        P(None, ("bulk", "grid")),
        P(None, ("bulk", "grid")),
        P("grid", "bulk", None),
        P("grid", "bulk"),
        P("grid", "bulk"),
    )
    out_specs = (
        P("grid", None, "bulk", None, None),
        P("grid", "bulk", None, None),
        P("grid", None, "bulk", None, None),
    )
    return jax.shard_map(local, mesh=mesh, in_specs=in_specs, out_specs=out_specs, check_vma=False)
```

```python
import functools
import math

import jax
import jax.numpy as jnp
from jax import lax
from jax.experimental import pallas as pl
from jax.experimental.pallas import tpu as pltpu
from jax.sharding import PartitionSpec as P

MESH = pl.DeviceIdType.MESH
SUPPORT = 1.25
CULL = SUPPORT * SUPPORT * 1.0001
FAR = 1.0e9
JOIN = 2
TILES = 3
MOST = 28
HALF = MOST // 2
HOLD = 32
F32 = jnp.float32
I32 = jnp.int32
BF16 = jnp.bfloat16
VMEM_SPEC = pl.BlockSpec(memory_space=pltpu.VMEM)
SMEM_SPEC = pl.BlockSpec(memory_space=pltpu.SMEM)


def take_lanes(x, idx):
    dims = lax.GatherDimensionNumbers(
        offset_dims=(),
        collapsed_slice_dims=(1,),
        start_index_map=(1,),
        operand_batching_dims=(0,),
        start_indices_batching_dims=(0,),
    )
    return lax.gather(
        x, idx[..., None], dims, slice_sizes=(1, 1), mode=lax.GatherScatterMode.PROMISE_IN_BOUNDS
    )


def iota(shape, axis):
    return lax.broadcasted_iota(I32, shape, axis)


def search(near, upper, marks, want):
    counts = jnp.dot(near, upper, preferred_element_type=F32).astype(I32)
    known = jnp.dot(near, marks, preferred_element_type=F32).astype(I32)
    high = known[:, 128:256] <= want
    pos = jnp.where(high, 64, 0)
    pos += jnp.where(jnp.where(high, known[:, 256:384], known[:, 0:128]) <= want, 32, 0)
    for step in (16, 8, 4, 2, 1):
        pos = jnp.where(take_lanes(counts, pos + (step - 1)) <= want, pos + step, pos)
    return pos, known[:, 384:512]


def halves(n):
    return (n // 2, 2) if n % 2 == 0 else (n, 1)


def split(x):
    high = x.astype(BF16).astype(F32)
    rest = x - high
    middle = rest.astype(BF16).astype(F32)
    return high, middle, rest - middle


def features(coords, extra, own):
    rows = []
    for x in coords:
        h, m, t = split(x)
        rows += [h, h, m, h, t, m] if own else [h, m, h, t, h, m]
    total = coords[0] * coords[0] + coords[1] * coords[1] + coords[2] * coords[2] + extra
    one = jnp.ones_like(total)
    square = list(split(total))
    return rows + (square + [one] * 3 if own else [one] * 3 + square)


def spread(shape, parts):
    depth = iota(shape, 0)
    return (depth < (128 // parts) * (iota(shape, 1) // 128 + 1)).astype(F32).astype(BF16)


def gather_kernel(
    nb,
    ng,
    rows,
    lrows,
    off_ref,
    cp_ref,
    rw_ref,
    po_ref,
    db_ref,
    rb_ref,
    flow_ref,
    base_ref,
    fil_ref,
    tot_ref,
    box_ref,
    midp_ref,
    nfeat_ref,
    don_ref,
    rec_ref,
    name_ref,
    allf_ref,
    pts,
    lst,
    allp,
    alll,
    pnt,
    node,
    mid,
    names,
    sp,
    rp,
    sl,
    rl,
    sf,
    rf,
):
    b = lax.axis_index("bulk")
    g = lax.axis_index("grid")
    high, low = halves(ng)
    along = g // low
    place = g - along * low

    def source(t):
        flip = t // high
        return lax.rem(along + (t - flip * high), high) * low + lax.rem(place + flip, low)

    line = [source(t) for t in range(1, high)]
    pair = [source(high)] if low == 2 else []
    barrier = pltpu.get_barrier_semaphore()

    def across(i):
        if nb & (nb - 1):
            return lax.rem(b + i, nb)
        at = b
        for k in range(nb.bit_length() - 1):
            if i >> k & 1:
                at = at + (1 << k) - (2 << k) * lax.rem(b // (1 << k), 2)
        return at

    def back(i):
        return -i % nb if nb & (nb - 1) else i

    def there(i, j):
        return (across(i), lax.rem(g + j, ng))

    peers = [there(0, j) for j in range(1, ng)] + [there(i, 0) for i in range(1, nb)]
    for peer in peers:
        pl.semaphore_signal(barrier, inc=1, device_id=peer, device_id_type=MESH)

    radial, lines = off_ref.shape[1:]
    slots = po_ref.shape[1]
    for c in range(3):
        for i in range(rows):
            pts[c * rows + i : c * rows + i + 1, :] = cp_ref[c : c + 1, 128 * i : 128 * i + 128]
            pts[(3 + c) * rows + i : (3 + c) * rows + i + 1, :] = rw_ref[c : c + 1, 128 * i : 128 * i + 128]
    for c, (ref, fill) in enumerate(((po_ref, -4 * ng), (db_ref, 0), (rb_ref, 0))):
        for i in range(lrows):
            at = c * lrows + i
            size = min(128, slots - 128 * i)
            if size < 128:
                lst[at : at + 1, :] = jnp.full((1, 128), fill, I32)
            lst[at : at + 1, 0:size] = ref[0:1, 128 * i : 128 * i + size]
    theta = jnp.full((1, 128), 2.0 * math.pi / nb, F32) * b.astype(F32)
    radius = 1.0 + 0.25 * iota((radial, 128), 0).astype(F32)
    height = 0.1 * iota((radial, 128), 1).astype(F32)
    base_ref[0] = (0.5 * g.astype(F32) + radius * jnp.cos(theta)) + off_ref[0]
    base_ref[1] = radius * jnp.sin(theta) + off_ref[1]
    base_ref[2] = height + off_ref[2]
    pl.semaphore_wait(barrier, len(peers))

    sent = {"p": [], "l": []}

    def ring(i, j):
        return back(i) * ng + (-j % ng)

    def send_points(source, slot, peer):
        copy = pltpu.make_async_remote_copy(
            src_ref=source,
            dst_ref=allp.at[slot],
            send_sem=sp.at[len(sent["p"])],
            recv_sem=rp.at[slot],
            device_id=peer,
            device_id_type=MESH,
        )
        copy.start()
        sent["p"].append(copy)

    def points_arrived(slot):
        pltpu.make_async_remote_copy(
            src_ref=pts,
            dst_ref=allp.at[slot],
            send_sem=sp.at[0],
            recv_sem=rp.at[slot],
            device_id=peers[0],
            device_id_type=MESH,
        ).wait_recv()

    def list_copy(slot, n, peer):
        return pltpu.make_async_remote_copy(
            src_ref=lst,
            dst_ref=alll.at[slot],
            send_sem=sl.at[n],
            recv_sem=rl.at[slot],
            device_id=peer,
            device_id_type=MESH,
        )

    flows = []

    def flow_copy(slot, n, t):
        return pltpu.make_async_remote_copy(
            src_ref=flow_ref,
            dst_ref=allf_ref.at[slot],
            send_sem=sf.at[n],
            recv_sem=rf.at[slot],
            device_id=(b, (pair + line)[t]),
            device_id_type=MESH,
        )

    for j in range(1, ng):
        send_points(pts, ring(0, j), there(0, j))
    for i in range(1, nb):
        send_points(pts, ring(i, 0), there(i, 0))
    for j in range(1, ng):
        copy = list_copy(g, j, there(0, j))
        copy.start()
        sent["l"].append(copy)
    allp[0] = pts[...]
    alll[g] = lst[...]

    npat = radial // JOIN
    lane8 = iota((8, 128), 1)
    sub8 = iota((8, 128), 0)
    blocks_of_lanes = lane8 // 16
    within = lane8 - 16 * blocks_of_lanes
    upper = (iota((128, 128), 0) <= iota((128, 128), 1)).astype(F32).astype(BF16)
    marks = spread((128, 512), 4)
    lows, highs = [], []
    for c in range(3):
        for jg in range(radial // 8):
            v = base_ref[c, 8 * jg : 8 * jg + 8, :]
            got = jnp.zeros((8, 128), F32)
            for j in range(8):
                row = jnp.broadcast_to(v[j : j + 1, :], (8, 128))
                got = jnp.where(blocks_of_lanes == j, take_lanes(row, 16 * sub8 + within), got)
            node[c, 8 * jg : 8 * jg + 8, :] = got
        full = node[c]
        lo = jnp.min(full, axis=1, keepdims=True)
        hi = jnp.max(full, axis=1, keepdims=True)
        for q in range(npat):
            mine = slice(q * JOIN, (q + 1) * JOIN)
            least = jnp.min(lo[mine], axis=0, keepdims=True)
            most = jnp.max(hi[mine], axis=0, keepdims=True)
            box_ref[2 * c, q] = jnp.broadcast_to(least, (8, 128))
            box_ref[2 * c + 1, q] = jnp.broadcast_to(most, (8, 128))
            half = (least + most) * 0.4
            mid[c, mine, :] = jnp.broadcast_to(half, (JOIN, 128))
            midp_ref[c, q * 4 : (q + 1) * 4, :] = jnp.broadcast_to(half, (4, 128))
        lows.append(jnp.min(lo, axis=0, keepdims=True))
        highs.append(jnp.max(hi, axis=0, keepdims=True))

    for j in range(1, ng):
        points_arrived(j)
        for i in range(1, nb):
            send_points(allp.at[j], back(i) * ng + j, there(i, 0))
    for t in range(len(pair + line)):
        copy = flow_copy(g, t, t)
        copy.start()
        flows.append(copy)
    mine = features([node[c] * 0.8 - mid[c] for c in range(3)], 0.0, True)
    for f in range(24):
        nfeat_ref[f // 8, pl.ds(f % 8, radial, stride=8), :] = mine[f] * (-2.0 if f < 18 else 1.0)

    chunk = ng * rows
    peak = jnp.zeros((8, 128), I32)
    for part in (range(0, 1), range(1, 2), range(2, nb)):
        for d in range(part.start * ng, part.stop * ng):
            if part.start:
                points_arrived(d)
            for c in range(6):
                pnt[c, d * rows : (d + 1) * rows, :] = allp[d, c * rows : (c + 1) * rows, :]
        size = chunk * len(part)
        if not size:
            continue
        mine = slice(part.start * chunk, part.stop * chunk)
        lane = iota((size, 128), 1)
        dist = jnp.zeros((size, 128), F32)
        for c in range(3):
            p = pnt[c, mine, :]
            e = jnp.maximum(jnp.maximum(lows[c] - p, p - highs[c]), 0.0)
            dist = dist + e * e
        near = (dist < CULL).astype(F32).astype(BF16)
        pos, total = search(near, upper, marks, lane)
        for r in range(size // 8):
            peak = jnp.maximum(peak, total[8 * r : 8 * r + 8])
        for c in range(6):
            v = take_lanes(pnt[c, mine, :], pos)
            v = jnp.where(lane < total, v, FAR if c < 3 else 0.0)
            fil_ref[c, :, mine] = v.T
        if part.start == 0:
            for j in range(1, ng):
                list_copy(lax.rem(g + j, ng), 0, peers[0]).wait_recv()
            for k in range(ng):
                for r in range(3 * lrows):
                    names[r, k : k + 1, :] = alll[k, r : r + 1, :]
            owner = iota((ng, 128), 0)
            place = iota((ng, 128), 1)
            before = jnp.zeros((ng, 128), I32)
            don = jnp.zeros((ng, 128), I32)
            rec = jnp.zeros((ng, 128), I32)
            for r in range(lrows):
                target = owner + 1 + names[r]
                target = jnp.where(target >= ng, target - ng, target)
                chosen = (target == g).astype(F32).astype(BF16)
                want = place - before
                pos, total = search(chosen, upper, marks, want)
                keep = jnp.logical_and(want >= 0, want < total)
                don = jnp.where(keep, take_lanes(names[lrows + r], pos), don)
                rec = jnp.where(keep, take_lanes(names[2 * lrows + r], pos), rec)
                before = before + total
            don_ref[...] = don
            rec_ref[...] = rec
            name_ref[...] = jnp.where(place < before, rec, -1)
    tot_ref[...] = peak
    for s in pair + line:
        flow_copy(s, 0, 0).wait_recv()
    for copy in flows:
        copy.wait_send()
    for kind in sent:
        for copy in sent[kind]:
            copy.wait_send()


def tile(p, nfeat, pfeat, wts):
    none = jnp.zeros((8, 128), F32)
    rhs = []
    for m in range(JOIN):
        row = pl.multiple_of((p * JOIN + m) * 8, 8)
        rhs.append(
            jnp.concatenate([nfeat[t, pl.ds(row, 8), :] for t in range(3)] + [none], axis=0)
        )
    rhs = jnp.concatenate(rhs, axis=1).astype(BF16)
    total = None
    for r in range(4):
        row = pl.multiple_of((p * 4 + r) * 8, 8)
        lhs = jnp.concatenate([pfeat[t, pl.ds(row, 8), :] for t in range(3)] + [none], axis=0)
        sq = lax.dot_general(
            lhs.astype(BF16), rhs, (((0,), (0,)), ((), ())), preferred_element_type=F32
        )
        sq = jnp.maximum(sq, 1e-30)
        near = jnp.maximum(1.0 - sq * lax.rsqrt(sq), 0.0)
        two = near * near
        phi = two * two * (1.25 - near)
        hi = phi.astype(BF16)
        lo = (phi - hi.astype(F32)).astype(BF16)
        vals = wts[pl.ds(row, 8), :]
        vhi = vals.astype(BF16).astype(F32)
        both = jnp.concatenate([vhi, vals - vhi], axis=0).astype(BF16)
        got = jnp.dot(
            jnp.concatenate([both, both], axis=1),
            jnp.concatenate([hi, lo], axis=0),
            preferred_element_type=F32,
        )
        total = got if total is None else total + got
    return total[0:8] + total[8:16]


def evaluate(first, last, nfeat, pfeat, wts, acc):
    @pl.loop(first // TILES, last // TILES)
    def _(i):
        for q in range(TILES):
            p = i * TILES + q
            total = tile(p, nfeat, pfeat, wts)
            for m in range(JOIN):
                row = pl.multiple_of((p * JOIN + m) * 8, 8)
                acc[pl.ds(row, 8), :] += total[:, 128 * m : 128 * m + 128]


def cull_kernel(
    fil, tot_ref, box, midp, nfeat, pfeat_ref, wts_ref, acc_ref, out, basec, pmore, wmore
):
    npat = box.shape[1]
    sub8 = iota((8, 128), 0)
    upper = (iota((128, 128), 0) <= iota((128, 128), 1)).astype(F32).astype(BF16)
    groups = (jnp.max(tot_ref[...]) + 7) // 8
    wide = npat * 8
    low_sub = sub8 < 4
    lane_w = iota((wide, 128), 1)
    row_w = iota((wide, 128), 0)
    slot = jnp.where(row_w - 8 * (row_w // 8) < 4, lane_w, 127 - lane_w)
    marks = spread((128, 512), 4)

    def close(gi):
        start = pl.multiple_of(gi * 8, 8)
        src = [fil[c, pl.ds(start, 8), :][None] for c in range(6)]
        dist = jnp.zeros((npat, 8, 128), F32)
        for c in range(3):
            e = jnp.maximum(jnp.maximum(box[2 * c] - src[c], src[c] - box[2 * c + 1]), 0.0)
            dist = dist + e * e
        return src, (dist < CULL).astype(F32).reshape(wide, 128).astype(BF16)

    basec[...] = jnp.zeros(basec.shape, I32)

    @pl.loop(0, groups)
    def _(gi):
        _, near = close(gi)
        basec[...] += jnp.dot(near, marks[:, 384:512], preferred_element_type=F32).astype(I32)

    length = basec[...].reshape(npat, 8, 128)
    pair = length + jnp.concatenate([length[:, 4:8], length[:, 0:4]], axis=1)
    whole = jnp.max(pair) <= 128
    width = jnp.where(whole, 128, 64)
    pages = (jnp.max(length) + width - 1) // width

    def compact(page, pfeat, wts):
        basec[...] = jnp.zeros(basec.shape, I32)
        out[...] = jnp.zeros(out.shape, F32)
        target = slot + width * page

        @pl.loop(0, groups)
        def _(gi):
            src, near = close(gi)
            before = basec[...]
            want = target - before
            pos, amount = search(near, upper, marks, want)
            keep = jnp.logical_and(jnp.logical_and(want >= 0, want < amount), slot < width)
            for c in range(6):
                v = jnp.broadcast_to(src[c], (npat, 8, 128)).reshape(wide, 128)
                out[c] = jnp.where(keep, take_lanes(v, pos), out[c])
            basec[...] = before + amount

        cols = []
        for c in range(6):
            parts = []
            for p in range(0, npat, 2):
                one = out[c, p * 8 : p * 8 + 8, :]
                two = out[c, p * 8 + 8 : p * 8 + 16, :]
                one = one + pltpu.roll(one, 4, 0)
                two = two + pltpu.roll(two, 4, 0)
                parts.append(jnp.where(low_sub, one, two))
            cols.append(jnp.concatenate(parts, axis=0))
        theirs = features([cols[c] * 0.8 - midp[c] for c in range(3)], 0.0, False)
        for f in range(24):
            pfeat[f // 8, pl.ds(f % 8, npat * 4, stride=8), :] = theirs[f]
        for c in range(8):
            wts[pl.ds(c, npat * 4, stride=8), :] = 4.0 * cols[3 + c] if c < 3 else jnp.zeros_like(cols[0])

    compact(0, pfeat_ref, wts_ref)
    acc_ref[...] = jnp.zeros(acc_ref.shape, F32)

    @pl.loop(1, pages)
    def _(page):
        compact(page, pmore, wmore)
        evaluate(0, npat, nfeat, pmore, wmore, acc_ref)


def finish_kernel(
    nb,
    ng,
    don_ref,
    rec_ref,
    name_ref,
    base_ref,
    nfeat_ref,
    pfeat_ref,
    wts_ref,
    more_ref,
    allf,
    mov_ref,
    met_ref,
    out_ref,
    acc,
    halo,
    allm,
    allt,
    allg,
    rows,
    own,
    far,
    val,
    wone,
    wtwo,
    res,
    sh,
    rh,
    sm,
    rm,
    st,
    rt,
    sf,
    rf,
):
    b = lax.axis_index("bulk")
    g = lax.axis_index("grid")
    after = lax.rem(b + 1, nb)
    before = lax.rem(b + nb - 1, nb)
    high, low = halves(ng)
    along = g // low
    place = g - along * low

    def source(t):
        flip = t // high
        return lax.rem(along + (t - flip * high), high) * low + lax.rem(place + flip, low)

    near = [source(t) for t in range(1, high)]
    pair = [source(high)] if low == 2 else []
    barrier = pltpu.get_barrier_semaphore()
    peers = [(before, g), (after, g)] + [(b, source(t)) for t in range(1, ng)]
    for peer in peers:
        pl.semaphore_signal(barrier, inc=1, device_id=peer, device_id_type=MESH)

    radial, lines = mov_ref.shape[1:]
    nvar = out_ref.shape[0]
    acc[...] = more_ref[...]
    npat = radial // JOIN
    middle = npat // (2 * TILES) * TILES
    evaluate(0, middle, nfeat_ref, pfeat_ref, wts_ref, acc)
    pl.semaphore_wait(barrier, len(peers))
    passed = []

    def flow_copy(t):
        return pltpu.make_async_remote_copy(
            src_ref=allf.at[source(t)],
            dst_ref=allg.at[t - 1],
            send_sem=sf.at[t - 1],
            recv_sem=rf.at[t - 1],
            device_id=(b, source(high)),
            device_id_type=MESH,
        )

    if pair:
        for t in range(1, high):
            copy = flow_copy(t)
            copy.start()
            passed.append(copy)
    evaluate(middle, npat, nfeat_ref, pfeat_ref, wts_ref, acc)
    lane8 = iota((8, 128), 1)
    sub8 = iota((8, 128), 0)
    blocks_of_lanes = lane8 // 16
    within = lane8 - 16 * blocks_of_lanes
    for c in range(3):
        for jg in range(radial // 8):
            s = acc[pl.ds(64 * jg + c, 8, stride=8), :]
            got = jnp.zeros((8, 128), F32)
            for kg in range(8):
                row = jnp.broadcast_to(s[kg : kg + 1, :], (8, 128))
                got = jnp.where(blocks_of_lanes == kg, take_lanes(row, 16 * sub8 + within), got)
            mov_ref[c, 8 * jg : 8 * jg + 8, :] = base_ref[c, 8 * jg : 8 * jg + 8, :] + got
    halos = [
        pltpu.make_async_remote_copy(
            src_ref=mov_ref,
            dst_ref=halo.at[i],
            send_sem=sh.at[i],
            recv_sem=rh.at[i],
            device_id=(t, g),
            device_id_type=MESH,
        )
        for i, t in enumerate((after, before))
    ]
    for copy in halos:
        copy.start()
    sent = {"m": [], "t": []}

    def describe(kind, slot, peer, mine, n):
        src, full, ss, rs = {
            "m": (mov_ref, allm, sm, rm),
            "t": (met_ref, allt, st, rt),
        }[kind]
        return pltpu.make_async_remote_copy(
            src_ref=src if mine else full.at[slot],
            dst_ref=full.at[slot],
            send_sem=ss.at[n],
            recv_sem=rs.at[slot],
            device_id=(b, peer),
            device_id_type=MESH,
        )

    def send(kind, slot, peer, mine):
        copy = describe(kind, slot, peer, mine, len(sent[kind]))
        copy.start()
        sent[kind].append(copy)

    def arrived(kind, slot):
        describe(kind, slot, source(1), False, 0).wait_recv()

    for t in pair + near:
        send("m", g, t, True)
    row = iota((radial, lines), 0)
    col = iota((radial, lines), 1)
    dj, dk, centre = [], [], []
    for c in range(3):
        m = mov_ref[c]
        up, down = pltpu.roll(m, radial - 1, 0), pltpu.roll(m, 1, 0)
        dj.append(
            jnp.where(row == 0, up - m, jnp.where(row == radial - 1, m - down, (up - down) * 0.5))
        )
        up, down = pltpu.roll(m, lines - 1, 1), pltpu.roll(m, 1, 1)
        dk.append(
            jnp.where(col == 0, up - m, jnp.where(col == lines - 1, m - down, (up - down) * 0.5))
        )
        total = jnp.sum(jnp.sum(m, axis=0, keepdims=True), axis=1, keepdims=True)
        centre.append(total * (1.0 / (radial * lines)))
    cross = [
        dj[1] * dk[2] - dj[2] * dk[1],
        dj[2] * dk[0] - dj[0] * dk[2],
        dj[0] * dk[1] - dj[1] * dk[0],
    ]
    zero = jnp.zeros((8, 128), F32)
    mine = features([mov_ref[c] - centre[c] for c in range(3)], 0.0, True)
    for f in range(24):
        rows[f // 8, pl.ds(f % 8, radial, stride=8), :] = mine[f] * (-2.0 if f < 18 else 1.0)
    for r in range(radial):
        parts = [rows[p, r * 8 : (r + 1) * 8, :] for p in range(3)]
        own[r] = jnp.concatenate(parts + [zero], axis=0).astype(BF16)
    res[...] = jnp.zeros(res.shape, F32)

    for copy in halos:
        copy.wait_recv()
    di = [(halo[1, c] - halo[0, c]) * 0.5 for c in range(3)]
    met_ref[...] = di[0] * cross[0] + di[1] * cross[1] + di[2] * cross[2]
    for t in range(ng - 1, 0, -1):
        send("t", g, source(t), True)
    for s in near:
        arrived("m", s)
        for t in pair:
            send("m", s, t, False)

    none = jnp.zeros((32, 128), BF16)

    def prepare(t, far):
        s = source(t)
        theirs = features([allm[s, c] - centre[c] for c in range(3)], 0.25, False)
        for f in range(24):
            rows[f // 8, pl.ds(f % 8, radial, stride=8), :] = theirs[f]
        for r in range(radial):
            for p in range(3):
                far[p, r] = rows[p, r * 8 : (r + 1) * 8, :]

    def weigh(t, e, far, wgt, slot):
        s = source(t)
        left, right = [], []
        for q in range(2):
            left += [far[p, don_ref[s, e + q]] for p in range(3)] + [zero]
            right.append(own[rec_ref[s, e + q]])
        right = [
            jnp.concatenate([right[0], none], axis=1),
            jnp.concatenate([none, right[1]], axis=1),
        ]
        den = lax.dot_general(
            jnp.concatenate(left, axis=0).astype(BF16),
            jnp.concatenate(right, axis=0),
            (((0,), (0,)), ((), ())),
            preferred_element_type=F32,
        )
        w = pl.reciprocal(den, approx=False)
        hi = w.astype(BF16)
        wgt[slot * HALF + e // 2, 0:128, :] = hi
        wgt[slot * HALF + e // 2, 128:256, :] = (w - hi.astype(F32)).astype(BF16)

    def load(t, flows, slot):
        met = allt[source(t)]
        for v in range(8):
            row = met * flows[slot, v] if v < nvar else jnp.full((radial, 128), 1.0 if v == nvar else 0.0, F32)
            rows[0, pl.ds(v, radial, stride=8), :] = row
        for r in range(radial):
            val[r] = rows[0, r * 8 : (r + 1) * 8, :]

    def blend(t, e, wgt, slot):
        s = source(t)
        left = []
        for q in range(2):
            vals = val[don_ref[s, e + q]]
            vhi = vals.astype(BF16).astype(F32)
            both = jnp.concatenate([vhi, vals - vhi], axis=0).astype(BF16)
            left.append(jnp.concatenate([both, both], axis=1))
        got = jnp.dot(
            jnp.concatenate(left, axis=0),
            wgt[slot * HALF + e // 2],
            preferred_element_type=F32,
        )
        for q in range(2):
            one = got[16 * q : 16 * q + 8, 128 * q : 128 * q + 128]
            one = one + got[16 * q + 8 : 16 * q + 16, 128 * q : 128 * q + 128]
            one = one / one[nvar : nvar + 1, :]
            at = pl.multiple_of((t * HOLD + e + q) * 8, 8)
            res[pl.ds(at, 8), :] = one

    for s in pair:
        arrived("m", s)
    first = high if pair else high - 1
    rest = ng - 1 - first

    @pl.loop(1, first + 1)
    def _(t):
        prepare(t, far)
        for e in range(0, MOST, 2):
            weigh(t, e, far, wone, t - 1)

    @pl.loop(1, rest + 1)
    def _(t):
        arrived("m", source(first + t))
        arrived("t", source(t))
        prepare(first + t, far)
        load(t, allf, source(t))
        for e in range(0, MOST, 2):
            weigh(first + t, e, far, wtwo, t - 1)
            blend(t, e, wone, t - 1)

    @pl.loop(rest + 1, first + 1)
    def _(t):
        arrived("t", source(t))
        load(t, allf, source(t))
        for e in range(0, MOST, 2):
            blend(t, e, wone, t - 1)

    for t in range(1, len(passed) + 1):
        flow_copy(t).wait_recv()

    @pl.loop(first + 1, ng)
    def _(t):
        arrived("t", source(t))
        load(t, allg, t - first - 1)
        for e in range(0, MOST, 2):
            blend(t, e, wtwo, t - first - 1)

    total = None
    blocks = iota((radial, 128), 0)
    for t in range(1, ng):
        name = jnp.broadcast_to(name_ref[pl.ds(source(t), 1), :], (radial, 128))
        pick = (name == blocks).astype(F32).astype(BF16)[:, 0:HOLD]
        cols = [res[pl.ds(t * HOLD * 8 + v, HOLD, stride=8), :] for v in range(nvar)]
        for part in split(jnp.concatenate(cols, axis=1))[:2]:
            got = jnp.dot(pick, part.astype(BF16), preferred_element_type=F32)
            total = got if total is None else total + got
    for v in range(nvar):
        out_ref[v] = total[:, 128 * v : 128 * v + 128]
    for copy in halos + passed + sent["m"] + sent["t"]:
        copy.wait_send()


def local(offsets, flow, control_points, rbf_weights, peer_offset, donor_block, receptor_block):
    _, _, planes, radial, lines = offsets.shape
    nvar = flow.shape[1]
    nb = lax.axis_size("bulk")
    ng = lax.axis_size("grid")
    nd = nb * ng
    nd = nb * ng
    rows = control_points.shape[1] // 128
    slots = donor_block.shape[1]
    lrows = -(-slots // 128)
    npat = radial // JOIN
    dma = pltpu.SemaphoreType.DMA
    sds = jax.ShapeDtypeStruct
    base, fil, tot, box, midp, nfeat, don, rec, name, allf = pl.pallas_call(
        functools.partial(gather_kernel, nb, ng, rows, lrows),
        out_shape=(
            sds((3, radial, lines), F32),
            sds((6, 128, 128), F32),
            sds((8, 128), I32),
            sds((6, npat, 8, 128), F32),
            sds((3, npat * 4, 128), F32),
            sds((3, radial * 8, 128), F32),
            sds((ng, 128), I32),
            sds((ng, 128), I32),
            sds((ng, 128), I32),
            sds((ng, nvar, radial, lines), F32),
        ),
        in_specs=[VMEM_SPEC] * 7,
        out_specs=[VMEM_SPEC] * 10,
        scratch_shapes=[
            pltpu.VMEM((6 * rows, 128), F32),
            pltpu.VMEM((3 * lrows, 128), I32),
            pltpu.VMEM((nd, 6 * rows, 128), F32),
            pltpu.VMEM((ng, 3 * lrows, 128), I32),
            pltpu.VMEM((6, nd * rows, 128), F32),
            pltpu.VMEM((3, radial, 128), F32),
            pltpu.VMEM((3, radial, 128), F32),
            pltpu.VMEM((3 * lrows, ng, 128), I32),
            dma((nd,)),
            dma((nd,)),
            dma((ng,)),
            dma((ng,)),
            dma((2 * ng,)),
            dma((ng,)),
        ],
        compiler_params=pltpu.CompilerParams(collective_id=0, has_side_effects=True),
        name="gather_points",
    )(
        offsets.reshape(3, radial, lines),
        control_points,
        rbf_weights,
        peer_offset.reshape(1, slots),
        donor_block,
        receptor_block,
        flow.reshape(nvar, radial, lines),
    )
    pfeat, wts, more = pl.pallas_call(
        cull_kernel,
        out_shape=(
            sds((3, npat * 32, 128), F32),
            sds((npat * 32, 128), F32),
            sds((radial * 8, 128), F32),
        ),
        in_specs=[VMEM_SPEC] * 5,
        out_specs=[VMEM_SPEC] * 3,
        scratch_shapes=[
            pltpu.VMEM((6, npat * 8, 128), F32),
            pltpu.VMEM((npat * 8, 128), I32),
            pltpu.VMEM((3, npat * 32, 128), F32),
            pltpu.VMEM((npat * 32, 128), F32),
        ],
        name="cull_points",
    )(fil, tot, box, midp, nfeat)
    first = halves(ng)[0] if halves(ng)[1] == 2 else ng - 1
    moved, metric, fringe = pl.pallas_call(
        functools.partial(finish_kernel, nb, ng),
        out_shape=(
            sds((3, radial, lines), F32),
            sds((radial, lines), F32),
            sds((nvar, radial, lines), F32),
        ),
        in_specs=[SMEM_SPEC] * 2 + [VMEM_SPEC] * 7,
        out_specs=[VMEM_SPEC] * 3,
        scratch_shapes=[
            pltpu.VMEM((radial * 8, 128), F32),
            pltpu.VMEM((2, 3, radial, lines), F32),
            pltpu.VMEM((ng, 3, radial, lines), F32),
            pltpu.VMEM((ng, radial, lines), F32),
            pltpu.VMEM((halves(ng)[0], nvar, radial, lines), F32),
            pltpu.VMEM((3, radial * 8, 128), F32),
            pltpu.VMEM((radial, 32, 128), BF16),
            pltpu.VMEM((3, radial, 8, 128), F32),
            pltpu.VMEM((radial, 8, 128), F32),
            pltpu.VMEM((first * HALF, 256, 256), BF16),
            pltpu.VMEM(((ng - 1 - first) * HALF, 256, 256), BF16),
            pltpu.VMEM((ng * HOLD * 8, 128), F32),
            dma((2,)),
            dma((2,)),
            dma((2 * ng,)),
            dma((ng,)),
            dma((2 * ng,)),
            dma((ng,)),
            dma((ng,)),
            dma((ng,)),
        ],
        compiler_params=pltpu.CompilerParams(
            collective_id=1,
            has_side_effects=True,
            vmem_limit_bytes=60 << 20,
        ),
        name="finish",
    )(don, rec, name, base, nfeat, pfeat, wts, more, allf)
    return (
        moved.reshape(1, 3, planes, radial, lines),
        metric.reshape(1, planes, radial, lines),
        fringe.reshape(1, nvar, planes, radial, lines),
    )


def solution(mesh):
    in_specs = (
        P("grid", None, "bulk", None, None),
        P("grid", None, "bulk", None, None),
        P(None, ("bulk", "grid")),
        P(None, ("bulk", "grid")),
        P("grid", "bulk", None),
        P("grid", "bulk"),
        P("grid", "bulk"),
    )
    out_specs = (
        P("grid", None, "bulk", None, None),
        P("grid", "bulk", None, None),
        P("grid", None, "bulk", None, None),
    )
    return jax.shard_map(local, mesh=mesh, in_specs=in_specs, out_specs=out_specs, check_vma=False)
```

```python
import functools
import math

import jax
import jax.numpy as jnp
from jax import lax
from jax.experimental import pallas as pl
from jax.experimental.pallas import tpu as pltpu
from jax.sharding import PartitionSpec as P

MESH = pl.DeviceIdType.MESH
SUPPORT = 1.25
CULL = SUPPORT * SUPPORT * 1.0001
FAR = 1.0e9
JOIN = 2
TILES = 6
MOST = 28
HALF = MOST // 2
HOLD = 32
F32 = jnp.float32
I32 = jnp.int32
BF16 = jnp.bfloat16
VMEM_SPEC = pl.BlockSpec(memory_space=pltpu.VMEM)
SMEM_SPEC = pl.BlockSpec(memory_space=pltpu.SMEM)


def take_lanes(x, idx):
    dims = lax.GatherDimensionNumbers(
        offset_dims=(),
        collapsed_slice_dims=(1,),
        start_index_map=(1,),
        operand_batching_dims=(0,),
        start_indices_batching_dims=(0,),
    )
    return lax.gather(
        x, idx[..., None], dims, slice_sizes=(1, 1), mode=lax.GatherScatterMode.PROMISE_IN_BOUNDS
    )


def iota(shape, axis):
    return lax.broadcasted_iota(I32, shape, axis)


def search(near, upper, marks, want):
    counts = jnp.dot(near, upper, preferred_element_type=F32).astype(I32)
    known = jnp.dot(near, marks, preferred_element_type=F32).astype(I32)
    high = known[:, 128:256] <= want
    pos = jnp.where(high, 64, 0)
    pos += jnp.where(jnp.where(high, known[:, 256:384], known[:, 0:128]) <= want, 32, 0)
    for step in (16, 8, 4, 2, 1):
        pos = jnp.where(take_lanes(counts, pos + (step - 1)) <= want, pos + step, pos)
    return pos, known[:, 384:512]


def halves(n):
    return (n // 2, 2) if n % 2 == 0 else (n, 1)


def split(x):
    high = x.astype(BF16).astype(F32)
    rest = x - high
    middle = rest.astype(BF16).astype(F32)
    return high, middle, rest - middle


def features(coords, extra, own):
    rows = []
    for x in coords:
        h, m, t = split(x)
        rows += [h, h, m, h, t, m] if own else [h, m, h, t, h, m]
    total = coords[0] * coords[0] + coords[1] * coords[1] + coords[2] * coords[2] + extra
    one = jnp.ones_like(total)
    square = list(split(total))
    return rows + (square + [one] * 3 if own else [one] * 3 + square)


def spread(shape, parts):
    depth = iota(shape, 0)
    return (depth < (128 // parts) * (iota(shape, 1) // 128 + 1)).astype(F32).astype(BF16)


def gather_kernel(
    nb,
    ng,
    rows,
    lrows,
    off_ref,
    cp_ref,
    rw_ref,
    po_ref,
    db_ref,
    rb_ref,
    flow_ref,
    base_ref,
    fil_ref,
    tot_ref,
    box_ref,
    midp_ref,
    nfeat_ref,
    don_ref,
    rec_ref,
    name_ref,
    allf_ref,
    pts,
    lst,
    allp,
    alll,
    pnt,
    node,
    mid,
    names,
    sp,
    rp,
    sl,
    rl,
    sf,
    rf,
):
    b = lax.axis_index("bulk")
    g = lax.axis_index("grid")
    high, low = halves(ng)
    along = g // low
    place = g - along * low

    def source(t):
        flip = t // high
        return lax.rem(along + (t - flip * high), high) * low + lax.rem(place + flip, low)

    line = [source(t) for t in range(1, high)]
    pair = [source(high)] if low == 2 else []
    barrier = pltpu.get_barrier_semaphore()

    def across(at, size, i):
        if size & (size - 1):
            return lax.rem(at + i, size)
        to = at
        for k in range(size.bit_length() - 1):
            if i >> k & 1:
                to = to + (1 << k) - (2 << k) * lax.rem(at // (1 << k), 2)
        return to

    def back(size, i):
        return -i % size if size & (size - 1) else i

    def there(i, j):
        return (across(b, nb, i), across(g, ng, j))

    peers = [there(0, j) for j in range(1, ng)] + [there(i, 0) for i in range(1, nb)]
    for peer in peers:
        pl.semaphore_signal(barrier, inc=1, device_id=peer, device_id_type=MESH)

    radial, lines = off_ref.shape[1:]
    slots = po_ref.shape[1]
    for c in range(3):
        for i in range(rows):
            pts[c * rows + i : c * rows + i + 1, :] = cp_ref[c : c + 1, 128 * i : 128 * i + 128]
            pts[(3 + c) * rows + i : (3 + c) * rows + i + 1, :] = rw_ref[c : c + 1, 128 * i : 128 * i + 128]
    for c, (ref, fill) in enumerate(((po_ref, -4 * ng), (db_ref, 0), (rb_ref, 0))):
        for i in range(lrows):
            at = c * lrows + i
            size = min(128, slots - 128 * i)
            if size < 128:
                lst[at : at + 1, :] = jnp.full((1, 128), fill, I32)
            lst[at : at + 1, 0:size] = ref[0:1, 128 * i : 128 * i + size]
    theta = jnp.full((1, 128), 2.0 * math.pi / nb, F32) * b.astype(F32)
    radius = 1.0 + 0.25 * iota((radial, 128), 0).astype(F32)
    height = 0.1 * iota((radial, 128), 1).astype(F32)
    base_ref[0] = (0.5 * g.astype(F32) + radius * jnp.cos(theta)) + off_ref[0]
    base_ref[1] = radius * jnp.sin(theta) + off_ref[1]
    base_ref[2] = height + off_ref[2]
    pl.semaphore_wait(barrier, len(peers))

    sent = {"p": [], "l": []}

    def ring(i, j):
        return back(nb, i) * ng + back(ng, j)

    def send_points(source, slot, peer):
        copy = pltpu.make_async_remote_copy(
            src_ref=source,
            dst_ref=allp.at[slot],
            send_sem=sp.at[len(sent["p"])],
            recv_sem=rp.at[slot],
            device_id=peer,
            device_id_type=MESH,
        )
        copy.start()
        sent["p"].append(copy)

    def points_arrived(slot):
        pltpu.make_async_remote_copy(
            src_ref=pts,
            dst_ref=allp.at[slot],
            send_sem=sp.at[0],
            recv_sem=rp.at[slot],
            device_id=peers[0],
            device_id_type=MESH,
        ).wait_recv()

    def list_copy(slot, n, peer):
        return pltpu.make_async_remote_copy(
            src_ref=lst,
            dst_ref=alll.at[slot],
            send_sem=sl.at[n],
            recv_sem=rl.at[slot],
            device_id=peer,
            device_id_type=MESH,
        )

    flows = []

    def flow_copy(slot, n, t):
        return pltpu.make_async_remote_copy(
            src_ref=flow_ref,
            dst_ref=allf_ref.at[slot],
            send_sem=sf.at[n],
            recv_sem=rf.at[slot],
            device_id=(b, (pair + line)[t]),
            device_id_type=MESH,
        )

    for j in range(1, ng):
        send_points(pts, ring(0, j), there(0, j))
    for i in range(1, nb):
        send_points(pts, ring(i, 0), there(i, 0))
    for j in range(1, ng):
        copy = list_copy(g, j, there(0, j))
        copy.start()
        sent["l"].append(copy)
    allp[0] = pts[...]
    alll[g] = lst[...]

    npat = radial // JOIN
    lane8 = iota((8, 128), 1)
    sub8 = iota((8, 128), 0)
    blocks_of_lanes = lane8 // 16
    within = lane8 - 16 * blocks_of_lanes
    upper = (iota((128, 128), 0) <= iota((128, 128), 1)).astype(F32).astype(BF16)
    marks = spread((128, 512), 4)
    lows, highs = [], []
    for c in range(3):
        for jg in range(radial // 8):
            v = base_ref[c, 8 * jg : 8 * jg + 8, :]
            got = jnp.zeros((8, 128), F32)
            for j in range(8):
                row = jnp.broadcast_to(v[j : j + 1, :], (8, 128))
                got = jnp.where(blocks_of_lanes == j, take_lanes(row, 16 * sub8 + within), got)
            node[c, 8 * jg : 8 * jg + 8, :] = got
        full = node[c]
        lo = jnp.min(full, axis=1, keepdims=True)
        hi = jnp.max(full, axis=1, keepdims=True)
        for q in range(npat):
            mine = slice(q * JOIN, (q + 1) * JOIN)
            least = jnp.min(lo[mine], axis=0, keepdims=True)
            most = jnp.max(hi[mine], axis=0, keepdims=True)
            box_ref[2 * c, q] = jnp.broadcast_to(least, (8, 128))
            box_ref[2 * c + 1, q] = jnp.broadcast_to(most, (8, 128))
            half = (least + most) * 0.4
            mid[c, mine, :] = jnp.broadcast_to(half, (JOIN, 128))
            midp_ref[c, q * 4 : (q + 1) * 4, :] = jnp.broadcast_to(half, (4, 128))
        lows.append(jnp.min(lo, axis=0, keepdims=True))
        highs.append(jnp.max(hi, axis=0, keepdims=True))

    for j in range(1, ng):
        points_arrived(j)
        for i in range(1, nb):
            send_points(allp.at[j], back(nb, i) * ng + j, there(i, 0))
    for t in range(len(pair + line)):
        copy = flow_copy(g, t, t)
        copy.start()
        flows.append(copy)
    mine = features([node[c] * 0.8 - mid[c] for c in range(3)], 0.0, True)
    for f in range(24):
        nfeat_ref[f // 8, pl.ds(f % 8, radial, stride=8), :] = mine[f] * (-2.0 if f < 18 else 1.0)

    chunk = ng * rows
    peak = jnp.zeros((8, 128), I32)
    for part in (range(0, 1), range(1, 2), range(2, nb)):
        for d in range(part.start * ng, part.stop * ng):
            if part.start:
                points_arrived(d)
            for c in range(6):
                pnt[c, d * rows : (d + 1) * rows, :] = allp[d, c * rows : (c + 1) * rows, :]
        size = chunk * len(part)
        if not size:
            continue
        mine = slice(part.start * chunk, part.stop * chunk)
        lane = iota((size, 128), 1)
        dist = jnp.zeros((size, 128), F32)
        for c in range(3):
            p = pnt[c, mine, :]
            e = jnp.maximum(jnp.maximum(lows[c] - p, p - highs[c]), 0.0)
            dist = dist + e * e
        near = (dist < CULL).astype(F32).astype(BF16)
        pos, total = search(near, upper, marks, lane)
        for r in range(size // 8):
            peak = jnp.maximum(peak, total[8 * r : 8 * r + 8])
        for c in range(6):
            v = take_lanes(pnt[c, mine, :], pos)
            v = jnp.where(lane < total, v, FAR if c < 3 else 0.0)
            fil_ref[c, :, mine] = v.T
        if part.start == 0:
            for j in range(1, ng):
                list_copy(lax.rem(g + j, ng), 0, peers[0]).wait_recv()
            for k in range(ng):
                for r in range(3 * lrows):
                    names[r, k : k + 1, :] = alll[k, r : r + 1, :]
            owner = iota((ng, 128), 0)
            place = iota((ng, 128), 1)
            before = jnp.zeros((ng, 128), I32)
            don = jnp.zeros((ng, 128), I32)
            rec = jnp.zeros((ng, 128), I32)
            for r in range(lrows):
                target = owner + 1 + names[r]
                target = jnp.where(target >= ng, target - ng, target)
                chosen = (target == g).astype(F32).astype(BF16)
                want = place - before
                pos, total = search(chosen, upper, marks, want)
                keep = jnp.logical_and(want >= 0, want < total)
                don = jnp.where(keep, take_lanes(names[lrows + r], pos), don)
                rec = jnp.where(keep, take_lanes(names[2 * lrows + r], pos), rec)
                before = before + total
            don_ref[...] = don
            rec_ref[...] = rec
            name_ref[...] = jnp.where(place < before, rec, -1)
    tot_ref[...] = peak
    for s in pair + line:
        flow_copy(s, 0, 0).wait_recv()
    for copy in flows:
        copy.wait_send()
    for kind in sent:
        for copy in sent[kind]:
            copy.wait_send()


def tile(p, nfeat, pfeat, wts):
    none = jnp.zeros((8, 128), F32)
    rhs = []
    for m in range(JOIN):
        row = pl.multiple_of((p * JOIN + m) * 8, 8)
        rhs.append(
            jnp.concatenate([nfeat[t, pl.ds(row, 8), :] for t in range(3)] + [none], axis=0)
        )
    rhs = jnp.concatenate(rhs, axis=1).astype(BF16)
    total = None
    for r in range(4):
        row = pl.multiple_of((p * 4 + r) * 8, 8)
        lhs = jnp.concatenate([pfeat[t, pl.ds(row, 8), :] for t in range(3)] + [none], axis=0)
        sq = lax.dot_general(
            lhs.astype(BF16), rhs, (((0,), (0,)), ((), ())), preferred_element_type=F32
        )
        sq = jnp.maximum(sq, 1e-30)
        near = jnp.maximum(1.0 - sq * lax.rsqrt(sq), 0.0)
        two = near * near
        phi = two * two * (1.25 - near)
        hi = phi.astype(BF16)
        lo = (phi - hi.astype(F32)).astype(BF16)
        vals = wts[pl.ds(row, 8), :]
        vhi = vals.astype(BF16).astype(F32)
        both = jnp.concatenate([vhi, vals - vhi], axis=0).astype(BF16)
        got = jnp.dot(
            jnp.concatenate([both, both], axis=1),
            jnp.concatenate([hi, lo], axis=0),
            preferred_element_type=F32,
        )
        total = got if total is None else total + got
    return total[0:8] + total[8:16]


def evaluate(first, last, nfeat, pfeat, wts, acc):
    @pl.loop(first // TILES, last // TILES)
    def _(i):
        for q in range(TILES):
            p = i * TILES + q
            total = tile(p, nfeat, pfeat, wts)
            for m in range(JOIN):
                row = pl.multiple_of((p * JOIN + m) * 8, 8)
                acc[pl.ds(row, 8), :] += total[:, 128 * m : 128 * m + 128]


def cull_kernel(
    fil, tot_ref, box, midp, nfeat, pfeat_ref, wts_ref, acc_ref, out, basec, pmore, wmore
):
    npat = box.shape[1]
    sub8 = iota((8, 128), 0)
    upper = (iota((128, 128), 0) <= iota((128, 128), 1)).astype(F32).astype(BF16)
    groups = (jnp.max(tot_ref[...]) + 7) // 8
    wide = npat * 8
    low_sub = sub8 < 4
    lane_w = iota((wide, 128), 1)
    row_w = iota((wide, 128), 0)
    slot = jnp.where(row_w - 8 * (row_w // 8) < 4, lane_w, 127 - lane_w)
    marks = spread((128, 512), 4)

    def close(gi):
        start = pl.multiple_of(gi * 8, 8)
        src = [fil[c, pl.ds(start, 8), :][None] for c in range(6)]
        dist = jnp.zeros((npat, 8, 128), F32)
        for c in range(3):
            e = jnp.maximum(jnp.maximum(box[2 * c] - src[c], src[c] - box[2 * c + 1]), 0.0)
            dist = dist + e * e
        return src, (dist < CULL).astype(F32).reshape(wide, 128).astype(BF16)

    basec[...] = jnp.zeros(basec.shape, I32)

    @pl.loop(0, groups)
    def _(gi):
        _, near = close(gi)
        basec[...] += jnp.dot(near, marks[:, 384:512], preferred_element_type=F32).astype(I32)

    length = basec[...].reshape(npat, 8, 128)
    pair = length + jnp.concatenate([length[:, 4:8], length[:, 0:4]], axis=1)
    whole = jnp.max(pair) <= 128
    width = jnp.where(whole, 128, 64)
    pages = (jnp.max(length) + width - 1) // width

    def compact(page, pfeat, wts):
        basec[...] = jnp.zeros(basec.shape, I32)
        out[...] = jnp.zeros(out.shape, F32)
        target = slot + width * page

        @pl.loop(0, groups)
        def _(gi):
            src, near = close(gi)
            before = basec[...]
            want = target - before
            pos, amount = search(near, upper, marks, want)
            keep = jnp.logical_and(jnp.logical_and(want >= 0, want < amount), slot < width)
            for c in range(6):
                v = jnp.broadcast_to(src[c], (npat, 8, 128)).reshape(wide, 128)
                out[c] = jnp.where(keep, take_lanes(v, pos), out[c])
            basec[...] = before + amount

        cols = []
        for c in range(6):
            parts = []
            for p in range(0, npat, 2):
                one = out[c, p * 8 : p * 8 + 8, :]
                two = out[c, p * 8 + 8 : p * 8 + 16, :]
                one = one + pltpu.roll(one, 4, 0)
                two = two + pltpu.roll(two, 4, 0)
                parts.append(jnp.where(low_sub, one, two))
            cols.append(jnp.concatenate(parts, axis=0))
        theirs = features([cols[c] * 0.8 - midp[c] for c in range(3)], 0.0, False)
        for f in range(24):
            pfeat[f // 8, pl.ds(f % 8, npat * 4, stride=8), :] = theirs[f]
        for c in range(8):
            wts[pl.ds(c, npat * 4, stride=8), :] = 4.0 * cols[3 + c] if c < 3 else jnp.zeros_like(cols[0])

    compact(0, pfeat_ref, wts_ref)
    acc_ref[...] = jnp.zeros(acc_ref.shape, F32)

    @pl.loop(1, pages)
    def _(page):
        compact(page, pmore, wmore)
        evaluate(0, npat, nfeat, pmore, wmore, acc_ref)


def finish_kernel(
    nb,
    ng,
    don_ref,
    rec_ref,
    name_ref,
    base_ref,
    nfeat_ref,
    pfeat_ref,
    wts_ref,
    more_ref,
    allf,
    mov_ref,
    met_ref,
    out_ref,
    acc,
    halo,
    allm,
    allt,
    allg,
    rows,
    own,
    far,
    val,
    wone,
    wtwo,
    res,
    sh,
    rh,
    sm,
    rm,
    st,
    rt,
    sf,
    rf,
):
    b = lax.axis_index("bulk")
    g = lax.axis_index("grid")
    after = lax.rem(b + 1, nb)
    before = lax.rem(b + nb - 1, nb)
    high, low = halves(ng)
    along = g // low
    place = g - along * low

    def source(t):
        flip = t // high
        return lax.rem(along + (t - flip * high), high) * low + lax.rem(place + flip, low)

    near = [source(t) for t in range(1, high)]
    pair = [source(high)] if low == 2 else []
    barrier = pltpu.get_barrier_semaphore()
    peers = [(before, g), (after, g)] + [(b, source(t)) for t in range(1, ng)]
    for peer in peers:
        pl.semaphore_signal(barrier, inc=1, device_id=peer, device_id_type=MESH)

    radial, lines = mov_ref.shape[1:]
    nvar = out_ref.shape[0]
    acc[...] = more_ref[...]
    npat = radial // JOIN
    middle = npat // (2 * TILES) * TILES
    evaluate(0, middle, nfeat_ref, pfeat_ref, wts_ref, acc)
    pl.semaphore_wait(barrier, len(peers))
    passed = []

    def flow_copy(t):
        return pltpu.make_async_remote_copy(
            src_ref=allf.at[source(t)],
            dst_ref=allg.at[t - 1],
            send_sem=sf.at[t - 1],
            recv_sem=rf.at[t - 1],
            device_id=(b, source(high)),
            device_id_type=MESH,
        )

    if pair:
        for t in range(1, high):
            copy = flow_copy(t)
            copy.start()
            passed.append(copy)
    evaluate(middle, npat, nfeat_ref, pfeat_ref, wts_ref, acc)
    lane8 = iota((8, 128), 1)
    sub8 = iota((8, 128), 0)
    blocks_of_lanes = lane8 // 16
    within = lane8 - 16 * blocks_of_lanes
    for c in range(3):
        for jg in range(radial // 8):
            s = acc[pl.ds(64 * jg + c, 8, stride=8), :]
            got = jnp.zeros((8, 128), F32)
            for kg in range(8):
                row = jnp.broadcast_to(s[kg : kg + 1, :], (8, 128))
                got = jnp.where(blocks_of_lanes == kg, take_lanes(row, 16 * sub8 + within), got)
            mov_ref[c, 8 * jg : 8 * jg + 8, :] = base_ref[c, 8 * jg : 8 * jg + 8, :] + got
    halos = [
        pltpu.make_async_remote_copy(
            src_ref=mov_ref,
            dst_ref=halo.at[i],
            send_sem=sh.at[i],
            recv_sem=rh.at[i],
            device_id=(t, g),
            device_id_type=MESH,
        )
        for i, t in enumerate((after, before))
    ]
    for copy in halos:
        copy.start()
    sent = {"m": [], "t": []}

    def describe(kind, slot, peer, mine, n):
        src, full, ss, rs = {
            "m": (mov_ref, allm, sm, rm),
            "t": (met_ref, allt, st, rt),
        }[kind]
        return pltpu.make_async_remote_copy(
            src_ref=src if mine else full.at[slot],
            dst_ref=full.at[slot],
            send_sem=ss.at[n],
            recv_sem=rs.at[slot],
            device_id=(b, peer),
            device_id_type=MESH,
        )

    def send(kind, slot, peer, mine):
        copy = describe(kind, slot, peer, mine, len(sent[kind]))
        copy.start()
        sent[kind].append(copy)

    def arrived(kind, slot):
        describe(kind, slot, source(1), False, 0).wait_recv()

    for t in pair + near:
        send("m", g, t, True)
    row = iota((radial, lines), 0)
    col = iota((radial, lines), 1)
    dj, dk, centre = [], [], []
    for c in range(3):
        m = mov_ref[c]
        up, down = pltpu.roll(m, radial - 1, 0), pltpu.roll(m, 1, 0)
        dj.append(
            jnp.where(row == 0, up - m, jnp.where(row == radial - 1, m - down, (up - down) * 0.5))
        )
        up, down = pltpu.roll(m, lines - 1, 1), pltpu.roll(m, 1, 1)
        dk.append(
            jnp.where(col == 0, up - m, jnp.where(col == lines - 1, m - down, (up - down) * 0.5))
        )
        total = jnp.sum(jnp.sum(m, axis=0, keepdims=True), axis=1, keepdims=True)
        centre.append(total * (1.0 / (radial * lines)))
    cross = [
        dj[1] * dk[2] - dj[2] * dk[1],
        dj[2] * dk[0] - dj[0] * dk[2],
        dj[0] * dk[1] - dj[1] * dk[0],
    ]
    zero = jnp.zeros((8, 128), F32)
    mine = features([mov_ref[c] - centre[c] for c in range(3)], 0.0, True)
    for f in range(24):
        rows[f // 8, pl.ds(f % 8, radial, stride=8), :] = mine[f] * (-2.0 if f < 18 else 1.0)
    for r in range(radial):
        parts = [rows[p, r * 8 : (r + 1) * 8, :] for p in range(3)]
        own[r] = jnp.concatenate(parts + [zero], axis=0).astype(BF16)
    res[...] = jnp.zeros(res.shape, F32)

    for copy in halos:
        copy.wait_recv()
    di = [(halo[1, c] - halo[0, c]) * 0.5 for c in range(3)]
    met_ref[...] = di[0] * cross[0] + di[1] * cross[1] + di[2] * cross[2]
    for t in range(ng - 1, 0, -1):
        send("t", g, source(t), True)
    for s in near:
        arrived("m", s)
        for t in pair:
            send("m", s, t, False)

    none = jnp.zeros((32, 128), BF16)

    def prepare(t, far):
        s = source(t)
        theirs = features([allm[s, c] - centre[c] for c in range(3)], 0.25, False)
        for f in range(24):
            rows[f // 8, pl.ds(f % 8, radial, stride=8), :] = theirs[f]
        for r in range(radial):
            for p in range(3):
                far[p, r] = rows[p, r * 8 : (r + 1) * 8, :]

    def weigh(t, e, far, wgt, slot):
        s = source(t)
        left, right = [], []
        for q in range(2):
            left += [far[p, don_ref[s, e + q]] for p in range(3)] + [zero]
            right.append(own[rec_ref[s, e + q]])
        right = [
            jnp.concatenate([right[0], none], axis=1),
            jnp.concatenate([none, right[1]], axis=1),
        ]
        den = lax.dot_general(
            jnp.concatenate(left, axis=0).astype(BF16),
            jnp.concatenate(right, axis=0),
            (((0,), (0,)), ((), ())),
            preferred_element_type=F32,
        )
        w = pl.reciprocal(den, approx=False)
        hi = w.astype(BF16)
        wgt[slot * HALF + e // 2, 0:128, :] = hi
        wgt[slot * HALF + e // 2, 128:256, :] = (w - hi.astype(F32)).astype(BF16)

    def load(t, flows, slot):
        met = allt[source(t)]
        for v in range(8):
            row = met * flows[slot, v] if v < nvar else jnp.full((radial, 128), 1.0 if v == nvar else 0.0, F32)
            rows[0, pl.ds(v, radial, stride=8), :] = row
        for r in range(radial):
            val[r] = rows[0, r * 8 : (r + 1) * 8, :]

    def blend(t, e, wgt, slot):
        s = source(t)
        left = []
        for q in range(2):
            vals = val[don_ref[s, e + q]]
            vhi = vals.astype(BF16).astype(F32)
            both = jnp.concatenate([vhi, vals - vhi], axis=0).astype(BF16)
            left.append(jnp.concatenate([both, both], axis=1))
        got = jnp.dot(
            jnp.concatenate(left, axis=0),
            wgt[slot * HALF + e // 2],
            preferred_element_type=F32,
        )
        for q in range(2):
            one = got[16 * q : 16 * q + 8, 128 * q : 128 * q + 128]
            one = one + got[16 * q + 8 : 16 * q + 16, 128 * q : 128 * q + 128]
            one = one / one[nvar : nvar + 1, :]
            at = pl.multiple_of((t * HOLD + e + q) * 8, 8)
            res[pl.ds(at, 8), :] = one

    for s in pair:
        arrived("m", s)
    first = high if pair else high - 1
    rest = ng - 1 - first

    @pl.loop(1, first + 1)
    def _(t):
        prepare(t, far)
        for e in range(0, MOST, 2):
            weigh(t, e, far, wone, t - 1)

    @pl.loop(1, rest + 1)
    def _(t):
        arrived("m", source(first + t))
        arrived("t", source(t))
        prepare(first + t, far)
        load(t, allf, source(t))
        for e in range(0, MOST, 2):
            weigh(first + t, e, far, wtwo, t - 1)
            blend(t, e, wone, t - 1)

    @pl.loop(rest + 1, first + 1)
    def _(t):
        arrived("t", source(t))
        load(t, allf, source(t))
        for e in range(0, MOST, 2):
            blend(t, e, wone, t - 1)

    for t in range(1, len(passed) + 1):
        flow_copy(t).wait_recv()

    @pl.loop(first + 1, ng)
    def _(t):
        arrived("t", source(t))
        load(t, allg, t - first - 1)
        for e in range(0, MOST, 2):
            blend(t, e, wtwo, t - first - 1)

    total = None
    blocks = iota((radial, 128), 0)
    for t in range(1, ng):
        name = jnp.broadcast_to(name_ref[pl.ds(source(t), 1), :], (radial, 128))
        pick = (name == blocks).astype(F32).astype(BF16)[:, 0:HOLD]
        cols = [res[pl.ds(t * HOLD * 8 + v, HOLD, stride=8), :] for v in range(nvar)]
        for part in split(jnp.concatenate(cols, axis=1))[:2]:
            got = jnp.dot(pick, part.astype(BF16), preferred_element_type=F32)
            total = got if total is None else total + got
    for v in range(nvar):
        out_ref[v] = total[:, 128 * v : 128 * v + 128]
    for copy in halos + passed + sent["m"] + sent["t"]:
        copy.wait_send()


def local(offsets, flow, control_points, rbf_weights, peer_offset, donor_block, receptor_block):
    _, _, planes, radial, lines = offsets.shape
    nvar = flow.shape[1]
    nb = lax.axis_size("bulk")
    ng = lax.axis_size("grid")
    nd = nb * ng
    nd = nb * ng
    rows = control_points.shape[1] // 128
    slots = donor_block.shape[1]
    lrows = -(-slots // 128)
    npat = radial // JOIN
    dma = pltpu.SemaphoreType.DMA
    sds = jax.ShapeDtypeStruct
    base, fil, tot, box, midp, nfeat, don, rec, name, allf = pl.pallas_call(
        functools.partial(gather_kernel, nb, ng, rows, lrows),
        out_shape=(
            sds((3, radial, lines), F32),
            sds((6, 128, 128), F32),
            sds((8, 128), I32),
            sds((6, npat, 8, 128), F32),
            sds((3, npat * 4, 128), F32),
            sds((3, radial * 8, 128), F32),
            sds((ng, 128), I32),
            sds((ng, 128), I32),
            sds((ng, 128), I32),
            sds((ng, nvar, radial, lines), F32),
        ),
        in_specs=[VMEM_SPEC] * 7,
        out_specs=[VMEM_SPEC] * 10,
        scratch_shapes=[
            pltpu.VMEM((6 * rows, 128), F32),
            pltpu.VMEM((3 * lrows, 128), I32),
            pltpu.VMEM((nd, 6 * rows, 128), F32),
            pltpu.VMEM((ng, 3 * lrows, 128), I32),
            pltpu.VMEM((6, nd * rows, 128), F32),
            pltpu.VMEM((3, radial, 128), F32),
            pltpu.VMEM((3, radial, 128), F32),
            pltpu.VMEM((3 * lrows, ng, 128), I32),
            dma((nd,)),
            dma((nd,)),
            dma((ng,)),
            dma((ng,)),
            dma((2 * ng,)),
            dma((ng,)),
        ],
        compiler_params=pltpu.CompilerParams(collective_id=0, has_side_effects=True),
        name="gather_points",
    )(
        offsets.reshape(3, radial, lines),
        control_points,
        rbf_weights,
        peer_offset.reshape(1, slots),
        donor_block,
        receptor_block,
        flow.reshape(nvar, radial, lines),
    )
    pfeat, wts, more = pl.pallas_call(
        cull_kernel,
        out_shape=(
            sds((3, npat * 32, 128), F32),
            sds((npat * 32, 128), F32),
            sds((radial * 8, 128), F32),
        ),
        in_specs=[VMEM_SPEC] * 5,
        out_specs=[VMEM_SPEC] * 3,
        scratch_shapes=[
            pltpu.VMEM((6, npat * 8, 128), F32),
            pltpu.VMEM((npat * 8, 128), I32),
            pltpu.VMEM((3, npat * 32, 128), F32),
            pltpu.VMEM((npat * 32, 128), F32),
        ],
        name="cull_points",
    )(fil, tot, box, midp, nfeat)
    first = halves(ng)[0] if halves(ng)[1] == 2 else ng - 1
    moved, metric, fringe = pl.pallas_call(
        functools.partial(finish_kernel, nb, ng),
        out_shape=(
            sds((3, radial, lines), F32),
            sds((radial, lines), F32),
            sds((nvar, radial, lines), F32),
        ),
        in_specs=[SMEM_SPEC] * 2 + [VMEM_SPEC] * 7,
        out_specs=[VMEM_SPEC] * 3,
        scratch_shapes=[
            pltpu.VMEM((radial * 8, 128), F32),
            pltpu.VMEM((2, 3, radial, lines), F32),
            pltpu.VMEM((ng, 3, radial, lines), F32),
            pltpu.VMEM((ng, radial, lines), F32),
            pltpu.VMEM((halves(ng)[0], nvar, radial, lines), F32),
            pltpu.VMEM((3, radial * 8, 128), F32),
            pltpu.VMEM((radial, 32, 128), BF16),
            pltpu.VMEM((3, radial, 8, 128), F32),
            pltpu.VMEM((radial, 8, 128), F32),
            pltpu.VMEM((first * HALF, 256, 256), BF16),
            pltpu.VMEM(((ng - 1 - first) * HALF, 256, 256), BF16),
            pltpu.VMEM((ng * HOLD * 8, 128), F32),
            dma((2,)),
            dma((2,)),
            dma((2 * ng,)),
            dma((ng,)),
            dma((2 * ng,)),
            dma((ng,)),
            dma((ng,)),
            dma((ng,)),
        ],
        compiler_params=pltpu.CompilerParams(
            collective_id=1,
            has_side_effects=True,
            vmem_limit_bytes=60 << 20,
        ),
        name="finish",
    )(don, rec, name, base, nfeat, pfeat, wts, more, allf)
    return (
        moved.reshape(1, 3, planes, radial, lines),
        metric.reshape(1, planes, radial, lines),
        fringe.reshape(1, nvar, planes, radial, lines),
    )


def solution(mesh):
    in_specs = (
        P("grid", None, "bulk", None, None),
        P("grid", None, "bulk", None, None),
        P(None, ("bulk", "grid")),
        P(None, ("bulk", "grid")),
        P("grid", "bulk", None),
        P("grid", "bulk"),
        P("grid", "bulk"),
    )
    out_specs = (
        P("grid", None, "bulk", None, None),
        P("grid", "bulk", None, None),
        P("grid", None, "bulk", None, None),
    )
    return jax.shard_map(local, mesh=mesh, in_specs=in_specs, out_specs=out_specs, check_vma=False)
```

```python
import functools
import math

import jax
import jax.numpy as jnp
from jax import lax
from jax.experimental import pallas as pl
from jax.experimental.pallas import tpu as pltpu
from jax.sharding import PartitionSpec as P

MESH = pl.DeviceIdType.MESH
SUPPORT = 1.25
CULL = SUPPORT * SUPPORT * 1.0001
FAR = 1.0e9
JOIN = 2
TILES = 6
MOST = 28
HALF = MOST // 2
HOLD = 32
F32 = jnp.float32
I32 = jnp.int32
BF16 = jnp.bfloat16
VMEM_SPEC = pl.BlockSpec(memory_space=pltpu.VMEM)
SMEM_SPEC = pl.BlockSpec(memory_space=pltpu.SMEM)


def take_lanes(x, idx):
    dims = lax.GatherDimensionNumbers(
        offset_dims=(),
        collapsed_slice_dims=(1,),
        start_index_map=(1,),
        operand_batching_dims=(0,),
        start_indices_batching_dims=(0,),
    )
    return lax.gather(
        x, idx[..., None], dims, slice_sizes=(1, 1), mode=lax.GatherScatterMode.PROMISE_IN_BOUNDS
    )


def iota(shape, axis):
    return lax.broadcasted_iota(I32, shape, axis)


def search(near, upper, marks, want):
    counts = jnp.dot(near, upper, preferred_element_type=F32).astype(I32)
    known = jnp.dot(near, marks, preferred_element_type=F32).astype(I32)
    high = known[:, 128:256] <= want
    pos = jnp.where(high, 64, 0)
    pos += jnp.where(jnp.where(high, known[:, 256:384], known[:, 0:128]) <= want, 32, 0)
    for step in (16, 8, 4, 2, 1):
        pos = jnp.where(take_lanes(counts, pos + (step - 1)) <= want, pos + step, pos)
    return pos, known[:, 384:512]


def halves(n):
    return (n // 2, 2) if n % 2 == 0 else (n, 1)


def split(x):
    high = x.astype(BF16).astype(F32)
    rest = x - high
    middle = rest.astype(BF16).astype(F32)
    return high, middle, rest - middle


def features(coords, extra, own):
    rows = []
    for x in coords:
        h, m, t = split(x)
        rows += [h, h, m, h, t, m] if own else [h, m, h, t, h, m]
    total = coords[0] * coords[0] + coords[1] * coords[1] + coords[2] * coords[2] + extra
    one = jnp.ones_like(total)
    square = list(split(total))
    return rows + (square + [one] * 3 if own else [one] * 3 + square)


def spread(shape, parts):
    depth = iota(shape, 0)
    return (depth < (128 // parts) * (iota(shape, 1) // 128 + 1)).astype(F32).astype(BF16)


def gather_kernel(
    nb,
    ng,
    rows,
    lrows,
    off_ref,
    cp_ref,
    rw_ref,
    po_ref,
    db_ref,
    rb_ref,
    flow_ref,
    base_ref,
    fil_ref,
    tot_ref,
    box_ref,
    midp_ref,
    nfeat_ref,
    don_ref,
    rec_ref,
    name_ref,
    allf_ref,
    pts,
    lst,
    allp,
    alll,
    pnt,
    node,
    mid,
    names,
    sp,
    rp,
    sl,
    rl,
    sf,
    rf,
):
    b = lax.axis_index("bulk")
    g = lax.axis_index("grid")
    high, low = halves(ng)
    along = g // low
    place = g - along * low

    def source(t):
        flip = t // high
        return lax.rem(along + (t - flip * high), high) * low + lax.rem(place + flip, low)

    line = [source(t) for t in range(1, high)]
    pair = [source(high)] if low == 2 else []
    barrier = pltpu.get_barrier_semaphore()

    def across(at, size, i):
        if size & (size - 1):
            return lax.rem(at + i, size)
        to = at
        for k in range(size.bit_length() - 1):
            if i >> k & 1:
                to = to + (1 << k) - (2 << k) * lax.rem(at // (1 << k), 2)
        return to

    def back(size, i):
        return -i % size if size & (size - 1) else i

    def there(i, j):
        return (across(b, nb, i), across(g, ng, j))

    peers = [there(0, j) for j in range(1, ng)] + [there(i, 0) for i in range(1, nb)]
    for peer in peers:
        pl.semaphore_signal(barrier, inc=1, device_id=peer, device_id_type=MESH)

    radial, lines = off_ref.shape[1:]
    slots = po_ref.shape[1]
    for c in range(3):
        for i in range(rows):
            pts[c * rows + i : c * rows + i + 1, :] = cp_ref[c : c + 1, 128 * i : 128 * i + 128]
            pts[(3 + c) * rows + i : (3 + c) * rows + i + 1, :] = rw_ref[c : c + 1, 128 * i : 128 * i + 128]
    for c, (ref, fill) in enumerate(((po_ref, -4 * ng), (db_ref, 0), (rb_ref, 0))):
        for i in range(lrows):
            at = c * lrows + i
            size = min(128, slots - 128 * i)
            if size < 128:
                lst[at : at + 1, :] = jnp.full((1, 128), fill, I32)
            lst[at : at + 1, 0:size] = ref[0:1, 128 * i : 128 * i + size]
    theta = jnp.full((1, 128), 2.0 * math.pi / nb, F32) * b.astype(F32)
    radius = 1.0 + 0.25 * iota((radial, 128), 0).astype(F32)
    height = 0.1 * iota((radial, 128), 1).astype(F32)
    base_ref[0] = (0.5 * g.astype(F32) + radius * jnp.cos(theta)) + off_ref[0]
    base_ref[1] = radius * jnp.sin(theta) + off_ref[1]
    base_ref[2] = height + off_ref[2]
    pl.semaphore_wait(barrier, len(peers))

    sent = {"p": [], "l": []}

    def ring(i, j):
        return back(nb, i) * ng + back(ng, j)

    def send_points(source, slot, peer):
        copy = pltpu.make_async_remote_copy(
            src_ref=source,
            dst_ref=allp.at[slot],
            send_sem=sp.at[len(sent["p"])],
            recv_sem=rp.at[slot],
            device_id=peer,
            device_id_type=MESH,
        )
        copy.start()
        sent["p"].append(copy)

    def points_arrived(slot):
        pltpu.make_async_remote_copy(
            src_ref=pts,
            dst_ref=allp.at[slot],
            send_sem=sp.at[0],
            recv_sem=rp.at[slot],
            device_id=peers[0],
            device_id_type=MESH,
        ).wait_recv()

    def list_copy(slot, n, peer):
        return pltpu.make_async_remote_copy(
            src_ref=lst,
            dst_ref=alll.at[slot],
            send_sem=sl.at[n],
            recv_sem=rl.at[slot],
            device_id=peer,
            device_id_type=MESH,
        )

    flows = []

    def flow_copy(slot, n, t):
        return pltpu.make_async_remote_copy(
            src_ref=flow_ref,
            dst_ref=allf_ref.at[slot],
            send_sem=sf.at[n],
            recv_sem=rf.at[slot],
            device_id=(b, (pair + line)[t]),
            device_id_type=MESH,
        )

    for j in range(1, ng):
        send_points(pts, ring(0, j), there(0, j))
    for i in range(1, nb):
        send_points(pts, ring(i, 0), there(i, 0))
    for j in range(1, ng):
        copy = list_copy(g, j, there(0, j))
        copy.start()
        sent["l"].append(copy)
    allp[0] = pts[...]
    alll[g] = lst[...]

    npat = radial // JOIN
    lane8 = iota((8, 128), 1)
    sub8 = iota((8, 128), 0)
    blocks_of_lanes = lane8 // 16
    within = lane8 - 16 * blocks_of_lanes
    upper = (iota((128, 128), 0) <= iota((128, 128), 1)).astype(F32).astype(BF16)
    marks = spread((128, 512), 4)
    lows, highs = [], []
    for c in range(3):
        for jg in range(radial // 8):
            v = base_ref[c, 8 * jg : 8 * jg + 8, :]
            got = jnp.zeros((8, 128), F32)
            for j in range(8):
                row = jnp.broadcast_to(v[j : j + 1, :], (8, 128))
                got = jnp.where(blocks_of_lanes == j, take_lanes(row, 16 * sub8 + within), got)
            node[c, 8 * jg : 8 * jg + 8, :] = got
        full = node[c]
        lo = jnp.min(full, axis=1, keepdims=True)
        hi = jnp.max(full, axis=1, keepdims=True)
        for q in range(npat):
            mine = slice(q * JOIN, (q + 1) * JOIN)
            least = jnp.min(lo[mine], axis=0, keepdims=True)
            most = jnp.max(hi[mine], axis=0, keepdims=True)
            box_ref[2 * c, q] = jnp.broadcast_to(least, (8, 128))
            box_ref[2 * c + 1, q] = jnp.broadcast_to(most, (8, 128))
            half = (least + most) * 0.4
            mid[c, mine, :] = jnp.broadcast_to(half, (JOIN, 128))
            midp_ref[c, q * 4 : (q + 1) * 4, :] = jnp.broadcast_to(half, (4, 128))
        lows.append(jnp.min(lo, axis=0, keepdims=True))
        highs.append(jnp.max(hi, axis=0, keepdims=True))

    for j in range(1, ng):
        points_arrived(j)
        for i in range(1, nb):
            send_points(allp.at[j], back(nb, i) * ng + j, there(i, 0))
    for t in range(len(pair + line)):
        copy = flow_copy(g, t, t)
        copy.start()
        flows.append(copy)
    mine = features([node[c] * 0.8 - mid[c] for c in range(3)], 0.0, True)
    for f in range(24):
        nfeat_ref[f // 8, pl.ds(f % 8, radial, stride=8), :] = mine[f] * (-2.0 if f < 18 else 1.0)

    chunk = ng * rows
    peak = jnp.zeros((8, 128), I32)
    for part in (range(0, 1), range(1, 2), range(2, nb)):
        for d in range(part.start * ng, part.stop * ng):
            if part.start:
                points_arrived(d)
            for c in range(6):
                pnt[c, d * rows : (d + 1) * rows, :] = allp[d, c * rows : (c + 1) * rows, :]
        size = chunk * len(part)
        if not size:
            continue
        mine = slice(part.start * chunk, part.stop * chunk)
        lane = iota((size, 128), 1)
        dist = jnp.zeros((size, 128), F32)
        for c in range(3):
            p = pnt[c, mine, :]
            e = jnp.maximum(jnp.maximum(lows[c] - p, p - highs[c]), 0.0)
            dist = dist + e * e
        near = (dist < CULL).astype(F32).astype(BF16)
        pos, total = search(near, upper, marks, lane)
        for r in range(size // 8):
            peak = jnp.maximum(peak, total[8 * r : 8 * r + 8])
        for c in range(6):
            v = take_lanes(pnt[c, mine, :], pos)
            v = jnp.where(lane < total, v, FAR if c < 3 else 0.0)
            fil_ref[c, :, mine] = v.T
        if part.start == 0:
            for j in range(1, ng):
                list_copy(lax.rem(g + j, ng), 0, peers[0]).wait_recv()
            for k in range(ng):
                for r in range(3 * lrows):
                    names[r, k : k + 1, :] = alll[k, r : r + 1, :]
            owner = iota((ng, 128), 0)
            place = iota((ng, 128), 1)
            before = jnp.zeros((ng, 128), I32)
            don = jnp.zeros((ng, 128), I32)
            rec = jnp.zeros((ng, 128), I32)
            for r in range(lrows):
                target = owner + 1 + names[r]
                target = jnp.where(target >= ng, target - ng, target)
                chosen = (target == g).astype(F32).astype(BF16)
                want = place - before
                pos, total = search(chosen, upper, marks, want)
                keep = jnp.logical_and(want >= 0, want < total)
                don = jnp.where(keep, take_lanes(names[lrows + r], pos), don)
                rec = jnp.where(keep, take_lanes(names[2 * lrows + r], pos), rec)
                before = before + total
            don_ref[...] = don
            rec_ref[...] = rec
            name_ref[...] = jnp.where(place < before, rec, -1)
    tot_ref[...] = peak
    for s in pair + line:
        flow_copy(s, 0, 0).wait_recv()
    for copy in flows:
        copy.wait_send()
    for kind in sent:
        for copy in sent[kind]:
            copy.wait_send()


def tile(p, nfeat, pfeat, wts):
    none = jnp.zeros((8, 128), F32)
    rhs = []
    for m in range(JOIN):
        row = pl.multiple_of((p * JOIN + m) * 8, 8)
        rhs.append(
            jnp.concatenate([nfeat[t, pl.ds(row, 8), :] for t in range(3)] + [none], axis=0)
        )
    rhs = jnp.concatenate(rhs, axis=1).astype(BF16)
    total = None
    for r in range(4):
        row = pl.multiple_of((p * 4 + r) * 8, 8)
        lhs = jnp.concatenate([pfeat[t, pl.ds(row, 8), :] for t in range(3)] + [none], axis=0)
        sq = lax.dot_general(
            lhs.astype(BF16), rhs, (((0,), (0,)), ((), ())), preferred_element_type=F32
        )
        sq = jnp.maximum(sq, 1e-30)
        near = jnp.maximum(1.0 - sq * lax.rsqrt(sq), 0.0)
        two = near * near
        phi = two * two * (1.25 - near)
        hi = phi.astype(BF16)
        lo = (phi - hi.astype(F32)).astype(BF16)
        vals = wts[pl.ds(row, 8), :]
        vhi = vals.astype(BF16).astype(F32)
        both = jnp.concatenate([vhi, vals - vhi], axis=0).astype(BF16)
        got = jnp.dot(
            jnp.concatenate([both, both], axis=1),
            jnp.concatenate([hi, lo], axis=0),
            preferred_element_type=F32,
        )
        total = got if total is None else total + got
    return total[0:8] + total[8:16]


def evaluate(first, last, nfeat, pfeat, wts, acc):
    @pl.loop(first // TILES, last // TILES)
    def _(i):
        for q in range(TILES):
            p = i * TILES + q
            total = tile(p, nfeat, pfeat, wts)
            for m in range(JOIN):
                row = pl.multiple_of((p * JOIN + m) * 8, 8)
                acc[pl.ds(row, 8), :] += total[:, 128 * m : 128 * m + 128]


def cull_kernel(
    fil, tot_ref, box, midp, nfeat, pfeat_ref, wts_ref, acc_ref, out, basec, pmore, wmore
):
    npat = box.shape[1]
    sub8 = iota((8, 128), 0)
    upper = (iota((128, 128), 0) <= iota((128, 128), 1)).astype(F32).astype(BF16)
    groups = (jnp.max(tot_ref[...]) + 7) // 8
    wide = npat * 8
    low_sub = sub8 < 4
    lane_w = iota((wide, 128), 1)
    row_w = iota((wide, 128), 0)
    slot = jnp.where(row_w - 8 * (row_w // 8) < 4, lane_w, 127 - lane_w)
    marks = spread((128, 512), 4)

    def close(gi):
        start = pl.multiple_of(gi * 8, 8)
        src = [fil[c, pl.ds(start, 8), :][None] for c in range(6)]
        dist = jnp.zeros((npat, 8, 128), F32)
        for c in range(3):
            e = jnp.maximum(jnp.maximum(box[2 * c] - src[c], src[c] - box[2 * c + 1]), 0.0)
            dist = dist + e * e
        return src, (dist < CULL).astype(F32).reshape(wide, 128).astype(BF16)

    basec[...] = jnp.zeros(basec.shape, I32)

    @pl.loop(0, groups)
    def _(gi):
        _, near = close(gi)
        basec[...] += jnp.dot(near, marks[:, 384:512], preferred_element_type=F32).astype(I32)

    length = basec[...].reshape(npat, 8, 128)
    pair = length + jnp.concatenate([length[:, 4:8], length[:, 0:4]], axis=1)
    whole = jnp.max(pair) <= 128
    width = jnp.where(whole, 128, 64)
    pages = (jnp.max(length) + width - 1) // width

    def compact(page, pfeat, wts):
        basec[...] = jnp.zeros(basec.shape, I32)
        out[...] = jnp.zeros(out.shape, F32)
        target = slot + width * page

        @pl.loop(0, groups)
        def _(gi):
            src, near = close(gi)
            before = basec[...]
            want = target - before
            pos, amount = search(near, upper, marks, want)
            keep = jnp.logical_and(jnp.logical_and(want >= 0, want < amount), slot < width)
            for c in range(6):
                v = jnp.broadcast_to(src[c], (npat, 8, 128)).reshape(wide, 128)
                out[c] = jnp.where(keep, take_lanes(v, pos), out[c])
            basec[...] = before + amount

        cols = []
        for c in range(6):
            parts = []
            for p in range(0, npat, 2):
                one = out[c, p * 8 : p * 8 + 8, :]
                two = out[c, p * 8 + 8 : p * 8 + 16, :]
                one = one + pltpu.roll(one, 4, 0)
                two = two + pltpu.roll(two, 4, 0)
                parts.append(jnp.where(low_sub, one, two))
            cols.append(jnp.concatenate(parts, axis=0))
        theirs = features([cols[c] * 0.8 - midp[c] for c in range(3)], 0.0, False)
        for f in range(24):
            pfeat[f // 8, pl.ds(f % 8, npat * 4, stride=8), :] = theirs[f]
        for c in range(8):
            wts[pl.ds(c, npat * 4, stride=8), :] = 4.0 * cols[3 + c] if c < 3 else jnp.zeros_like(cols[0])

    compact(0, pfeat_ref, wts_ref)
    acc_ref[...] = jnp.zeros(acc_ref.shape, F32)

    @pl.loop(1, pages)
    def _(page):
        compact(page, pmore, wmore)
        evaluate(0, npat, nfeat, pmore, wmore, acc_ref)


def finish_kernel(
    nb,
    ng,
    don_ref,
    rec_ref,
    name_ref,
    base_ref,
    nfeat_ref,
    pfeat_ref,
    wts_ref,
    more_ref,
    allf,
    mov_ref,
    met_ref,
    out_ref,
    acc,
    halo,
    allm,
    allt,
    allg,
    rows,
    own,
    far,
    far_too,
    val,
    wone,
    wtwo,
    res,
    sh,
    rh,
    sm,
    rm,
    st,
    rt,
    sf,
    rf,
):
    b = lax.axis_index("bulk")
    g = lax.axis_index("grid")
    after = lax.rem(b + 1, nb)
    before = lax.rem(b + nb - 1, nb)
    high, low = halves(ng)
    along = g // low
    place = g - along * low

    def source(t):
        flip = t // high
        return lax.rem(along + (t - flip * high), high) * low + lax.rem(place + flip, low)

    near = [source(t) for t in range(1, high)]
    pair = [source(high)] if low == 2 else []
    barrier = pltpu.get_barrier_semaphore()
    peers = [(before, g), (after, g)] + [(b, source(t)) for t in range(1, ng)]
    for peer in peers:
        pl.semaphore_signal(barrier, inc=1, device_id=peer, device_id_type=MESH)

    radial, lines = mov_ref.shape[1:]
    nvar = out_ref.shape[0]
    acc[...] = more_ref[...]
    npat = radial // JOIN
    middle = npat // (2 * TILES) * TILES
    evaluate(0, middle, nfeat_ref, pfeat_ref, wts_ref, acc)
    pl.semaphore_wait(barrier, len(peers))
    passed = []

    def flow_copy(t):
        return pltpu.make_async_remote_copy(
            src_ref=allf.at[source(t)],
            dst_ref=allg.at[t - 1],
            send_sem=sf.at[t - 1],
            recv_sem=rf.at[t - 1],
            device_id=(b, source(high)),
            device_id_type=MESH,
        )

    if pair:
        for t in range(1, high):
            copy = flow_copy(t)
            copy.start()
            passed.append(copy)
    evaluate(middle, npat, nfeat_ref, pfeat_ref, wts_ref, acc)
    lane8 = iota((8, 128), 1)
    sub8 = iota((8, 128), 0)
    blocks_of_lanes = lane8 // 16
    within = lane8 - 16 * blocks_of_lanes
    for c in range(3):
        for jg in range(radial // 8):
            s = acc[pl.ds(64 * jg + c, 8, stride=8), :]
            got = jnp.zeros((8, 128), F32)
            for kg in range(8):
                row = jnp.broadcast_to(s[kg : kg + 1, :], (8, 128))
                got = jnp.where(blocks_of_lanes == kg, take_lanes(row, 16 * sub8 + within), got)
            mov_ref[c, 8 * jg : 8 * jg + 8, :] = base_ref[c, 8 * jg : 8 * jg + 8, :] + got
    halos = [
        pltpu.make_async_remote_copy(
            src_ref=mov_ref,
            dst_ref=halo.at[i],
            send_sem=sh.at[i],
            recv_sem=rh.at[i],
            device_id=(t, g),
            device_id_type=MESH,
        )
        for i, t in enumerate((after, before))
    ]
    for copy in halos:
        copy.start()
    sent = {"m": [], "t": []}

    def describe(kind, slot, peer, mine, n):
        src, full, ss, rs = {
            "m": (mov_ref, allm, sm, rm),
            "t": (met_ref, allt, st, rt),
        }[kind]
        return pltpu.make_async_remote_copy(
            src_ref=src if mine else full.at[slot],
            dst_ref=full.at[slot],
            send_sem=ss.at[n],
            recv_sem=rs.at[slot],
            device_id=(b, peer),
            device_id_type=MESH,
        )

    def send(kind, slot, peer, mine):
        copy = describe(kind, slot, peer, mine, len(sent[kind]))
        copy.start()
        sent[kind].append(copy)

    def arrived(kind, slot):
        describe(kind, slot, source(1), False, 0).wait_recv()

    for t in pair + near:
        send("m", g, t, True)
    row = iota((radial, lines), 0)
    col = iota((radial, lines), 1)
    dj, dk, centre = [], [], []
    for c in range(3):
        m = mov_ref[c]
        up, down = pltpu.roll(m, radial - 1, 0), pltpu.roll(m, 1, 0)
        dj.append(
            jnp.where(row == 0, up - m, jnp.where(row == radial - 1, m - down, (up - down) * 0.5))
        )
        up, down = pltpu.roll(m, lines - 1, 1), pltpu.roll(m, 1, 1)
        dk.append(
            jnp.where(col == 0, up - m, jnp.where(col == lines - 1, m - down, (up - down) * 0.5))
        )
        total = jnp.sum(jnp.sum(m, axis=0, keepdims=True), axis=1, keepdims=True)
        centre.append(total * (1.0 / (radial * lines)))
    cross = [
        dj[1] * dk[2] - dj[2] * dk[1],
        dj[2] * dk[0] - dj[0] * dk[2],
        dj[0] * dk[1] - dj[1] * dk[0],
    ]
    zero = jnp.zeros((8, 128), F32)
    mine = features([mov_ref[c] - centre[c] for c in range(3)], 0.0, True)
    for f in range(24):
        rows[f // 8, pl.ds(f % 8, radial, stride=8), :] = mine[f] * (-2.0 if f < 18 else 1.0)
    for r in range(radial):
        parts = [rows[p, r * 8 : (r + 1) * 8, :] for p in range(3)]
        own[r] = jnp.concatenate(parts + [zero], axis=0).astype(BF16)
    res[...] = jnp.zeros(res.shape, F32)

    for copy in halos:
        copy.wait_recv()
    di = [(halo[1, c] - halo[0, c]) * 0.5 for c in range(3)]
    met_ref[...] = di[0] * cross[0] + di[1] * cross[1] + di[2] * cross[2]
    for t in range(ng - 1, 0, -1):
        send("t", g, source(t), True)
    for s in near:
        arrived("m", s)
        for t in pair:
            send("m", s, t, False)

    none = jnp.zeros((32, 128), BF16)

    def prepare(t, far):
        s = source(t)
        theirs = features([allm[s, c] - centre[c] for c in range(3)], 0.25, False)
        for f in range(24):
            rows[f // 8, pl.ds(f % 8, radial, stride=8), :] = theirs[f]
        for r in range(radial):
            for p in range(3):
                far[p, r] = rows[p, r * 8 : (r + 1) * 8, :]

    def weigh(t, e, far, wgt, slot):
        s = source(t)
        left, right = [], []
        for q in range(2):
            left += [far[p, don_ref[s, e + q]] for p in range(3)] + [zero]
            right.append(own[rec_ref[s, e + q]])
        right = [
            jnp.concatenate([right[0], none], axis=1),
            jnp.concatenate([none, right[1]], axis=1),
        ]
        den = lax.dot_general(
            jnp.concatenate(left, axis=0).astype(BF16),
            jnp.concatenate(right, axis=0),
            (((0,), (0,)), ((), ())),
            preferred_element_type=F32,
        )
        w = pl.reciprocal(den, approx=False)
        hi = w.astype(BF16)
        wgt[slot * HALF + e // 2, 0:128, :] = hi
        wgt[slot * HALF + e // 2, 128:256, :] = (w - hi.astype(F32)).astype(BF16)

    def load(t, flows, slot):
        met = allt[source(t)]
        for v in range(8):
            row = met * flows[slot, v] if v < nvar else jnp.full((radial, 128), 1.0 if v == nvar else 0.0, F32)
            rows[0, pl.ds(v, radial, stride=8), :] = row
        for r in range(radial):
            val[r] = rows[0, r * 8 : (r + 1) * 8, :]

    def blend(t, e, wgt, slot):
        s = source(t)
        left = []
        for q in range(2):
            vals = val[don_ref[s, e + q]]
            vhi = vals.astype(BF16).astype(F32)
            both = jnp.concatenate([vhi, vals - vhi], axis=0).astype(BF16)
            left.append(jnp.concatenate([both, both], axis=1))
        got = jnp.dot(
            jnp.concatenate(left, axis=0),
            wgt[slot * HALF + e // 2],
            preferred_element_type=F32,
        )
        for q in range(2):
            one = got[16 * q : 16 * q + 8, 128 * q : 128 * q + 128]
            one = one + got[16 * q + 8 : 16 * q + 16, 128 * q : 128 * q + 128]
            one = one / one[nvar : nvar + 1, :]
            at = pl.multiple_of((t * HOLD + e + q) * 8, 8)
            res[pl.ds(at, 8), :] = one

    for s in pair:
        arrived("m", s)
    first = high if pair else high - 1
    rest = ng - 1 - first

    both = 2 - first % 2

    @pl.loop(0, first // both)
    def _(i):
        for q in range(both):
            prepare(1 + i * both + q, (far, far_too)[q])
        for e in range(0, MOST, 2):
            for q in range(both):
                t = 1 + i * both + q
                weigh(t, e, (far, far_too)[q], wone, t - 1)

    @pl.loop(1, rest + 1)
    def _(t):
        arrived("m", source(first + t))
        arrived("t", source(t))
        prepare(first + t, far)
        load(t, allf, source(t))
        for e in range(0, MOST, 2):
            weigh(first + t, e, far, wtwo, t - 1)
            blend(t, e, wone, t - 1)

    @pl.loop(rest + 1, first + 1)
    def _(t):
        arrived("t", source(t))
        load(t, allf, source(t))
        for e in range(0, MOST, 2):
            blend(t, e, wone, t - 1)

    for t in range(1, len(passed) + 1):
        flow_copy(t).wait_recv()

    @pl.loop(first + 1, ng)
    def _(t):
        arrived("t", source(t))
        load(t, allg, t - first - 1)
        for e in range(0, MOST, 2):
            blend(t, e, wtwo, t - first - 1)

    total = None
    blocks = iota((radial, 128), 0)
    for t in range(1, ng):
        name = jnp.broadcast_to(name_ref[pl.ds(source(t), 1), :], (radial, 128))
        pick = (name == blocks).astype(F32).astype(BF16)[:, 0:HOLD]
        cols = [res[pl.ds(t * HOLD * 8 + v, HOLD, stride=8), :] for v in range(nvar)]
        for part in split(jnp.concatenate(cols, axis=1))[:2]:
            got = jnp.dot(pick, part.astype(BF16), preferred_element_type=F32)
            total = got if total is None else total + got
    for v in range(nvar):
        out_ref[v] = total[:, 128 * v : 128 * v + 128]
    for copy in halos + passed + sent["m"] + sent["t"]:
        copy.wait_send()


def local(offsets, flow, control_points, rbf_weights, peer_offset, donor_block, receptor_block):
    _, _, planes, radial, lines = offsets.shape
    nvar = flow.shape[1]
    nb = lax.axis_size("bulk")
    ng = lax.axis_size("grid")
    nd = nb * ng
    nd = nb * ng
    rows = control_points.shape[1] // 128
    slots = donor_block.shape[1]
    lrows = -(-slots // 128)
    npat = radial // JOIN
    dma = pltpu.SemaphoreType.DMA
    sds = jax.ShapeDtypeStruct
    base, fil, tot, box, midp, nfeat, don, rec, name, allf = pl.pallas_call(
        functools.partial(gather_kernel, nb, ng, rows, lrows),
        out_shape=(
            sds((3, radial, lines), F32),
            sds((6, 128, 128), F32),
            sds((8, 128), I32),
            sds((6, npat, 8, 128), F32),
            sds((3, npat * 4, 128), F32),
            sds((3, radial * 8, 128), F32),
            sds((ng, 128), I32),
            sds((ng, 128), I32),
            sds((ng, 128), I32),
            sds((ng, nvar, radial, lines), F32),
        ),
        in_specs=[VMEM_SPEC] * 7,
        out_specs=[VMEM_SPEC] * 10,
        scratch_shapes=[
            pltpu.VMEM((6 * rows, 128), F32),
            pltpu.VMEM((3 * lrows, 128), I32),
            pltpu.VMEM((nd, 6 * rows, 128), F32),
            pltpu.VMEM((ng, 3 * lrows, 128), I32),
            pltpu.VMEM((6, nd * rows, 128), F32),
            pltpu.VMEM((3, radial, 128), F32),
            pltpu.VMEM((3, radial, 128), F32),
            pltpu.VMEM((3 * lrows, ng, 128), I32),
            dma((nd,)),
            dma((nd,)),
            dma((ng,)),
            dma((ng,)),
            dma((2 * ng,)),
            dma((ng,)),
        ],
        compiler_params=pltpu.CompilerParams(collective_id=0, has_side_effects=True),
        name="gather_points",
    )(
        offsets.reshape(3, radial, lines),
        control_points,
        rbf_weights,
        peer_offset.reshape(1, slots),
        donor_block,
        receptor_block,
        flow.reshape(nvar, radial, lines),
    )
    pfeat, wts, more = pl.pallas_call(
        cull_kernel,
        out_shape=(
            sds((3, npat * 32, 128), F32),
            sds((npat * 32, 128), F32),
            sds((radial * 8, 128), F32),
        ),
        in_specs=[VMEM_SPEC] * 5,
        out_specs=[VMEM_SPEC] * 3,
        scratch_shapes=[
            pltpu.VMEM((6, npat * 8, 128), F32),
            pltpu.VMEM((npat * 8, 128), I32),
            pltpu.VMEM((3, npat * 32, 128), F32),
            pltpu.VMEM((npat * 32, 128), F32),
        ],
        name="cull_points",
    )(fil, tot, box, midp, nfeat)
    first = halves(ng)[0] if halves(ng)[1] == 2 else ng - 1
    moved, metric, fringe = pl.pallas_call(
        functools.partial(finish_kernel, nb, ng),
        out_shape=(
            sds((3, radial, lines), F32),
            sds((radial, lines), F32),
            sds((nvar, radial, lines), F32),
        ),
        in_specs=[SMEM_SPEC] * 2 + [VMEM_SPEC] * 7,
        out_specs=[VMEM_SPEC] * 3,
        scratch_shapes=[
            pltpu.VMEM((radial * 8, 128), F32),
            pltpu.VMEM((2, 3, radial, lines), F32),
            pltpu.VMEM((ng, 3, radial, lines), F32),
            pltpu.VMEM((ng, radial, lines), F32),
            pltpu.VMEM((halves(ng)[0], nvar, radial, lines), F32),
            pltpu.VMEM((3, radial * 8, 128), F32),
            pltpu.VMEM((radial, 32, 128), BF16),
            pltpu.VMEM((3, radial, 8, 128), F32),
            pltpu.VMEM((3, radial, 8, 128), F32),
            pltpu.VMEM((radial, 8, 128), F32),
            pltpu.VMEM((first * HALF, 256, 256), BF16),
            pltpu.VMEM(((ng - 1 - first) * HALF, 256, 256), BF16),
            pltpu.VMEM((ng * HOLD * 8, 128), F32),
            dma((2,)),
            dma((2,)),
            dma((2 * ng,)),
            dma((ng,)),
            dma((2 * ng,)),
            dma((ng,)),
            dma((ng,)),
            dma((ng,)),
        ],
        compiler_params=pltpu.CompilerParams(
            collective_id=1,
            has_side_effects=True,
            vmem_limit_bytes=60 << 20,
        ),
        name="finish",
    )(don, rec, name, base, nfeat, pfeat, wts, more, allf)
    return (
        moved.reshape(1, 3, planes, radial, lines),
        metric.reshape(1, planes, radial, lines),
        fringe.reshape(1, nvar, planes, radial, lines),
    )


def solution(mesh):
    in_specs = (
        P("grid", None, "bulk", None, None),
        P("grid", None, "bulk", None, None),
        P(None, ("bulk", "grid")),
        P(None, ("bulk", "grid")),
        P("grid", "bulk", None),
        P("grid", "bulk"),
        P("grid", "bulk"),
    )
    out_specs = (
        P("grid", None, "bulk", None, None),
        P("grid", "bulk", None, None),
        P("grid", None, "bulk", None, None),
    )
    return jax.shard_map(local, mesh=mesh, in_specs=in_specs, out_specs=out_specs, check_vma=False)
```

```python
import functools
import math

import jax
import jax.numpy as jnp
from jax import lax
from jax.experimental import pallas as pl
from jax.experimental.pallas import tpu as pltpu
from jax.sharding import PartitionSpec as P

MESH = pl.DeviceIdType.MESH
SUPPORT = 1.25
CULL = SUPPORT * SUPPORT * 1.0001
FAR = 1.0e9
JOIN = 2
TILES = 6
MOST = 28
HALF = MOST // 2
HOLD = 32
F32 = jnp.float32
I32 = jnp.int32
BF16 = jnp.bfloat16
VMEM_SPEC = pl.BlockSpec(memory_space=pltpu.VMEM)
SMEM_SPEC = pl.BlockSpec(memory_space=pltpu.SMEM)


def take_lanes(x, idx):
    dims = lax.GatherDimensionNumbers(
        offset_dims=(),
        collapsed_slice_dims=(1,),
        start_index_map=(1,),
        operand_batching_dims=(0,),
        start_indices_batching_dims=(0,),
    )
    return lax.gather(
        x, idx[..., None], dims, slice_sizes=(1, 1), mode=lax.GatherScatterMode.PROMISE_IN_BOUNDS
    )


def iota(shape, axis):
    return lax.broadcasted_iota(I32, shape, axis)


def search(near, upper, marks, want):
    counts = jnp.dot(near, upper, preferred_element_type=F32).astype(I32)
    known = jnp.dot(near, marks, preferred_element_type=F32).astype(I32)
    high = known[:, 128:256] <= want
    pos = jnp.where(high, 64, 0)
    pos += jnp.where(jnp.where(high, known[:, 256:384], known[:, 0:128]) <= want, 32, 0)
    for step in (16, 8, 4, 2, 1):
        pos = jnp.where(take_lanes(counts, pos + (step - 1)) <= want, pos + step, pos)
    return pos, known[:, 384:512]


def halves(n):
    return (n // 2, 2) if n % 2 == 0 else (n, 1)


def split(x):
    high = x.astype(BF16).astype(F32)
    rest = x - high
    middle = rest.astype(BF16).astype(F32)
    return high, middle, rest - middle


def features(coords, extra, own):
    rows = []
    for x in coords:
        h, m, t = split(x)
        rows += [h, h, m, h, t, m] if own else [h, m, h, t, h, m]
    total = coords[0] * coords[0] + coords[1] * coords[1] + coords[2] * coords[2] + extra
    one = jnp.ones_like(total)
    square = list(split(total))
    return rows + (square + [one] * 3 if own else [one] * 3 + square)


def spread(shape, parts):
    depth = iota(shape, 0)
    return (depth < (128 // parts) * (iota(shape, 1) // 128 + 1)).astype(F32).astype(BF16)


def gather_kernel(
    nb,
    ng,
    rows,
    lrows,
    off_ref,
    cp_ref,
    rw_ref,
    po_ref,
    db_ref,
    rb_ref,
    flow_ref,
    base_ref,
    fil_ref,
    tot_ref,
    box_ref,
    midp_ref,
    nfeat_ref,
    don_ref,
    rec_ref,
    name_ref,
    allf_ref,
    pts,
    lst,
    allp,
    alll,
    pnt,
    node,
    mid,
    names,
    sp,
    rp,
    sl,
    rl,
    sf,
    rf,
):
    b = lax.axis_index("bulk")
    g = lax.axis_index("grid")
    high, low = halves(ng)
    along = g // low
    place = g - along * low

    def source(t):
        flip = t // high
        return lax.rem(along + (t - flip * high), high) * low + lax.rem(place + flip, low)

    line = [source(t) for t in range(1, high)]
    pair = [source(high)] if low == 2 else []
    barrier = pltpu.get_barrier_semaphore()

    def across(at, size, i):
        if size & (size - 1):
            return lax.rem(at + i, size)
        to = at
        for k in range(size.bit_length() - 1):
            if i >> k & 1:
                to = to + (1 << k) - (2 << k) * lax.rem(at // (1 << k), 2)
        return to

    def back(size, i):
        return -i % size if size & (size - 1) else i

    def there(i, j):
        return (across(b, nb, i), across(g, ng, j))

    peers = [there(0, j) for j in range(1, ng)] + [there(i, 0) for i in range(1, nb)]
    for peer in peers:
        pl.semaphore_signal(barrier, inc=1, device_id=peer, device_id_type=MESH)

    radial, lines = off_ref.shape[1:]
    slots = po_ref.shape[1]
    for c in range(3):
        for i in range(rows):
            pts[c * rows + i : c * rows + i + 1, :] = cp_ref[c : c + 1, 128 * i : 128 * i + 128]
            pts[(3 + c) * rows + i : (3 + c) * rows + i + 1, :] = rw_ref[c : c + 1, 128 * i : 128 * i + 128]
    for c, (ref, fill) in enumerate(((po_ref, -4 * ng), (db_ref, 0), (rb_ref, 0))):
        for i in range(lrows):
            at = c * lrows + i
            size = min(128, slots - 128 * i)
            if size < 128:
                lst[at : at + 1, :] = jnp.full((1, 128), fill, I32)
            lst[at : at + 1, 0:size] = ref[0:1, 128 * i : 128 * i + size]
    theta = jnp.full((1, 128), 2.0 * math.pi / nb, F32) * b.astype(F32)
    radius = 1.0 + 0.25 * iota((radial, 128), 0).astype(F32)
    height = 0.1 * iota((radial, 128), 1).astype(F32)
    base_ref[0] = (0.5 * g.astype(F32) + radius * jnp.cos(theta)) + off_ref[0]
    base_ref[1] = radius * jnp.sin(theta) + off_ref[1]
    base_ref[2] = height + off_ref[2]
    pl.semaphore_wait(barrier, len(peers))

    sent = {"p": [], "l": []}

    def ring(i, j):
        return back(nb, i) * ng + back(ng, j)

    def send_points(source, slot, peer):
        copy = pltpu.make_async_remote_copy(
            src_ref=source,
            dst_ref=allp.at[slot],
            send_sem=sp.at[len(sent["p"])],
            recv_sem=rp.at[slot],
            device_id=peer,
            device_id_type=MESH,
        )
        copy.start()
        sent["p"].append(copy)

    def points_arrived(slot):
        pltpu.make_async_remote_copy(
            src_ref=pts,
            dst_ref=allp.at[slot],
            send_sem=sp.at[0],
            recv_sem=rp.at[slot],
            device_id=peers[0],
            device_id_type=MESH,
        ).wait_recv()

    def list_copy(slot, n, peer):
        return pltpu.make_async_remote_copy(
            src_ref=lst,
            dst_ref=alll.at[slot],
            send_sem=sl.at[n],
            recv_sem=rl.at[slot],
            device_id=peer,
            device_id_type=MESH,
        )

    flows = []

    def flow_copy(slot, n, t):
        return pltpu.make_async_remote_copy(
            src_ref=flow_ref,
            dst_ref=allf_ref.at[slot],
            send_sem=sf.at[n],
            recv_sem=rf.at[slot],
            device_id=(b, (pair + line)[t]),
            device_id_type=MESH,
        )

    for j in range(1, ng):
        send_points(pts, ring(0, j), there(0, j))
    for i in range(1, nb):
        send_points(pts, ring(i, 0), there(i, 0))
    for j in range(1, ng):
        copy = list_copy(g, j, there(0, j))
        copy.start()
        sent["l"].append(copy)
    allp[0] = pts[...]
    alll[g] = lst[...]

    npat = radial // JOIN
    lane8 = iota((8, 128), 1)
    sub8 = iota((8, 128), 0)
    blocks_of_lanes = lane8 // 16
    within = lane8 - 16 * blocks_of_lanes
    upper = (iota((128, 128), 0) <= iota((128, 128), 1)).astype(F32).astype(BF16)
    marks = spread((128, 512), 4)
    lows, highs = [], []
    for c in range(3):
        for jg in range(radial // 8):
            v = base_ref[c, 8 * jg : 8 * jg + 8, :]
            got = jnp.zeros((8, 128), F32)
            for j in range(8):
                row = jnp.broadcast_to(v[j : j + 1, :], (8, 128))
                got = jnp.where(blocks_of_lanes == j, take_lanes(row, 16 * sub8 + within), got)
            node[c, 8 * jg : 8 * jg + 8, :] = got
        full = node[c]
        lo = jnp.min(full, axis=1, keepdims=True)
        hi = jnp.max(full, axis=1, keepdims=True)
        for q in range(npat):
            mine = slice(q * JOIN, (q + 1) * JOIN)
            least = jnp.min(lo[mine], axis=0, keepdims=True)
            most = jnp.max(hi[mine], axis=0, keepdims=True)
            box_ref[2 * c, q] = jnp.broadcast_to(least, (8, 128))
            box_ref[2 * c + 1, q] = jnp.broadcast_to(most, (8, 128))
            half = (least + most) * 0.4
            mid[c, mine, :] = jnp.broadcast_to(half, (JOIN, 128))
            midp_ref[c, q * 4 : (q + 1) * 4, :] = jnp.broadcast_to(half, (4, 128))
        lows.append(jnp.min(lo, axis=0, keepdims=True))
        highs.append(jnp.max(hi, axis=0, keepdims=True))

    for j in range(1, ng):
        points_arrived(j)
        for i in range(1, nb):
            send_points(allp.at[j], back(nb, i) * ng + j, there(i, 0))
    for t in range(len(pair + line)):
        copy = flow_copy(g, t, t)
        copy.start()
        flows.append(copy)
    mine = features([node[c] * 0.8 - mid[c] for c in range(3)], 0.0, True)
    for f in range(24):
        nfeat_ref[f // 8, pl.ds(f % 8, radial, stride=8), :] = mine[f] * (-2.0 if f < 18 else 1.0)

    chunk = ng * rows
    peak = jnp.zeros((8, 128), I32)
    for part in (range(0, 1), range(1, 2), range(2, nb)):
        for d in range(part.start * ng, part.stop * ng):
            if part.start:
                points_arrived(d)
            for c in range(6):
                pnt[c, d * rows : (d + 1) * rows, :] = allp[d, c * rows : (c + 1) * rows, :]
        size = chunk * len(part)
        if not size:
            continue
        mine = slice(part.start * chunk, part.stop * chunk)
        lane = iota((size, 128), 1)
        dist = jnp.zeros((size, 128), F32)
        for c in range(3):
            p = pnt[c, mine, :]
            e = jnp.maximum(jnp.maximum(lows[c] - p, p - highs[c]), 0.0)
            dist = dist + e * e
        near = (dist < CULL).astype(F32).astype(BF16)
        pos, total = search(near, upper, marks, lane)
        for r in range(size // 8):
            peak = jnp.maximum(peak, total[8 * r : 8 * r + 8])
        for c in range(6):
            v = take_lanes(pnt[c, mine, :], pos)
            v = jnp.where(lane < total, v, FAR if c < 3 else 0.0)
            fil_ref[c, :, mine] = v.T
        if part.start == 0:
            for j in range(1, ng):
                list_copy(lax.rem(g + j, ng), 0, peers[0]).wait_recv()
            for k in range(ng):
                for r in range(3 * lrows):
                    names[r, k : k + 1, :] = alll[k, r : r + 1, :]
            owner = iota((ng, 128), 0)
            place = iota((ng, 128), 1)
            before = jnp.zeros((ng, 128), I32)
            don = jnp.zeros((ng, 128), I32)
            rec = jnp.zeros((ng, 128), I32)
            for r in range(lrows):
                target = owner + 1 + names[r]
                target = jnp.where(target >= ng, target - ng, target)
                chosen = (target == g).astype(F32).astype(BF16)
                want = place - before
                pos, total = search(chosen, upper, marks, want)
                keep = jnp.logical_and(want >= 0, want < total)
                don = jnp.where(keep, take_lanes(names[lrows + r], pos), don)
                rec = jnp.where(keep, take_lanes(names[2 * lrows + r], pos), rec)
                before = before + total
            don_ref[...] = don
            rec_ref[...] = rec
            name_ref[...] = jnp.where(place < before, rec, -1)
    tot_ref[...] = peak
    for s in pair + line:
        flow_copy(s, 0, 0).wait_recv()
    for copy in flows:
        copy.wait_send()
    for kind in sent:
        for copy in sent[kind]:
            copy.wait_send()


def tile(p, nfeat, pfeat, wts):
    none = jnp.zeros((8, 128), F32)
    rhs = []
    for m in range(JOIN):
        row = pl.multiple_of((p * JOIN + m) * 8, 8)
        rhs.append(
            jnp.concatenate([nfeat[t, pl.ds(row, 8), :] for t in range(3)] + [none], axis=0)
        )
    rhs = jnp.concatenate(rhs, axis=1).astype(BF16)
    total = None
    for r in range(4):
        row = pl.multiple_of((p * 4 + r) * 8, 8)
        lhs = jnp.concatenate([pfeat[t, pl.ds(row, 8), :] for t in range(3)] + [none], axis=0)
        sq = lax.dot_general(
            lhs.astype(BF16), rhs, (((0,), (0,)), ((), ())), preferred_element_type=F32
        )
        sq = jnp.maximum(sq, 1e-30)
        near = jnp.maximum(1.0 - sq * lax.rsqrt(sq), 0.0)
        two = near * near
        phi = two * two * (1.25 - near)
        hi = phi.astype(BF16)
        lo = (phi - hi.astype(F32)).astype(BF16)
        vals = wts[pl.ds(row, 8), :]
        vhi = vals.astype(BF16).astype(F32)
        both = jnp.concatenate([vhi, vals - vhi], axis=0).astype(BF16)
        got = jnp.dot(
            jnp.concatenate([both, both], axis=1),
            jnp.concatenate([hi, lo], axis=0),
            preferred_element_type=F32,
        )
        total = got if total is None else total + got
    return total[0:8] + total[8:16]


def evaluate(first, last, nfeat, pfeat, wts, acc):
    @pl.loop(first // TILES, last // TILES)
    def _(i):
        for q in range(TILES):
            p = i * TILES + q
            total = tile(p, nfeat, pfeat, wts)
            for m in range(JOIN):
                row = pl.multiple_of((p * JOIN + m) * 8, 8)
                acc[pl.ds(row, 8), :] += total[:, 128 * m : 128 * m + 128]


def cull_kernel(
    fil, tot_ref, box, midp, nfeat, pfeat_ref, wts_ref, acc_ref, out, basec, pmore, wmore
):
    npat = box.shape[1]
    sub8 = iota((8, 128), 0)
    upper = (iota((128, 128), 0) <= iota((128, 128), 1)).astype(F32).astype(BF16)
    groups = (jnp.max(tot_ref[...]) + 7) // 8
    wide = npat * 8
    low_sub = sub8 < 4
    lane_w = iota((wide, 128), 1)
    row_w = iota((wide, 128), 0)
    slot = jnp.where(row_w - 8 * (row_w // 8) < 4, lane_w, 127 - lane_w)
    marks = spread((128, 512), 4)

    def close(gi):
        start = pl.multiple_of(gi * 8, 8)
        src = [fil[c, pl.ds(start, 8), :][None] for c in range(6)]
        dist = jnp.zeros((npat, 8, 128), F32)
        for c in range(3):
            e = jnp.maximum(jnp.maximum(box[2 * c] - src[c], src[c] - box[2 * c + 1]), 0.0)
            dist = dist + e * e
        return src, (dist < CULL).astype(F32).reshape(wide, 128).astype(BF16)

    basec[...] = jnp.zeros(basec.shape, I32)

    @pl.loop(0, groups)
    def _(gi):
        _, near = close(gi)
        basec[...] += jnp.dot(near, marks[:, 384:512], preferred_element_type=F32).astype(I32)

    length = basec[...].reshape(npat, 8, 128)
    pair = length + jnp.concatenate([length[:, 4:8], length[:, 0:4]], axis=1)
    whole = jnp.max(pair) <= 128
    width = jnp.where(whole, 128, 64)
    pages = (jnp.max(length) + width - 1) // width

    def compact(page, pfeat, wts):
        basec[...] = jnp.zeros(basec.shape, I32)
        out[...] = jnp.zeros(out.shape, F32)
        target = slot + width * page

        @pl.loop(0, groups)
        def _(gi):
            src, near = close(gi)
            before = basec[...]
            want = target - before
            pos, amount = search(near, upper, marks, want)
            keep = jnp.logical_and(jnp.logical_and(want >= 0, want < amount), slot < width)
            for c in range(6):
                v = jnp.broadcast_to(src[c], (npat, 8, 128)).reshape(wide, 128)
                out[c] = jnp.where(keep, take_lanes(v, pos), out[c])
            basec[...] = before + amount

        cols = []
        for c in range(6):
            parts = []
            for p in range(0, npat, 2):
                one = out[c, p * 8 : p * 8 + 8, :]
                two = out[c, p * 8 + 8 : p * 8 + 16, :]
                one = one + pltpu.roll(one, 4, 0)
                two = two + pltpu.roll(two, 4, 0)
                parts.append(jnp.where(low_sub, one, two))
            cols.append(jnp.concatenate(parts, axis=0))
        theirs = features([cols[c] * 0.8 - midp[c] for c in range(3)], 0.0, False)
        for f in range(24):
            pfeat[f // 8, pl.ds(f % 8, npat * 4, stride=8), :] = theirs[f]
        for c in range(8):
            wts[pl.ds(c, npat * 4, stride=8), :] = 4.0 * cols[3 + c] if c < 3 else jnp.zeros_like(cols[0])

    compact(0, pfeat_ref, wts_ref)
    acc_ref[...] = jnp.zeros(acc_ref.shape, F32)

    @pl.loop(1, pages)
    def _(page):
        compact(page, pmore, wmore)
        evaluate(0, npat, nfeat, pmore, wmore, acc_ref)


def finish_kernel(
    nb,
    ng,
    don_ref,
    rec_ref,
    name_ref,
    base_ref,
    nfeat_ref,
    pfeat_ref,
    wts_ref,
    more_ref,
    allf,
    mov_ref,
    met_ref,
    out_ref,
    acc,
    halo,
    allm,
    allt,
    allg,
    rows,
    own,
    far,
    far_too,
    val,
    wone,
    wtwo,
    res,
    sh,
    rh,
    sm,
    rm,
    st,
    rt,
    sf,
    rf,
):
    b = lax.axis_index("bulk")
    g = lax.axis_index("grid")
    after = lax.rem(b + 1, nb)
    before = lax.rem(b + nb - 1, nb)
    high, low = halves(ng)
    along = g // low
    place = g - along * low

    def source(t):
        flip = t // high
        return lax.rem(along + (t - flip * high), high) * low + lax.rem(place + flip, low)

    near = [source(t) for t in range(1, high)]
    pair = [source(high)] if low == 2 else []
    barrier = pltpu.get_barrier_semaphore()
    peers = [(before, g), (after, g)] + [(b, source(t)) for t in range(1, ng)]
    for peer in peers:
        pl.semaphore_signal(barrier, inc=1, device_id=peer, device_id_type=MESH)

    radial, lines = mov_ref.shape[1:]
    nvar = out_ref.shape[0]
    acc[...] = more_ref[...]
    npat = radial // JOIN
    middle = npat // (2 * TILES) * TILES
    evaluate(0, middle, nfeat_ref, pfeat_ref, wts_ref, acc)
    pl.semaphore_wait(barrier, len(peers))
    passed = []

    def flow_copy(t):
        return pltpu.make_async_remote_copy(
            src_ref=allf.at[source(t)],
            dst_ref=allg.at[t - 1],
            send_sem=sf.at[t - 1],
            recv_sem=rf.at[t - 1],
            device_id=(b, source(high)),
            device_id_type=MESH,
        )

    if pair:
        for t in range(1, high):
            copy = flow_copy(t)
            copy.start()
            passed.append(copy)
    evaluate(middle, npat, nfeat_ref, pfeat_ref, wts_ref, acc)
    lane8 = iota((8, 128), 1)
    sub8 = iota((8, 128), 0)
    blocks_of_lanes = lane8 // 16
    within = lane8 - 16 * blocks_of_lanes
    for c in range(3):
        for jg in range(radial // 8):
            s = acc[pl.ds(64 * jg + c, 8, stride=8), :]
            got = jnp.zeros((8, 128), F32)
            for kg in range(8):
                row = jnp.broadcast_to(s[kg : kg + 1, :], (8, 128))
                got = jnp.where(blocks_of_lanes == kg, take_lanes(row, 16 * sub8 + within), got)
            mov_ref[c, 8 * jg : 8 * jg + 8, :] = base_ref[c, 8 * jg : 8 * jg + 8, :] + got
    halos = [
        pltpu.make_async_remote_copy(
            src_ref=mov_ref,
            dst_ref=halo.at[i],
            send_sem=sh.at[i],
            recv_sem=rh.at[i],
            device_id=(t, g),
            device_id_type=MESH,
        )
        for i, t in enumerate((after, before))
    ]
    for copy in halos:
        copy.start()
    sent = {"m": [], "t": []}

    def describe(kind, slot, peer, mine, n):
        src, full, ss, rs = {
            "m": (mov_ref, allm, sm, rm),
            "t": (met_ref, allt, st, rt),
        }[kind]
        return pltpu.make_async_remote_copy(
            src_ref=src if mine else full.at[slot],
            dst_ref=full.at[slot],
            send_sem=ss.at[n],
            recv_sem=rs.at[slot],
            device_id=(b, peer),
            device_id_type=MESH,
        )

    def send(kind, slot, peer, mine):
        copy = describe(kind, slot, peer, mine, len(sent[kind]))
        copy.start()
        sent[kind].append(copy)

    def arrived(kind, slot):
        describe(kind, slot, source(1), False, 0).wait_recv()

    for t in pair + near:
        send("m", g, t, True)
    row = iota((radial, lines), 0)
    col = iota((radial, lines), 1)
    dj, dk, centre = [], [], []
    for c in range(3):
        m = mov_ref[c]
        up, down = pltpu.roll(m, radial - 1, 0), pltpu.roll(m, 1, 0)
        dj.append(
            jnp.where(row == 0, up - m, jnp.where(row == radial - 1, m - down, (up - down) * 0.5))
        )
        up, down = pltpu.roll(m, lines - 1, 1), pltpu.roll(m, 1, 1)
        dk.append(
            jnp.where(col == 0, up - m, jnp.where(col == lines - 1, m - down, (up - down) * 0.5))
        )
        total = jnp.sum(jnp.sum(m, axis=0, keepdims=True), axis=1, keepdims=True)
        centre.append(total * (1.0 / (radial * lines)))
    cross = [
        dj[1] * dk[2] - dj[2] * dk[1],
        dj[2] * dk[0] - dj[0] * dk[2],
        dj[0] * dk[1] - dj[1] * dk[0],
    ]
    zero = jnp.zeros((8, 128), F32)
    mine = features([mov_ref[c] - centre[c] for c in range(3)], 0.0, True)
    for f in range(24):
        rows[f // 8, pl.ds(f % 8, radial, stride=8), :] = mine[f] * (-2.0 if f < 18 else 1.0)
    for r in range(radial):
        parts = [rows[p, r * 8 : (r + 1) * 8, :] for p in range(3)]
        own[r] = jnp.concatenate(parts + [zero], axis=0).astype(BF16)
    res[...] = jnp.zeros(res.shape, F32)

    for copy in halos:
        copy.wait_recv()
    di = [(halo[1, c] - halo[0, c]) * 0.5 for c in range(3)]
    met_ref[...] = di[0] * cross[0] + di[1] * cross[1] + di[2] * cross[2]
    for t in range(ng - 1, 0, -1):
        send("t", g, source(t), True)
    for s in near:
        arrived("m", s)
        for t in pair:
            send("m", s, t, False)

    none = jnp.zeros((32, 128), BF16)

    def prepare(t, far):
        flat = far.reshape(3, radial * 8, 128)
        s = source(t)
        theirs = features([allm[s, c] - centre[c] for c in range(3)], 0.25, False)
        for f in range(24):
            flat[f // 8, pl.ds(f % 8, radial, stride=8), :] = theirs[f]

    def weigh(t, e, far, wgt, slot):
        s = source(t)
        left, right = [], []
        for q in range(2):
            left += [far[p, don_ref[s, e + q]] for p in range(3)] + [zero]
            right.append(own[rec_ref[s, e + q]])
        right = [
            jnp.concatenate([right[0], none], axis=1),
            jnp.concatenate([none, right[1]], axis=1),
        ]
        den = lax.dot_general(
            jnp.concatenate(left, axis=0).astype(BF16),
            jnp.concatenate(right, axis=0),
            (((0,), (0,)), ((), ())),
            preferred_element_type=F32,
        )
        w = pl.reciprocal(den, approx=False)
        hi = w.astype(BF16)
        wgt[slot * HALF + e // 2, 0:128, :] = hi
        wgt[slot * HALF + e // 2, 128:256, :] = (w - hi.astype(F32)).astype(BF16)

    def load(t, flows, slot):
        met = allt[source(t)]
        for v in range(8):
            row = met * flows[slot, v] if v < nvar else jnp.full((radial, 128), 1.0 if v == nvar else 0.0, F32)
            val.reshape(radial * 8, 128)[pl.ds(v, radial, stride=8), :] = row

    def blend(t, e, wgt, slot):
        s = source(t)
        left = []
        for q in range(2):
            vals = val[don_ref[s, e + q]]
            vhi = vals.astype(BF16).astype(F32)
            both = jnp.concatenate([vhi, vals - vhi], axis=0).astype(BF16)
            left.append(jnp.concatenate([both, both], axis=1))
        got = jnp.dot(
            jnp.concatenate(left, axis=0),
            wgt[slot * HALF + e // 2],
            preferred_element_type=F32,
        )
        for q in range(2):
            one = got[16 * q : 16 * q + 8, 128 * q : 128 * q + 128]
            one = one + got[16 * q + 8 : 16 * q + 16, 128 * q : 128 * q + 128]
            one = one / one[nvar : nvar + 1, :]
            at = pl.multiple_of((t * HOLD + e + q) * 8, 8)
            res[pl.ds(at, 8), :] = one

    for s in pair:
        arrived("m", s)
    first = high if pair else high - 1
    rest = ng - 1 - first

    both = 2 - first % 2

    @pl.loop(0, first // both)
    def _(i):
        for q in range(both):
            prepare(1 + i * both + q, (far, far_too)[q])
        for e in range(0, MOST, 2):
            for q in range(both):
                t = 1 + i * both + q
                weigh(t, e, (far, far_too)[q], wone, t - 1)

    @pl.loop(1, rest + 1)
    def _(t):
        arrived("m", source(first + t))
        arrived("t", source(t))
        prepare(first + t, far)
        load(t, allf, source(t))
        for e in range(0, MOST, 2):
            weigh(first + t, e, far, wtwo, t - 1)
            blend(t, e, wone, t - 1)

    @pl.loop(rest + 1, first + 1)
    def _(t):
        arrived("t", source(t))
        load(t, allf, source(t))
        for e in range(0, MOST, 2):
            blend(t, e, wone, t - 1)

    for t in range(1, len(passed) + 1):
        flow_copy(t).wait_recv()

    @pl.loop(first + 1, ng)
    def _(t):
        arrived("t", source(t))
        load(t, allg, t - first - 1)
        for e in range(0, MOST, 2):
            blend(t, e, wtwo, t - first - 1)

    total = None
    blocks = iota((radial, 128), 0)
    for t in range(1, ng):
        name = jnp.broadcast_to(name_ref[pl.ds(source(t), 1), :], (radial, 128))
        pick = (name == blocks).astype(F32).astype(BF16)[:, 0:HOLD]
        cols = [res[pl.ds(t * HOLD * 8 + v, HOLD, stride=8), :] for v in range(nvar)]
        for part in split(jnp.concatenate(cols, axis=1))[:2]:
            got = jnp.dot(pick, part.astype(BF16), preferred_element_type=F32)
            total = got if total is None else total + got
    for v in range(nvar):
        out_ref[v] = total[:, 128 * v : 128 * v + 128]
    for copy in halos + passed + sent["m"] + sent["t"]:
        copy.wait_send()


def local(offsets, flow, control_points, rbf_weights, peer_offset, donor_block, receptor_block):
    _, _, planes, radial, lines = offsets.shape
    nvar = flow.shape[1]
    nb = lax.axis_size("bulk")
    ng = lax.axis_size("grid")
    nd = nb * ng
    nd = nb * ng
    rows = control_points.shape[1] // 128
    slots = donor_block.shape[1]
    lrows = -(-slots // 128)
    npat = radial // JOIN
    dma = pltpu.SemaphoreType.DMA
    sds = jax.ShapeDtypeStruct
    base, fil, tot, box, midp, nfeat, don, rec, name, allf = pl.pallas_call(
        functools.partial(gather_kernel, nb, ng, rows, lrows),
        out_shape=(
            sds((3, radial, lines), F32),
            sds((6, 128, 128), F32),
            sds((8, 128), I32),
            sds((6, npat, 8, 128), F32),
            sds((3, npat * 4, 128), F32),
            sds((3, radial * 8, 128), F32),
            sds((ng, 128), I32),
            sds((ng, 128), I32),
            sds((ng, 128), I32),
            sds((ng, nvar, radial, lines), F32),
        ),
        in_specs=[VMEM_SPEC] * 7,
        out_specs=[VMEM_SPEC] * 10,
        scratch_shapes=[
            pltpu.VMEM((6 * rows, 128), F32),
            pltpu.VMEM((3 * lrows, 128), I32),
            pltpu.VMEM((nd, 6 * rows, 128), F32),
            pltpu.VMEM((ng, 3 * lrows, 128), I32),
            pltpu.VMEM((6, nd * rows, 128), F32),
            pltpu.VMEM((3, radial, 128), F32),
            pltpu.VMEM((3, radial, 128), F32),
            pltpu.VMEM((3 * lrows, ng, 128), I32),
            dma((nd,)),
            dma((nd,)),
            dma((ng,)),
            dma((ng,)),
            dma((2 * ng,)),
            dma((ng,)),
        ],
        compiler_params=pltpu.CompilerParams(collective_id=0, has_side_effects=True),
        name="gather_points",
    )(
        offsets.reshape(3, radial, lines),
        control_points,
        rbf_weights,
        peer_offset.reshape(1, slots),
        donor_block,
        receptor_block,
        flow.reshape(nvar, radial, lines),
    )
    pfeat, wts, more = pl.pallas_call(
        cull_kernel,
        out_shape=(
            sds((3, npat * 32, 128), F32),
            sds((npat * 32, 128), F32),
            sds((radial * 8, 128), F32),
        ),
        in_specs=[VMEM_SPEC] * 5,
        out_specs=[VMEM_SPEC] * 3,
        scratch_shapes=[
            pltpu.VMEM((6, npat * 8, 128), F32),
            pltpu.VMEM((npat * 8, 128), I32),
            pltpu.VMEM((3, npat * 32, 128), F32),
            pltpu.VMEM((npat * 32, 128), F32),
        ],
        name="cull_points",
    )(fil, tot, box, midp, nfeat)
    first = halves(ng)[0] if halves(ng)[1] == 2 else ng - 1
    moved, metric, fringe = pl.pallas_call(
        functools.partial(finish_kernel, nb, ng),
        out_shape=(
            sds((3, radial, lines), F32),
            sds((radial, lines), F32),
            sds((nvar, radial, lines), F32),
        ),
        in_specs=[SMEM_SPEC] * 2 + [VMEM_SPEC] * 7,
        out_specs=[VMEM_SPEC] * 3,
        scratch_shapes=[
            pltpu.VMEM((radial * 8, 128), F32),
            pltpu.VMEM((2, 3, radial, lines), F32),
            pltpu.VMEM((ng, 3, radial, lines), F32),
            pltpu.VMEM((ng, radial, lines), F32),
            pltpu.VMEM((halves(ng)[0], nvar, radial, lines), F32),
            pltpu.VMEM((3, radial * 8, 128), F32),
            pltpu.VMEM((radial, 32, 128), BF16),
            pltpu.VMEM((3, radial, 8, 128), F32),
            pltpu.VMEM((3, radial, 8, 128), F32),
            pltpu.VMEM((radial, 8, 128), F32),
            pltpu.VMEM((first * HALF, 256, 256), BF16),
            pltpu.VMEM(((ng - 1 - first) * HALF, 256, 256), BF16),
            pltpu.VMEM((ng * HOLD * 8, 128), F32),
            dma((2,)),
            dma((2,)),
            dma((2 * ng,)),
            dma((ng,)),
            dma((2 * ng,)),
            dma((ng,)),
            dma((ng,)),
            dma((ng,)),
        ],
        compiler_params=pltpu.CompilerParams(
            collective_id=1,
            has_side_effects=True,
            vmem_limit_bytes=60 << 20,
        ),
        name="finish",
    )(don, rec, name, base, nfeat, pfeat, wts, more, allf)
    return (
        moved.reshape(1, 3, planes, radial, lines),
        metric.reshape(1, planes, radial, lines),
        fringe.reshape(1, nvar, planes, radial, lines),
    )


def solution(mesh):
    in_specs = (
        P("grid", None, "bulk", None, None),
        P("grid", None, "bulk", None, None),
        P(None, ("bulk", "grid")),
        P(None, ("bulk", "grid")),
        P("grid", "bulk", None),
        P("grid", "bulk"),
        P("grid", "bulk"),
    )
    out_specs = (
        P("grid", None, "bulk", None, None),
        P("grid", "bulk", None, None),
        P("grid", None, "bulk", None, None),
    )
    return jax.shard_map(local, mesh=mesh, in_specs=in_specs, out_specs=out_specs, check_vma=False)
```
